256 devices in a mesh: det: 2 (over core), grp: 4 (over x), filt: 32 (over y, z).
Axes of the slice: x: 4, y: 4, z: 8, core: 2. Of those that a mesh axis runs over, the one named last changes fastest.
Arguments:
- strain: float32 [2, 131072], P('det'), may hold values from -6 to 6
- inv_asd: float32 [2, 65536], P('det'), may hold values from 0.25 to 4
- templates: bfloat16 [1536, 4096], P(('grp', 'filt')), may hold values from -6 to 6
- chirp_blocks: int32 [1536], P(('grp', 'filt')), may hold values from 1 to 32, as said below
- owner: int32 [1536], P(('grp', 'filt')), may hold values from 0 to 31, as said below
- slide: int32 [4], P('grp'), may hold values from 0 to 1023
Outputs:
- peaks: float32 [1536, 1024], P(('grp', 'filt'), 'det')
- loudest: float32 [1024], P('det')
The draws below stay inside these ranges and needn't reach their ends.
Inputs may be any that keep to these rules, and one draw needn't show every extreme that they name: `chirp_blocks`: every device holds a template of 32 blocks. Each device sends either 1 or none of its templates to each owner of its group, and each owner receives exactly 12 templates.
All inputs are finite; a program needn't handle non-finite values.
Results may differ from the reference program's by a relative error of at most 0.0052.
Values may be sent and summed in bfloat16 or wider, within the bound.
A program may use at most 64 MiB of HBM per device.

```python
import math
import jax
import jax.numpy as jnp
from jax import lax

N1 = 256
N2 = 512
NFFT = 131072
BLK = 128
MAXB = 32
TL = 4096
NBLK = 1024
TPL_DEV = 12
CAP = 1
TEMPLATES = 1536
N_DET = 2
N_GRP = 4
N_FILT = 32


def draw_chirp_blocks(key, part):
    devices = N_GRP * N_FILT
    lengths = jax.random.randint(jax.random.fold_in(key, 21), (devices, TPL_DEV), 1, MAXB + 1)
    longest = jax.random.randint(jax.random.fold_in(key, 22), (devices, 1), 0, TPL_DEV)
    lengths = jnp.where(jnp.arange(TPL_DEV, dtype=jnp.int32)[None, :] == longest, MAXB, lengths)
    return lengths.reshape(TEMPLATES).astype(jnp.int32)


def draw_owner(key, part):
    shift_keys = jax.random.split(jax.random.fold_in(key, 11), N_GRP)
    shifts = jax.vmap(lambda shift_key: jax.random.permutation(shift_key, N_FILT)[:TPL_DEV // CAP])(shift_keys)
    source = jnp.arange(N_FILT, dtype=jnp.int32)[None, :, None]
    picked = jnp.arange(TPL_DEV, dtype=jnp.int32) // CAP
    based = (source + shifts[:, None, picked].astype(jnp.int32)) % N_FILT
    scores = jax.random.randint(jax.random.fold_in(key, 12), (N_GRP, N_FILT, TPL_DEV), 0, 1 << 20) * TPL_DEV
    scores = scores + jnp.arange(TPL_DEV, dtype=jnp.int32)
    shuffle = jnp.argsort(scores, axis=-1)
    return jnp.take_along_axis(based, shuffle, axis=-1).reshape(TEMPLATES).astype(jnp.int32)


def touch_ends(values, own_key, low, top_value):
    longest = values.shape.index(max(values.shape))
    spots = []
    for shift in (0, 1):
        where = [jax.random.randint(jax.random.fold_in(own_key, axis), (), 0, length) for axis, length in enumerate(values.shape)]
        where[longest] = (where[longest] + shift) % values.shape[longest]
        spots.append(tuple(where))
    return values.at[spots[0]].set(low).at[spots[1]].set(top_value)


def block_levels(rng, dims, cuts, smallest, top_value):
    loudness, own = 1.0, jax.random.fold_in(rng, 6)
    for position, parts in cuts:
        draws = jnp.exp(jax.random.uniform(jax.random.fold_in(own, position), (parts,), jnp.float32, smallest / len(cuts), top_value / len(cuts)))
        loudness = loudness * jnp.repeat(draws, dims[position] // parts).reshape([-1 if axis == position else 1 for axis in range(len(dims))])
    return loudness


def scatter_about(rng, extent, width, reach, cuts=(), kind=jnp.bfloat16):
    loudness = block_levels(rng, extent, cuts, -0.22, 0.18) if cuts else 1.0
    array = jax.random.normal(rng, extent, jnp.float32) * width * loudness
    return jnp.minimum(jnp.maximum(array, -reach), reach).astype(kind)


def setup_inputs(seed: int = 0) -> dict:
    arg_keys = jax.random.split(jax.random.key(seed), 7)
    return {
        "strain": scatter_about(arg_keys[0], (N_DET, NFFT), 1.0, 6.0, ((0, 2),), jnp.float32),
        "inv_asd": jnp.clip(jnp.exp(math.log(4.0) - 2.7725887 * jax.random.uniform(arg_keys[1], (N_DET, NFFT // 2), jnp.float32) ** block_levels(arg_keys[1], (N_DET, NFFT // 2), ((0, 2),), -0.2, 0.2)), 0.25, 4.0),
        "templates": scatter_about(arg_keys[2], (TEMPLATES, TL), 1.0, 6.0, ((0, 128),)),
        "chirp_blocks": draw_chirp_blocks(jax.random.fold_in(arg_keys[6], 71), 0),
        "owner": draw_owner(jax.random.fold_in(arg_keys[6], 71), 0),
        "slide": touch_ends(jax.random.randint(arg_keys[5], (N_GRP,), 0, NBLK), jax.random.fold_in(arg_keys[5], 1), 0, NBLK - 1).astype(jnp.int32),
    }


TWO_PI = 6.283185307179586


def angle_table(rows, cols, period):
    left = jnp.arange(rows, dtype=jnp.int32)[:, None]
    right = jnp.arange(cols, dtype=jnp.int32)[None, :]
    return (TWO_PI / period) * ((left * right) % period).astype(jnp.float32)


def make_tables():
    first = angle_table(N1, N1, N1)
    twist = angle_table(N1, N2, NFFT)
    second = angle_table(N2, N2 // 2, N2)
    back = angle_table(N2 // 2, N2, N2)
    return (jnp.cos(first).astype(jnp.bfloat16), jnp.sin(first).astype(jnp.bfloat16),
            jnp.cos(twist), jnp.sin(twist),
            jnp.cos(second).astype(jnp.bfloat16), jnp.sin(second).astype(jnp.bfloat16),
            jnp.cos(back).astype(jnp.bfloat16), jnp.sin(back).astype(jnp.bfloat16))


def forward(signal, cos_rows, sin_rows, tables):
    cos_first, sin_first, cos_twist, sin_twist, cos_second, sin_second, cos_back, sin_back = tables
    real_a = jnp.dot(cos_rows, signal, preferred_element_type=jnp.float32)
    imag_a = -jnp.dot(sin_rows, signal, preferred_element_type=jnp.float32)
    real_b = (real_a * cos_twist + imag_a * sin_twist).astype(jnp.bfloat16)
    imag_b = (imag_a * cos_twist - real_a * sin_twist).astype(jnp.bfloat16)
    real_x = jnp.dot(real_b, cos_second, preferred_element_type=jnp.float32) + jnp.dot(imag_b, sin_second, preferred_element_type=jnp.float32)
    imag_x = jnp.dot(imag_b, cos_second, preferred_element_type=jnp.float32) - jnp.dot(real_b, sin_second, preferred_element_type=jnp.float32)
    return real_x, imag_x


def correlate(windowed, spectrum, weight2d, tables):
    cos_first, sin_first, cos_twist, sin_twist, cos_second, sin_second, cos_back, sin_back = tables
    rows_used = windowed.shape[0]
    temp_real, temp_imag = forward(windowed, cos_first[:, :rows_used], sin_first[:, :rows_used], tables)
    sigma = jnp.sum(weight2d * weight2d * (temp_real * temp_real + temp_imag * temp_imag))
    data_real, data_imag = spectrum
    q_real = (temp_real * data_real + temp_imag * data_imag).astype(jnp.bfloat16)
    q_imag = (temp_real * data_imag - temp_imag * data_real).astype(jnp.bfloat16)
    d_real = jnp.dot(q_real, cos_back, preferred_element_type=jnp.float32) - jnp.dot(q_imag, sin_back, preferred_element_type=jnp.float32)
    d_imag = jnp.dot(q_real, sin_back, preferred_element_type=jnp.float32) + jnp.dot(q_imag, cos_back, preferred_element_type=jnp.float32)
    e_real = (d_real * cos_twist - d_imag * sin_twist).astype(jnp.bfloat16)
    e_imag = (d_real * sin_twist + d_imag * cos_twist).astype(jnp.bfloat16)
    z_real = jnp.dot(cos_first, e_real, preferred_element_type=jnp.float32) - jnp.dot(sin_first, e_imag, preferred_element_type=jnp.float32)
    z_imag = jnp.dot(sin_first, e_real, preferred_element_type=jnp.float32) + jnp.dot(cos_first, e_imag, preferred_element_type=jnp.float32)
    return ((z_real * z_real + z_imag * z_imag) / (NFFT * sigma)).reshape(NFFT)


def data_spectrum(strain_row, weight_row, tables):
    weight2d = weight_row.reshape(N2 // 2, N1).T
    signal = strain_row.astype(jnp.bfloat16).reshape(N1, N2)
    real_s, imag_s = forward(signal, tables[0], tables[1], tables)
    return (weight2d * real_s, weight2d * imag_s), weight2d


def reference(strain, inv_asd, templates, chirp_blocks, owner, slide):
    tables = make_tables()
    first_spec, first_weight = data_spectrum(strain[0], inv_asd[0], tables)
    second_spec, second_weight = data_spectrum(strain[1], inv_asd[1], tables)
    group_of = jnp.arange(TEMPLATES, dtype=jnp.int32) // (N_FILT * TPL_DEV)
    owner_order = jnp.argsort(group_of * N_FILT + owner, stable=True).astype(jnp.int32)
    samples = jnp.arange(TL, dtype=jnp.int32)

    def filter_template(template_id):
        bank_row = templates[template_id]
        windowed = jnp.where(samples < BLK * chirp_blocks[template_id], bank_row, jnp.zeros_like(bank_row))
        windowed = windowed.reshape(TL // N2, N2)
        first_snr = correlate(windowed, first_spec, first_weight, tables)
        second_snr = correlate(windowed, second_spec, second_weight, tables)
        slide_shift = BLK * slide[group_of[template_id]]
        network = first_snr + jnp.roll(second_snr, -slide_shift)
        return jnp.max(network.reshape(NBLK, BLK), axis=1)

    peaks = lax.map(filter_template, owner_order)
    loudest = jnp.max(peaks, axis=0)
    return peaks, loudest
```

```python
import jax
import jax.numpy as jnp
from jax import lax
from jax.sharding import PartitionSpec as P

N1 = 256
N2 = 512
NFFT = 131072
BLK = 128
TL = 4096


TWO_PI = 6.283185307179586


def partner_2(value, axis, stride):
    mask = 2**stride
    pairs = [(source, source ^ mask) for source in range(lax.axis_size(axis))]
    return lax.ppermute(value, axis, pairs)


def angle_table(rows, cols, period):
    left = jnp.arange(rows, dtype=jnp.int32)[:, None]
    right = jnp.arange(cols, dtype=jnp.int32)[None, :]
    return TWO_PI / period * (left * right % period).astype(jnp.float32)


def make_tables():
    first = angle_table(N1, N1, N1)
    twist = angle_table(N1, N2, NFFT)
    second = angle_table(N2, N2 // 2, N2)
    back = angle_table(N2 // 2, N2, N2)
    return (
        jnp.cos(first).astype(jnp.bfloat16),
        jnp.sin(first).astype(jnp.bfloat16),
        jnp.cos(twist),
        jnp.sin(twist),
        jnp.cos(second).astype(jnp.bfloat16),
        jnp.sin(second).astype(jnp.bfloat16),
        jnp.cos(back).astype(jnp.bfloat16),
        jnp.sin(back).astype(jnp.bfloat16),
    )


def forward(signal, cos_rows, sin_rows, tables):
    cos_first, sin_first, cos_twist, sin_twist, cos_second, sin_second, cos_back, sin_back = tables
    real_a = jnp.dot(cos_rows, signal, preferred_element_type=jnp.float32)
    imag_a = -jnp.dot(sin_rows, signal, preferred_element_type=jnp.float32)
    real_b = (real_a * cos_twist + imag_a * sin_twist).astype(jnp.bfloat16)
    imag_b = (imag_a * cos_twist - real_a * sin_twist).astype(jnp.bfloat16)
    real_x = jnp.dot(real_b, cos_second, preferred_element_type=jnp.float32) + jnp.dot(
        imag_b, sin_second, preferred_element_type=jnp.float32
    )
    imag_x = jnp.dot(imag_b, cos_second, preferred_element_type=jnp.float32) - jnp.dot(
        real_b, sin_second, preferred_element_type=jnp.float32
    )
    return (real_x, imag_x)


def correlate(windowed, spectrum, weight2d, tables):
    cos_first, sin_first, cos_twist, sin_twist, cos_second, sin_second, cos_back, sin_back = tables
    rows_used = windowed.shape[0]
    temp_real, temp_imag = forward(
        windowed, cos_first[:, :rows_used], sin_first[:, :rows_used], tables
    )
    sigma = jnp.sum(weight2d * weight2d * (temp_real * temp_real + temp_imag * temp_imag))
    data_real, data_imag = spectrum
    q_real = (temp_real * data_real + temp_imag * data_imag).astype(jnp.bfloat16)
    q_imag = (temp_real * data_imag - temp_imag * data_real).astype(jnp.bfloat16)
    d_real = jnp.dot(q_real, cos_back, preferred_element_type=jnp.float32) - jnp.dot(
        q_imag, sin_back, preferred_element_type=jnp.float32
    )
    d_imag = jnp.dot(q_real, sin_back, preferred_element_type=jnp.float32) + jnp.dot(
        q_imag, cos_back, preferred_element_type=jnp.float32
    )
    e_real = (d_real * cos_twist - d_imag * sin_twist).astype(jnp.bfloat16)
    e_imag = (d_real * sin_twist + d_imag * cos_twist).astype(jnp.bfloat16)
    z_real = jnp.dot(cos_first, e_real, preferred_element_type=jnp.float32) - jnp.dot(
        sin_first, e_imag, preferred_element_type=jnp.float32
    )
    z_imag = jnp.dot(sin_first, e_real, preferred_element_type=jnp.float32) + jnp.dot(
        cos_first, e_imag, preferred_element_type=jnp.float32
    )
    return ((z_real * z_real + z_imag * z_imag) / (NFFT * sigma)).reshape(NFFT)


def data_spectrum(strain_row, weight_row, tables):
    weight2d = weight_row.reshape(N2 // 2, N1).T
    signal = strain_row.astype(jnp.bfloat16).reshape(N1, N2)
    real_s, imag_s = forward(signal, tables[0], tables[1], tables)
    return ((weight2d * real_s, weight2d * imag_s), weight2d)


def compact(rows, blocks, valid, count):
    slot_rank = jnp.cumsum(valid.astype(jnp.int32)) - 1
    wanted = jnp.arange(count, dtype=jnp.int32)[:, None]
    picker = jnp.logical_and(valid[None, :], slot_rank[None, :] == wanted)
    picked = jnp.dot(picker.astype(jnp.bfloat16), rows, preferred_element_type=jnp.float32).astype(
        jnp.bfloat16
    )
    picked_blocks = jnp.sum(jnp.where(picker, blocks[None, :], 0), axis=1).astype(jnp.int32)
    return (picked, picked_blocks)


def template_transform(windowed, tables):
    rows_used = windowed.shape[0]
    return forward(windowed, tables[0][:, :rows_used], tables[1][:, :rows_used], tables)


def correlate_with(temp_real, temp_imag, spectrum, weight2d, tables):
    cos_first, sin_first, cos_twist, sin_twist, cos_second, sin_second, cos_back, sin_back = tables
    sigma = jnp.sum(weight2d * weight2d * (temp_real * temp_real + temp_imag * temp_imag))
    data_real, data_imag = spectrum
    q_real = (temp_real * data_real + temp_imag * data_imag).astype(jnp.bfloat16)
    q_imag = (temp_real * data_imag - temp_imag * data_real).astype(jnp.bfloat16)
    d_real = jnp.dot(q_real, cos_back, preferred_element_type=jnp.float32) - jnp.dot(
        q_imag, sin_back, preferred_element_type=jnp.float32
    )
    d_imag = jnp.dot(q_real, sin_back, preferred_element_type=jnp.float32) + jnp.dot(
        q_imag, cos_back, preferred_element_type=jnp.float32
    )
    e_real = (d_real * cos_twist - d_imag * sin_twist).astype(jnp.bfloat16)
    e_imag = (d_real * sin_twist + d_imag * cos_twist).astype(jnp.bfloat16)
    z_real = jnp.dot(cos_first, e_real, preferred_element_type=jnp.float32) - jnp.dot(
        sin_first, e_imag, preferred_element_type=jnp.float32
    )
    z_imag = jnp.dot(sin_first, e_real, preferred_element_type=jnp.float32) + jnp.dot(
        cos_first, e_imag, preferred_element_type=jnp.float32
    )
    return (z_real * z_real + z_imag * z_imag) / (NFFT * sigma)


def shards(strain, inv_asd, templates, chirp_blocks, owner, slide):
    tables = lax.optimization_barrier(make_tables())
    detector = lax.axis_index("det")
    per_dev = templates.shape[0]
    mine = per_dev // 2
    n_blk = NFFT // BLK
    half_blk = n_blk // 2
    filt_count = lax.axis_size("filt")
    capacity = (per_dev + filt_count - 1) // filt_count
    positions = jnp.arange(per_dev, dtype=jnp.int32)
    same_owner = owner[:, None] == owner[None, :]
    earlier = positions[None, :] < positions[:, None]
    owner_rank = jnp.sum(jnp.logical_and(same_owner, earlier).astype(jnp.int32), axis=1)
    dest_slot = owner * capacity + owner_rank
    slot_ids = jnp.arange(filt_count * capacity, dtype=jnp.int32)[:, None]
    placing = slot_ids == dest_slot[None, :]
    send_rows = jnp.dot(
        placing.astype(jnp.bfloat16), templates, preferred_element_type=jnp.float32
    ).astype(jnp.bfloat16)
    send_blocks = jnp.sum(jnp.where(placing, chirp_blocks[None, :], 0), axis=1)
    recv_rows, recv_blocks = (
        lax.all_to_all(send_rows, "filt", split_axis=0, concat_axis=0, tiled=True),
        lax.all_to_all(send_blocks, "filt", split_axis=0, concat_axis=0, tiled=True),
    )
    local_rows, local_blocks = compact(recv_rows, recv_blocks, recv_blocks > 0, per_dev)
    my_rows = lax.dynamic_slice_in_dim(local_rows, detector * mine, mine)
    my_blocks = lax.dynamic_slice_in_dim(local_blocks, detector * mine, mine)
    samples = jnp.arange(TL, dtype=jnp.int32)
    windowed = jnp.where(
        samples[None, :] < BLK * my_blocks[:, None], my_rows, jnp.zeros_like(my_rows)
    )
    windowed = windowed.reshape(mine, TL // N2, N2)
    strain_both = lax.all_gather(strain[0].astype(jnp.bfloat16), "det")
    asd_both = lax.all_gather(inv_asd[0], "det")
    spec_0, weight_0 = data_spectrum(strain_both[0], asd_both[0], tables)
    spec_1, weight_1 = data_spectrum(strain_both[1], asd_both[1], tables)
    shift = slide[0]

    def filter_template(kept_row):
        temp_real, temp_imag = template_transform(kept_row, tables)
        first = correlate_with(temp_real, temp_imag, spec_0, weight_0, tables)
        second = correlate_with(temp_real, temp_imag, spec_1, weight_1, tables)
        second = jnp.roll(second.reshape(n_blk, BLK), -shift, axis=0)
        network = first.reshape(n_blk, BLK) + second
        return jnp.max(network, axis=1)

    full = lax.map(filter_template, windowed)
    keep = lax.dynamic_slice_in_dim(full, detector * half_blk, half_blk, axis=1)
    give = lax.dynamic_slice_in_dim(full, (1 - detector) * half_blk, half_blk, axis=1)
    got = lax.ppermute(give, "det", [(0, 1), (1, 0)])
    peaks = jnp.where(
        detector == 0, jnp.concatenate([keep, got], axis=0), jnp.concatenate([got, keep], axis=0)
    )
    local_max = jnp.max(peaks, axis=0)
    gathered = lax.all_gather(local_max, ("grp", "filt"))
    loudest = jnp.max(gathered, axis=0)
    return (peaks, loudest)


def solution(mesh):
    return jax.shard_map(
        shards,
        mesh=mesh,
        in_specs=(
            P("det", None),
            P("det", None),
            P(("grp", "filt"), None),
            P(("grp", "filt")),
            P(("grp", "filt")),
            P("grp"),
        ),
        out_specs=(P(("grp", "filt"), "det"), P("det")),
        check_vma=False,
    )
```

```python
import functools

import jax
import jax.numpy as jnp
from jax import lax
from jax.experimental import pallas as pl
from jax.experimental.pallas import tpu as pltpu
from jax.sharding import PartitionSpec as P

N1 = 256
N2 = 512
NFFT = 131072
BLK = 128
TL = 4096


TWO_PI = 6.283185307179586


def partner_2(value, axis, stride):
    mask = 2**stride
    pairs = [(source, source ^ mask) for source in range(lax.axis_size(axis))]
    return lax.ppermute(value, axis, pairs)


def angle_table(rows, cols, period):
    left = jnp.arange(rows, dtype=jnp.int32)[:, None]
    right = jnp.arange(cols, dtype=jnp.int32)[None, :]
    return TWO_PI / period * (left * right % period).astype(jnp.float32)


def make_tables():
    first = angle_table(N1, N1, N1)
    twist = angle_table(N1, N2, NFFT)
    second = angle_table(N2, N2 // 2, N2)
    back = angle_table(N2 // 2, N2, N2)
    return (
        jnp.cos(first).astype(jnp.bfloat16),
        jnp.sin(first).astype(jnp.bfloat16),
        jnp.cos(twist),
        jnp.sin(twist),
        jnp.cos(second).astype(jnp.bfloat16),
        jnp.sin(second).astype(jnp.bfloat16),
        jnp.cos(back).astype(jnp.bfloat16),
        jnp.sin(back).astype(jnp.bfloat16),
    )


def forward(signal, cos_rows, sin_rows, tables):
    cos_first, sin_first, cos_twist, sin_twist, cos_second, sin_second, cos_back, sin_back = tables
    real_a = jnp.dot(cos_rows, signal, preferred_element_type=jnp.float32)
    imag_a = -jnp.dot(sin_rows, signal, preferred_element_type=jnp.float32)
    real_b = (real_a * cos_twist + imag_a * sin_twist).astype(jnp.bfloat16)
    imag_b = (imag_a * cos_twist - real_a * sin_twist).astype(jnp.bfloat16)
    real_x = jnp.dot(real_b, cos_second, preferred_element_type=jnp.float32) + jnp.dot(
        imag_b, sin_second, preferred_element_type=jnp.float32
    )
    imag_x = jnp.dot(imag_b, cos_second, preferred_element_type=jnp.float32) - jnp.dot(
        real_b, sin_second, preferred_element_type=jnp.float32
    )
    return (real_x, imag_x)


def correlate(windowed, spectrum, weight2d, tables):
    cos_first, sin_first, cos_twist, sin_twist, cos_second, sin_second, cos_back, sin_back = tables
    rows_used = windowed.shape[0]
    temp_real, temp_imag = forward(
        windowed, cos_first[:, :rows_used], sin_first[:, :rows_used], tables
    )
    sigma = jnp.sum(weight2d * weight2d * (temp_real * temp_real + temp_imag * temp_imag))
    data_real, data_imag = spectrum
    q_real = (temp_real * data_real + temp_imag * data_imag).astype(jnp.bfloat16)
    q_imag = (temp_real * data_imag - temp_imag * data_real).astype(jnp.bfloat16)
    d_real = jnp.dot(q_real, cos_back, preferred_element_type=jnp.float32) - jnp.dot(
        q_imag, sin_back, preferred_element_type=jnp.float32
    )
    d_imag = jnp.dot(q_real, sin_back, preferred_element_type=jnp.float32) + jnp.dot(
        q_imag, cos_back, preferred_element_type=jnp.float32
    )
    e_real = (d_real * cos_twist - d_imag * sin_twist).astype(jnp.bfloat16)
    e_imag = (d_real * sin_twist + d_imag * cos_twist).astype(jnp.bfloat16)
    z_real = jnp.dot(cos_first, e_real, preferred_element_type=jnp.float32) - jnp.dot(
        sin_first, e_imag, preferred_element_type=jnp.float32
    )
    z_imag = jnp.dot(sin_first, e_real, preferred_element_type=jnp.float32) + jnp.dot(
        cos_first, e_imag, preferred_element_type=jnp.float32
    )
    return ((z_real * z_real + z_imag * z_imag) / (NFFT * sigma)).reshape(NFFT)


def data_spectrum(strain_row, weight_row, tables):
    weight2d = weight_row.reshape(N2 // 2, N1).T
    signal = strain_row.astype(jnp.bfloat16).reshape(N1, N2)
    real_s, imag_s = forward(signal, tables[0], tables[1], tables)
    return ((weight2d * real_s, weight2d * imag_s), weight2d)


def compact(rows, valid, wanted):
    slot_rank = jnp.cumsum(valid.astype(jnp.int32)) - 1
    picker = jnp.logical_and(valid[None, :], slot_rank[None, :] == wanted[:, None])
    return jnp.dot(picker.astype(jnp.bfloat16), rows, preferred_element_type=jnp.float32).astype(
        jnp.bfloat16
    )


def loudest_kernel(n_grp, n_filt, local_ref, out_ref, held, send_sems, recv_sems):
    det = lax.axis_index("det")
    size = n_grp * n_filt
    me = lax.axis_index("grp") * n_filt + lax.axis_index("filt")
    mesh_ids = pl.DeviceIdType.MESH

    def peer_of(i):
        peer = lax.rem(me + 1 + i, size)
        return (det, peer // n_filt, lax.rem(peer, n_filt))

    def copy_to(i):
        row = size - 2 - i
        return pltpu.make_async_remote_copy(
            src_ref=local_ref,
            dst_ref=held.at[row],
            send_sem=send_sems.at[i],
            recv_sem=recv_sems.at[row],
            device_id=peer_of(i),
            device_id_type=mesh_ids,
        )

    barrier = pltpu.get_barrier_semaphore()

    def greet(i, carry):
        pl.semaphore_signal(barrier, inc=1, device_id=peer_of(i), device_id_type=mesh_ids)
        return carry

    lax.fori_loop(0, size - 1, greet, 0)
    pl.semaphore_wait(barrier, size - 1)

    def send(i, carry):
        copy_to(i).start()
        return carry

    lax.fori_loop(0, size - 1, send, 0)

    def finish(i, carry):
        copy = copy_to(i)
        copy.wait_send()
        copy.wait_recv()
        return carry

    lax.fori_loop(0, size - 1, finish, 0)
    out_ref[...] = jnp.maximum(local_ref[...], jnp.max(held[...], axis=0))


def group_max(local_max):
    n_grp = lax.axis_size("grp")
    n_filt = lax.axis_size("filt")
    size = n_grp * n_filt
    width = local_max.shape[-1]
    out = pl.pallas_call(
        functools.partial(loudest_kernel, n_grp, n_filt),
        out_shape=jax.ShapeDtypeStruct((1, width), jnp.float32),
        in_specs=[pl.BlockSpec(memory_space=pltpu.VMEM)],
        out_specs=pl.BlockSpec(memory_space=pltpu.VMEM),
        scratch_shapes=[
            pltpu.VMEM((size - 1, 1, width), jnp.float32),
            pltpu.SemaphoreType.DMA((size - 1,)),
            pltpu.SemaphoreType.DMA((size - 1,)),
        ],
        compiler_params=pltpu.CompilerParams(collective_id=0, has_side_effects=True),
    )(local_max.reshape(1, width))
    return out.reshape(width)


def template_transform(windowed, tables):
    rows_used = windowed.shape[0]
    return forward(windowed, tables[0][:, :rows_used], tables[1][:, :rows_used], tables)


def correlate_with(temp_real, temp_imag, spectrum, weight2d, tables):
    cos_first, sin_first, cos_twist, sin_twist, cos_second, sin_second, cos_back, sin_back = tables
    sigma = jnp.sum(weight2d * weight2d * (temp_real * temp_real + temp_imag * temp_imag))
    data_real, data_imag = spectrum
    q_real = (temp_real * data_real + temp_imag * data_imag).astype(jnp.bfloat16)
    q_imag = (temp_real * data_imag - temp_imag * data_real).astype(jnp.bfloat16)
    d_real = jnp.dot(q_real, cos_back, preferred_element_type=jnp.float32) - jnp.dot(
        q_imag, sin_back, preferred_element_type=jnp.float32
    )
    d_imag = jnp.dot(q_real, sin_back, preferred_element_type=jnp.float32) + jnp.dot(
        q_imag, cos_back, preferred_element_type=jnp.float32
    )
    e_real = (d_real * cos_twist - d_imag * sin_twist).astype(jnp.bfloat16)
    e_imag = (d_real * sin_twist + d_imag * cos_twist).astype(jnp.bfloat16)
    z_real = jnp.dot(cos_first, e_real, preferred_element_type=jnp.float32) - jnp.dot(
        sin_first, e_imag, preferred_element_type=jnp.float32
    )
    z_imag = jnp.dot(sin_first, e_real, preferred_element_type=jnp.float32) + jnp.dot(
        cos_first, e_imag, preferred_element_type=jnp.float32
    )
    return (z_real * z_real + z_imag * z_imag) / (NFFT * sigma)


def shards(strain, inv_asd, templates, chirp_blocks, owner, slide):
    tables = lax.optimization_barrier(make_tables())
    detector = lax.axis_index("det")
    per_dev = templates.shape[0]
    mine = per_dev // 2
    n_blk = NFFT // BLK
    half_blk = n_blk // 2
    filt_count = lax.axis_size("filt")
    capacity = (per_dev + filt_count - 1) // filt_count
    positions = jnp.arange(per_dev, dtype=jnp.int32)
    same_owner = owner[:, None] == owner[None, :]
    earlier = positions[None, :] < positions[:, None]
    owner_rank = jnp.sum(jnp.logical_and(same_owner, earlier).astype(jnp.int32), axis=1)
    dest_slot = owner * capacity + owner_rank
    slot_ids = jnp.arange(filt_count * capacity, dtype=jnp.int32)[:, None]
    placing = slot_ids == dest_slot[None, :]
    samples = jnp.arange(TL, dtype=jnp.int32)
    windowed = jnp.where(
        samples[None, :] < BLK * chirp_blocks[:, None], templates, jnp.zeros_like(templates)
    )
    payload = jnp.concatenate([windowed, jnp.ones((per_dev, 128), jnp.bfloat16)], axis=1)
    send_rows = jnp.dot(
        placing.astype(jnp.bfloat16), payload, preferred_element_type=jnp.float32
    ).astype(jnp.bfloat16)
    recv_rows = lax.all_to_all(send_rows, "filt", split_axis=0, concat_axis=0, tiled=True)
    valid = recv_rows[:, TL] > 0.5
    wanted = detector * mine + jnp.arange(mine, dtype=jnp.int32)
    my_rows = compact(recv_rows[:, :TL], valid, wanted)
    windowed = my_rows.reshape(mine, TL // N2, N2)
    strain_both = lax.all_gather(strain[0].astype(jnp.bfloat16), "det")
    asd_both = lax.all_gather(inv_asd[0], "det")
    spec_0, weight_0 = data_spectrum(strain_both[0], asd_both[0], tables)
    spec_1, weight_1 = data_spectrum(strain_both[1], asd_both[1], tables)
    shift = slide[0]

    def filter_template(kept_row):
        temp_real, temp_imag = template_transform(kept_row, tables)
        first = correlate_with(temp_real, temp_imag, spec_0, weight_0, tables)
        second = correlate_with(temp_real, temp_imag, spec_1, weight_1, tables)
        second = jnp.roll(second.reshape(n_blk, BLK), -shift, axis=0)
        network = first.reshape(n_blk, BLK) + second
        return jnp.max(network, axis=1)

    full = lax.map(filter_template, windowed)
    keep = lax.dynamic_slice_in_dim(full, detector * half_blk, half_blk, axis=1)
    give = lax.dynamic_slice_in_dim(full, (1 - detector) * half_blk, half_blk, axis=1)
    got = lax.ppermute(give, "det", [(0, 1), (1, 0)])
    peaks = jnp.where(
        detector == 0, jnp.concatenate([keep, got], axis=0), jnp.concatenate([got, keep], axis=0)
    )
    local_max = jnp.max(peaks, axis=0)
    loudest = group_max(local_max)
    return (peaks, loudest)


def solution(mesh):
    return jax.shard_map(
        shards,
        mesh=mesh,
        in_specs=(
            P("det", None),
            P("det", None),
            P(("grp", "filt"), None),
            P(("grp", "filt")),
            P(("grp", "filt")),
            P("grp"),
        ),
        out_specs=(P(("grp", "filt"), "det"), P("det")),
        check_vma=False,
    )
```

```python
import functools

import jax
import jax.numpy as jnp
from jax import lax
from jax.experimental import pallas as pl
from jax.experimental.pallas import tpu as pltpu
from jax.sharding import PartitionSpec as P

N1 = 256
N2 = 512
NFFT = 131072
BLK = 128
TL = 4096


TWO_PI = 6.283185307179586


def partner_2(value, axis, stride):
    mask = 2**stride
    pairs = [(source, source ^ mask) for source in range(lax.axis_size(axis))]
    return lax.ppermute(value, axis, pairs)


def angle_table(rows, cols, period):
    left = jnp.arange(rows, dtype=jnp.int32)[:, None]
    right = jnp.arange(cols, dtype=jnp.int32)[None, :]
    return TWO_PI / period * (left * right % period).astype(jnp.float32)


def make_tables():
    first = angle_table(N1, N1, N1)
    twist = angle_table(N1, N2, NFFT)
    second = angle_table(N2, N2 // 2, N2)
    back = angle_table(N2 // 2, N2, N2)
    return (
        jnp.cos(first).astype(jnp.bfloat16),
        jnp.sin(first).astype(jnp.bfloat16),
        jnp.cos(twist),
        jnp.sin(twist),
        jnp.cos(second).astype(jnp.bfloat16),
        jnp.sin(second).astype(jnp.bfloat16),
        jnp.cos(back).astype(jnp.bfloat16),
        jnp.sin(back).astype(jnp.bfloat16),
    )


def forward(signal, cos_rows, sin_rows, tables):
    cos_first, sin_first, cos_twist, sin_twist, cos_second, sin_second, cos_back, sin_back = tables
    real_a = jnp.dot(cos_rows, signal, preferred_element_type=jnp.float32)
    imag_a = -jnp.dot(sin_rows, signal, preferred_element_type=jnp.float32)
    real_b = (real_a * cos_twist + imag_a * sin_twist).astype(jnp.bfloat16)
    imag_b = (imag_a * cos_twist - real_a * sin_twist).astype(jnp.bfloat16)
    real_x = jnp.dot(real_b, cos_second, preferred_element_type=jnp.float32) + jnp.dot(
        imag_b, sin_second, preferred_element_type=jnp.float32
    )
    imag_x = jnp.dot(imag_b, cos_second, preferred_element_type=jnp.float32) - jnp.dot(
        real_b, sin_second, preferred_element_type=jnp.float32
    )
    return (real_x, imag_x)


def correlate(windowed, spectrum, weight2d, tables):
    cos_first, sin_first, cos_twist, sin_twist, cos_second, sin_second, cos_back, sin_back = tables
    rows_used = windowed.shape[0]
    temp_real, temp_imag = forward(
        windowed, cos_first[:, :rows_used], sin_first[:, :rows_used], tables
    )
    sigma = jnp.sum(weight2d * weight2d * (temp_real * temp_real + temp_imag * temp_imag))
    data_real, data_imag = spectrum
    q_real = (temp_real * data_real + temp_imag * data_imag).astype(jnp.bfloat16)
    q_imag = (temp_real * data_imag - temp_imag * data_real).astype(jnp.bfloat16)
    d_real = jnp.dot(q_real, cos_back, preferred_element_type=jnp.float32) - jnp.dot(
        q_imag, sin_back, preferred_element_type=jnp.float32
    )
    d_imag = jnp.dot(q_real, sin_back, preferred_element_type=jnp.float32) + jnp.dot(
        q_imag, cos_back, preferred_element_type=jnp.float32
    )
    e_real = (d_real * cos_twist - d_imag * sin_twist).astype(jnp.bfloat16)
    e_imag = (d_real * sin_twist + d_imag * cos_twist).astype(jnp.bfloat16)
    z_real = jnp.dot(cos_first, e_real, preferred_element_type=jnp.float32) - jnp.dot(
        sin_first, e_imag, preferred_element_type=jnp.float32
    )
    z_imag = jnp.dot(sin_first, e_real, preferred_element_type=jnp.float32) + jnp.dot(
        cos_first, e_imag, preferred_element_type=jnp.float32
    )
    return ((z_real * z_real + z_imag * z_imag) / (NFFT * sigma)).reshape(NFFT)


def data_spectrum(strain_row, weight_row, tables):
    weight2d = weight_row.reshape(N2 // 2, N1).T
    signal = strain_row.astype(jnp.bfloat16).reshape(N1, N2)
    real_s, imag_s = forward(signal, tables[0], tables[1], tables)
    return ((weight2d * real_s, weight2d * imag_s), weight2d)


def compact(rows, valid, wanted):
    slot_rank = jnp.cumsum(valid.astype(jnp.int32)) - 1
    picker = jnp.logical_and(valid[None, :], slot_rank[None, :] == wanted[:, None])
    return jnp.dot(picker.astype(jnp.bfloat16), rows, preferred_element_type=jnp.float32).astype(
        jnp.bfloat16
    )


def loudest_kernel(n_grp, n_filt, local_ref, out_ref, held, send_sems, recv_sems):
    det = lax.axis_index("det")
    size = n_grp * n_filt
    me = lax.axis_index("grp") * n_filt + lax.axis_index("filt")
    mesh_ids = pl.DeviceIdType.MESH

    def peer_of(i):
        peer = lax.rem(me + 1 + i, size)
        return (det, peer // n_filt, lax.rem(peer, n_filt))

    def copy_to(i):
        row = size - 2 - i
        return pltpu.make_async_remote_copy(
            src_ref=local_ref,
            dst_ref=held.at[row],
            send_sem=send_sems.at[i],
            recv_sem=recv_sems.at[row],
            device_id=peer_of(i),
            device_id_type=mesh_ids,
        )

    barrier = pltpu.get_barrier_semaphore()

    def greet(i, carry):
        pl.semaphore_signal(barrier, inc=1, device_id=peer_of(i), device_id_type=mesh_ids)
        return carry

    lax.fori_loop(0, size - 1, greet, 0)
    pl.semaphore_wait(barrier, size - 1)

    def send(i, carry):
        copy_to(i).start()
        return carry

    lax.fori_loop(0, size - 1, send, 0)

    def finish(i, carry):
        copy = copy_to(i)
        copy.wait_send()
        copy.wait_recv()
        return carry

    lax.fori_loop(0, size - 1, finish, 0)
    out_ref[...] = jnp.maximum(local_ref[...], jnp.max(held[...], axis=0))


def group_max(local_max):
    n_grp = lax.axis_size("grp")
    n_filt = lax.axis_size("filt")
    size = n_grp * n_filt
    width = local_max.shape[-1]
    out = pl.pallas_call(
        functools.partial(loudest_kernel, n_grp, n_filt),
        out_shape=jax.ShapeDtypeStruct((1, width), jnp.float32),
        in_specs=[pl.BlockSpec(memory_space=pltpu.VMEM)],
        out_specs=pl.BlockSpec(memory_space=pltpu.VMEM),
        scratch_shapes=[
            pltpu.VMEM((size - 1, 1, width), jnp.float32),
            pltpu.SemaphoreType.DMA((size - 1,)),
            pltpu.SemaphoreType.DMA((size - 1,)),
        ],
        compiler_params=pltpu.CompilerParams(collective_id=0, has_side_effects=True),
    )(local_max.reshape(1, width))
    return out.reshape(width)


def filter_kernel(
    rem_ref, x_ref, cfn_ref, sfn_ref, ct_ref, st_ref, cs_ref, ss_ref, cb_ref, sb_ref,
    cf_ref, sf_ref, cfr_ref, sfr_ref, pr_ref, pi_ref, w2_ref, out_ref, er_ref, ei_ref,
):
    f32 = jnp.float32
    bf16 = jnp.bfloat16
    x = x_ref[0]
    cos_twist = ct_ref[...]
    sin_twist = st_ref[...]
    real_a = jnp.dot(cfn_ref[...], x, preferred_element_type=f32)
    imag_a = -jnp.dot(sfn_ref[...], x, preferred_element_type=f32)
    real_b = (real_a * cos_twist + imag_a * sin_twist).astype(bf16)
    imag_b = (imag_a * cos_twist - real_a * sin_twist).astype(bf16)
    cos_second = cs_ref[...]
    sin_second = ss_ref[...]
    temp_real = jnp.dot(real_b, cos_second, preferred_element_type=f32) + jnp.dot(
        imag_b, sin_second, preferred_element_type=f32
    )
    temp_imag = jnp.dot(imag_b, cos_second, preferred_element_type=f32) - jnp.dot(
        real_b, sin_second, preferred_element_type=f32
    )
    power = temp_real * temp_real + temp_imag * temp_imag
    cos_back = cb_ref[...]
    sin_back = sb_ref[...]

    def back_half(d):
        sigma = jnp.sum(w2_ref[d] * power, axis=(0, 1), keepdims=True)
        data_real = pr_ref[d]
        data_imag = pi_ref[d]
        q_real = (temp_real * data_real + temp_imag * data_imag).astype(bf16)
        q_imag = (temp_real * data_imag - temp_imag * data_real).astype(bf16)
        d_real = jnp.dot(q_real, cos_back, preferred_element_type=f32) - jnp.dot(
            q_imag, sin_back, preferred_element_type=f32
        )
        d_imag = jnp.dot(q_real, sin_back, preferred_element_type=f32) + jnp.dot(
            q_imag, cos_back, preferred_element_type=f32
        )
        e_real = (d_real * cos_twist - d_imag * sin_twist).astype(bf16)
        e_imag = (d_real * sin_twist + d_imag * cos_twist).astype(bf16)
        return sigma, e_real, e_imag

    sigma0, e_real, e_imag = back_half(0)
    cos_first = cf_ref[...]
    sin_first = sf_ref[...]
    z_real = jnp.dot(cos_first, e_real, preferred_element_type=f32) - jnp.dot(
        sin_first, e_imag, preferred_element_type=f32
    )
    z_imag = jnp.dot(sin_first, e_real, preferred_element_type=f32) + jnp.dot(
        cos_first, e_imag, preferred_element_type=f32
    )
    first = (z_real * z_real + z_imag * z_imag) / (NFFT * sigma0)
    sigma1, e_real, e_imag = back_half(1)
    er_ref[...] = e_real
    ei_ref[...] = e_imag
    rem = rem_ref[0]
    tiles = first.shape[1] // BLK
    for col in range(tiles):
        src = lax.rem(col + rem, tiles)
        carry = (col + rem) // tiles
        cols = pl.ds(pl.multiple_of(src * BLK, BLK), BLK)
        e_r = er_ref[:, cols]
        e_i = ei_ref[:, cols]
        cos_rows = cfr_ref[carry]
        sin_rows = sfr_ref[carry]
        z_real = jnp.dot(cos_rows, e_r, preferred_element_type=f32) - jnp.dot(
            sin_rows, e_i, preferred_element_type=f32
        )
        z_imag = jnp.dot(sin_rows, e_r, preferred_element_type=f32) + jnp.dot(
            cos_rows, e_i, preferred_element_type=f32
        )
        second = (z_real * z_real + z_imag * z_imag) / (NFFT * sigma1)
        network = first[:, col * BLK:(col + 1) * BLK] + second
        out_ref[0, :, col:col + 1] = jnp.max(network, axis=1, keepdims=True)


def filter_bank(windowed, tables, spectra, weights, shift):
    cos_first, sin_first, cos_twist, sin_twist, cos_second, sin_second, cos_back, sin_back = tables
    count, rows_used, width = windowed.shape
    pad_rows = 128
    x = jnp.concatenate(
        [windowed, jnp.zeros((count, pad_rows - rows_used, width), windowed.dtype)], axis=1
    )
    tiles = N2 // BLK
    quot = shift // tiles
    rem = lax.rem(shift, tiles).reshape(1)
    cos_rolled = jnp.stack(
        [jnp.roll(cos_first, -quot, axis=0), jnp.roll(cos_first, -(quot + 1), axis=0)]
    )
    sin_rolled = jnp.stack(
        [jnp.roll(sin_first, -quot, axis=0), jnp.roll(sin_first, -(quot + 1), axis=0)]
    )
    data_real = jnp.stack([spectra[0][0], spectra[1][0]])
    data_imag = jnp.stack([spectra[0][1], spectra[1][1]])
    weight2 = jnp.stack([weights[0] * weights[0], weights[1] * weights[1]])
    operands = [
        cos_first[:, :pad_rows], sin_first[:, :pad_rows], cos_twist, sin_twist,
        cos_second, sin_second, cos_back, sin_back, cos_first, sin_first,
        cos_rolled, sin_rolled, data_real, data_imag, weight2,
    ]

    def whole(array):
        nd = array.ndim
        return pl.BlockSpec(array.shape, lambda i, r, nd=nd: (0,) * nd)

    grid_spec = pltpu.PrefetchScalarGridSpec(
        num_scalar_prefetch=1,
        grid=(count,),
        in_specs=[pl.BlockSpec((1, pad_rows, width), lambda i, r: (i, 0, 0))]
        + [whole(a) for a in operands],
        out_specs=pl.BlockSpec((1, N1, tiles), lambda i, r: (i, 0, 0)),
        scratch_shapes=[pltpu.VMEM((N1, N2), jnp.bfloat16), pltpu.VMEM((N1, N2), jnp.bfloat16)],
    )
    matmuls = 2 * N1 * pad_rows * N2 + 4 * N1 * N2 * (N2 // 2) + 16 * N1 * (N2 // 2) * N2
    out = pl.pallas_call(
        filter_kernel,
        out_shape=jax.ShapeDtypeStruct((count, N1, tiles), jnp.float32),
        grid_spec=grid_spec,
        compiler_params=pltpu.CompilerParams(vmem_limit_bytes=48 * 1024 * 1024),
        cost_estimate=pl.CostEstimate(
            flops=2 * matmuls * count, transcendentals=0, bytes_accessed=8 * 1024 * 1024
        ),
    )(rem, x, *operands)
    return out.reshape(count, N1 * tiles)


def shards(strain, inv_asd, templates, chirp_blocks, owner, slide):
    tables = lax.optimization_barrier(make_tables())
    detector = lax.axis_index("det")
    per_dev = templates.shape[0]
    mine = per_dev // 2
    n_blk = NFFT // BLK
    half_blk = n_blk // 2
    filt_count = lax.axis_size("filt")
    capacity = (per_dev + filt_count - 1) // filt_count
    positions = jnp.arange(per_dev, dtype=jnp.int32)
    same_owner = owner[:, None] == owner[None, :]
    earlier = positions[None, :] < positions[:, None]
    owner_rank = jnp.sum(jnp.logical_and(same_owner, earlier).astype(jnp.int32), axis=1)
    dest_slot = owner * capacity + owner_rank
    slot_ids = jnp.arange(filt_count * capacity, dtype=jnp.int32)[:, None]
    placing = slot_ids == dest_slot[None, :]
    samples = jnp.arange(TL, dtype=jnp.int32)
    windowed = jnp.where(
        samples[None, :] < BLK * chirp_blocks[:, None], templates, jnp.zeros_like(templates)
    )
    payload = jnp.concatenate([windowed, jnp.ones((per_dev, 128), jnp.bfloat16)], axis=1)
    send_rows = jnp.dot(
        placing.astype(jnp.bfloat16), payload, preferred_element_type=jnp.float32
    ).astype(jnp.bfloat16)
    recv_rows = lax.all_to_all(send_rows, "filt", split_axis=0, concat_axis=0, tiled=True)
    valid = recv_rows[:, TL] > 0.5
    wanted = detector * mine + jnp.arange(mine, dtype=jnp.int32)
    my_rows = compact(recv_rows[:, :TL], valid, wanted)
    windowed = my_rows.reshape(mine, TL // N2, N2)
    strain_both = lax.all_gather(strain[0].astype(jnp.bfloat16), "det")
    asd_both = lax.all_gather(inv_asd[0], "det")
    spec_0, weight_0 = data_spectrum(strain_both[0], asd_both[0], tables)
    spec_1, weight_1 = data_spectrum(strain_both[1], asd_both[1], tables)
    full = filter_bank(windowed, tables, (spec_0, spec_1), (weight_0, weight_1), slide[0])
    keep = lax.dynamic_slice_in_dim(full, detector * half_blk, half_blk, axis=1)
    give = lax.dynamic_slice_in_dim(full, (1 - detector) * half_blk, half_blk, axis=1)
    got = lax.ppermute(give, "det", [(0, 1), (1, 0)])
    peaks = jnp.where(
        detector == 0, jnp.concatenate([keep, got], axis=0), jnp.concatenate([got, keep], axis=0)
    )
    local_max = jnp.max(peaks, axis=0)
    loudest = group_max(local_max)
    return (peaks, loudest)


def solution(mesh):
    return jax.shard_map(
        shards,
        mesh=mesh,
        in_specs=(
            P("det", None),
            P("det", None),
            P(("grp", "filt"), None),
            P(("grp", "filt")),
            P(("grp", "filt")),
            P("grp"),
        ),
        out_specs=(P(("grp", "filt"), "det"), P("det")),
        check_vma=False,
    )
```

```python
import functools

import jax
import jax.numpy as jnp
from jax import lax
from jax.experimental import pallas as pl
from jax.experimental.pallas import tpu as pltpu
from jax.sharding import PartitionSpec as P

N1 = 256
N2 = 512
NFFT = 131072
BLK = 128
TL = 4096


TWO_PI = 6.283185307179586


def partner_2(value, axis, stride):
    mask = 2**stride
    pairs = [(source, source ^ mask) for source in range(lax.axis_size(axis))]
    return lax.ppermute(value, axis, pairs)


def angle_table(rows, cols, period):
    left = jnp.arange(rows, dtype=jnp.int32)[:, None]
    right = jnp.arange(cols, dtype=jnp.int32)[None, :]
    return TWO_PI / period * (left * right % period).astype(jnp.float32)


def make_tables():
    twist = angle_table(N1, N2, NFFT)
    second = angle_table(N2, N2 // 2, N2)
    cos_second = jnp.cos(second).astype(jnp.bfloat16)
    sin_second = jnp.sin(second).astype(jnp.bfloat16)
    return (
        cos_second[0::2],
        sin_second[0::2],
        jnp.cos(twist),
        jnp.sin(twist),
        cos_second,
        sin_second,
    )


def compact(rows, valid, wanted):
    slot_rank = jnp.cumsum(valid.astype(jnp.int32)) - 1
    picker = jnp.logical_and(valid[None, :], slot_rank[None, :] == wanted[:, None])
    return jnp.dot(picker.astype(jnp.bfloat16), rows, preferred_element_type=jnp.float32).astype(
        jnp.bfloat16
    )


def loudest_kernel(n_grp, n_filt, local_ref, out_ref, held, send_sems, recv_sems):
    det = lax.axis_index("det")
    size = n_grp * n_filt
    me = lax.axis_index("grp") * n_filt + lax.axis_index("filt")
    mesh_ids = pl.DeviceIdType.MESH

    def peer_of(i):
        peer = lax.rem(me + 1 + i, size)
        return (det, peer // n_filt, lax.rem(peer, n_filt))

    def copy_to(i):
        row = size - 2 - i
        return pltpu.make_async_remote_copy(
            src_ref=local_ref,
            dst_ref=held.at[row],
            send_sem=send_sems.at[i],
            recv_sem=recv_sems.at[row],
            device_id=peer_of(i),
            device_id_type=mesh_ids,
        )

    barrier = pltpu.get_barrier_semaphore()

    def greet(i, carry):
        pl.semaphore_signal(barrier, inc=1, device_id=peer_of(i), device_id_type=mesh_ids)
        return carry

    lax.fori_loop(0, size - 1, greet, 0)
    pl.semaphore_wait(barrier, size - 1)

    def send(i, carry):
        copy_to(i).start()
        return carry

    lax.fori_loop(0, size - 1, send, 0)

    def finish(i, carry):
        copy = copy_to(i)
        copy.wait_send()
        copy.wait_recv()
        return carry

    lax.fori_loop(0, size - 1, finish, 0)
    out_ref[...] = jnp.maximum(local_ref[...], jnp.max(held[...], axis=0))


def group_max(local_max):
    n_grp = lax.axis_size("grp")
    n_filt = lax.axis_size("filt")
    size = n_grp * n_filt
    width = local_max.shape[-1]
    out = pl.pallas_call(
        functools.partial(loudest_kernel, n_grp, n_filt),
        out_shape=jax.ShapeDtypeStruct((1, width), jnp.float32),
        in_specs=[pl.BlockSpec(memory_space=pltpu.VMEM)],
        out_specs=pl.BlockSpec(memory_space=pltpu.VMEM),
        scratch_shapes=[
            pltpu.VMEM((size - 1, 1, width), jnp.float32),
            pltpu.SemaphoreType.DMA((size - 1,)),
            pltpu.SemaphoreType.DMA((size - 1,)),
        ],
        compiler_params=pltpu.CompilerParams(collective_id=0, has_side_effects=True),
    )(local_max.reshape(1, width))
    return out.reshape(width)


def dot_nt(left, right):
    return lax.dot_general(
        left, right, (((1,), (1,)), ((), ())), preferred_element_type=jnp.float32
    )


def filter_kernel(
    scalar_ref, x_ref, cfn_ref, sfn_ref, ct_ref, st_ref, cs_ref, ss_ref, cf_ref, sf_ref,
    cfr_ref, sfr_ref, sown_ref, soth_ref, wown_ref, woth_ref, out_ref,
    er_ref, ei_ref, pr_ref, pi_ref, w2_ref,
):
    f32 = jnp.float32
    bf16 = jnp.bfloat16

    def first_stage(cos_rows, sin_rows, x):
        cos_twist = ct_ref[...]
        sin_twist = st_ref[...]
        real_a = jnp.dot(cos_rows, x, preferred_element_type=f32)
        imag_a = -jnp.dot(sin_rows, x, preferred_element_type=f32)
        real_b = (real_a * cos_twist + imag_a * sin_twist).astype(bf16)
        imag_b = (imag_a * cos_twist - real_a * sin_twist).astype(bf16)
        cos_second = cs_ref[...]
        sin_second = ss_ref[...]
        real_x = jnp.dot(real_b, cos_second, preferred_element_type=f32) + jnp.dot(
            imag_b, sin_second, preferred_element_type=f32
        )
        imag_x = jnp.dot(imag_b, cos_second, preferred_element_type=f32) - jnp.dot(
            real_b, sin_second, preferred_element_type=f32
        )
        return real_x, imag_x

    @pl.when(pl.program_id(0) == 0)
    def _():
        det = scalar_ref[1]
        for slot, sig_ref, w_ref in ((det, sown_ref, wown_ref), (1 - det, soth_ref, woth_ref)):
            real_s, imag_s = first_stage(cf_ref[...], sf_ref[...], sig_ref[...])
            weight = jnp.transpose(w_ref[...])
            pr_ref[slot] = weight * real_s
            pi_ref[slot] = weight * imag_s
            w2_ref[slot] = weight * weight

    temp_real, temp_imag = first_stage(cfn_ref[...], sfn_ref[...], x_ref[0])
    power = temp_real * temp_real + temp_imag * temp_imag
    cos_back = cs_ref[...]
    sin_back = ss_ref[...]

    def back_half(d):
        cos_twist = ct_ref[...]
        sin_twist = st_ref[...]
        sigma = jnp.sum(w2_ref[d] * power, axis=(0, 1), keepdims=True)
        data_real = pr_ref[d]
        data_imag = pi_ref[d]
        q_real = (temp_real * data_real + temp_imag * data_imag).astype(bf16)
        q_imag = (temp_real * data_imag - temp_imag * data_real).astype(bf16)
        d_real = dot_nt(q_real, cos_back) - dot_nt(q_imag, sin_back)
        d_imag = dot_nt(q_real, sin_back) + dot_nt(q_imag, cos_back)
        e_real = (d_real * cos_twist - d_imag * sin_twist).astype(bf16)
        e_imag = (d_real * sin_twist + d_imag * cos_twist).astype(bf16)
        return sigma, e_real, e_imag

    sigma0, e_real, e_imag = back_half(0)
    cos_first = cf_ref[...]
    sin_first = sf_ref[...]
    z_real = jnp.dot(cos_first, e_real, preferred_element_type=f32) - jnp.dot(
        sin_first, e_imag, preferred_element_type=f32
    )
    z_imag = jnp.dot(sin_first, e_real, preferred_element_type=f32) + jnp.dot(
        cos_first, e_imag, preferred_element_type=f32
    )
    first = (z_real * z_real + z_imag * z_imag) / (NFFT * sigma0)
    sigma1, e_real, e_imag = back_half(1)
    er_ref[...] = e_real
    ei_ref[...] = e_imag
    rem = scalar_ref[0]
    tiles = first.shape[1] // BLK
    for col in range(tiles):
        src = lax.rem(col + rem, tiles)
        carry = (col + rem) // tiles
        cols = pl.ds(pl.multiple_of(src * BLK, BLK), BLK)
        e_r = er_ref[:, cols]
        e_i = ei_ref[:, cols]
        cos_rows = cfr_ref[carry]
        sin_rows = sfr_ref[carry]
        z_real = jnp.dot(cos_rows, e_r, preferred_element_type=f32) - jnp.dot(
            sin_rows, e_i, preferred_element_type=f32
        )
        z_imag = jnp.dot(sin_rows, e_r, preferred_element_type=f32) + jnp.dot(
            cos_rows, e_i, preferred_element_type=f32
        )
        second = (z_real * z_real + z_imag * z_imag) / (NFFT * sigma1)
        network = first[:, col * BLK:(col + 1) * BLK] + second
        out_ref[0, :, col:col + 1] = jnp.max(network, axis=1, keepdims=True)


def filter_bank(windowed, tables, signals, weights, shift, det):
    cos_first, sin_first, cos_twist, sin_twist, cos_second, sin_second = tables
    count, rows_used, width = windowed.shape
    pad_rows = 128
    x = jnp.concatenate(
        [windowed, jnp.zeros((count, pad_rows - rows_used, width), windowed.dtype)], axis=1
    )
    tiles = N2 // BLK
    quot = shift // tiles
    scalars = jnp.stack([lax.rem(shift, tiles), det]).astype(jnp.int32)
    doubled_cos = jnp.concatenate([cos_first, cos_first], axis=0)
    doubled_sin = jnp.concatenate([sin_first, sin_first], axis=0)
    cos_rolled = jnp.stack(
        [lax.dynamic_slice_in_dim(doubled_cos, quot + v, N1) for v in range(2)]
    )
    sin_rolled = jnp.stack(
        [lax.dynamic_slice_in_dim(doubled_sin, quot + v, N1) for v in range(2)]
    )
    operands = [
        cos_first[:, :pad_rows], sin_first[:, :pad_rows], cos_twist, sin_twist,
        cos_second, sin_second, cos_first, sin_first, cos_rolled, sin_rolled,
        signals[0], signals[1], weights[0], weights[1],
    ]

    def whole(array):
        nd = array.ndim
        return pl.BlockSpec(array.shape, lambda i, r, nd=nd: (0,) * nd)

    grid_spec = pltpu.PrefetchScalarGridSpec(
        num_scalar_prefetch=1,
        grid=(count,),
        in_specs=[pl.BlockSpec((1, pad_rows, width), lambda i, r: (i, 0, 0))]
        + [whole(a) for a in operands],
        out_specs=pl.BlockSpec((1, N1, tiles), lambda i, r: (i, 0, 0)),
        scratch_shapes=[
            pltpu.VMEM((N1, N2), jnp.bfloat16),
            pltpu.VMEM((N1, N2), jnp.bfloat16),
            pltpu.VMEM((2, N1, N2 // 2), jnp.float32),
            pltpu.VMEM((2, N1, N2 // 2), jnp.float32),
            pltpu.VMEM((2, N1, N2 // 2), jnp.float32),
        ],
    )
    matmuls = 2 * N1 * pad_rows * N2 + 4 * N1 * N2 * (N2 // 2) + 16 * N1 * (N2 // 2) * N2
    out = pl.pallas_call(
        filter_kernel,
        out_shape=jax.ShapeDtypeStruct((count, N1, tiles), jnp.float32),
        grid_spec=grid_spec,
        compiler_params=pltpu.CompilerParams(vmem_limit_bytes=48 * 1024 * 1024),
        cost_estimate=pl.CostEstimate(
            flops=2 * matmuls * count, transcendentals=0, bytes_accessed=8 * 1024 * 1024
        ),
    )(scalars, x, *operands)
    return out.reshape(count, N1 * tiles)


def shards(strain, inv_asd, templates, chirp_blocks, owner, slide):
    tables = lax.optimization_barrier(make_tables())
    detector = lax.axis_index("det")
    per_dev = templates.shape[0]
    mine = per_dev // 2
    n_blk = NFFT // BLK
    half_blk = n_blk // 2
    filt_count = lax.axis_size("filt")
    capacity = (per_dev + filt_count - 1) // filt_count
    positions = jnp.arange(per_dev, dtype=jnp.int32)
    same_owner = owner[:, None] == owner[None, :]
    earlier = positions[None, :] < positions[:, None]
    owner_rank = jnp.sum(jnp.logical_and(same_owner, earlier).astype(jnp.int32), axis=1)
    dest_slot = owner * capacity + owner_rank
    slot_ids = jnp.arange(filt_count * capacity, dtype=jnp.int32)[:, None]
    placing = slot_ids == dest_slot[None, :]
    samples = jnp.arange(TL, dtype=jnp.int32)
    windowed = jnp.where(
        samples[None, :] < BLK * chirp_blocks[:, None], templates, jnp.zeros_like(templates)
    )
    payload = jnp.concatenate([windowed, jnp.ones((per_dev, 128), jnp.bfloat16)], axis=1)
    send_rows = jnp.dot(
        placing.astype(jnp.bfloat16), payload, preferred_element_type=jnp.float32
    ).astype(jnp.bfloat16)
    recv_rows = lax.all_to_all(send_rows, "filt", split_axis=0, concat_axis=0, tiled=True)
    valid = recv_rows[:, TL] > 0.5
    wanted = detector * mine + jnp.arange(mine, dtype=jnp.int32)
    my_rows = compact(recv_rows[:, :TL], valid, wanted)
    windowed = my_rows.reshape(mine, TL // N2, N2)
    swap = [(0, 1), (1, 0)]
    own_signal = strain[0].astype(jnp.bfloat16).reshape(N1, N2)
    own_weight = inv_asd[0].reshape(N2 // 2, N1)
    other_signal = lax.ppermute(own_signal, "det", swap)
    other_weight = lax.ppermute(own_weight, "det", swap)
    full = filter_bank(
        windowed, tables, (own_signal, other_signal), (own_weight, other_weight),
        slide[0], detector,
    )
    keep = lax.dynamic_slice_in_dim(full, detector * half_blk, half_blk, axis=1)
    give = lax.dynamic_slice_in_dim(full, (1 - detector) * half_blk, half_blk, axis=1)
    got = lax.ppermute(give, "det", swap)
    peaks = jnp.where(
        detector == 0, jnp.concatenate([keep, got], axis=0), jnp.concatenate([got, keep], axis=0)
    )
    local_max = jnp.max(peaks, axis=0)
    loudest = group_max(local_max)
    return (peaks, loudest)


def solution(mesh):
    return jax.shard_map(
        shards,
        mesh=mesh,
        in_specs=(
            P("det", None),
            P("det", None),
            P(("grp", "filt"), None),
            P(("grp", "filt")),
            P(("grp", "filt")),
            P("grp"),
        ),
        out_specs=(P(("grp", "filt"), "det"), P("det")),
        check_vma=False,
    )
```

```python
import functools

import jax
import jax.numpy as jnp
from jax import lax
from jax.experimental import pallas as pl
from jax.experimental.pallas import tpu as pltpu
from jax.sharding import PartitionSpec as P

N1 = 256
N2 = 512
NFFT = 131072
BLK = 128
TL = 4096


TWO_PI = 6.283185307179586


def partner_2(value, axis, stride):
    mask = 2**stride
    pairs = [(source, source ^ mask) for source in range(lax.axis_size(axis))]
    return lax.ppermute(value, axis, pairs)


def angle_table(rows, cols, period):
    left = jnp.arange(rows, dtype=jnp.int32)[:, None]
    right = jnp.arange(cols, dtype=jnp.int32)[None, :]
    return TWO_PI / period * (left * right % period).astype(jnp.float32)


def make_tables():
    twist = angle_table(N1, N2, NFFT)
    second = angle_table(N2, N2 // 2, N2)
    cos_second = jnp.cos(second).astype(jnp.bfloat16)
    sin_second = jnp.sin(second).astype(jnp.bfloat16)
    return (
        cos_second[0::2],
        sin_second[0::2],
        jnp.cos(twist),
        jnp.sin(twist),
        cos_second,
        sin_second,
    )


def compact(rows, valid, wanted):
    slot_rank = jnp.cumsum(valid.astype(jnp.int32)) - 1
    picker = jnp.logical_and(valid[None, :], slot_rank[None, :] == wanted[:, None])
    return jnp.dot(picker.astype(jnp.bfloat16), rows, preferred_element_type=jnp.float32).astype(
        jnp.bfloat16
    )


def stage_layout(n_grp, n_filt):
    inner = 8 if n_filt % 8 == 0 else n_filt
    return ((inner, 1), (n_filt // inner, inner), (n_grp, 0))


def loudest_kernel(stages, local_ref, out_ref, acc_ref, *scratch):
    det = lax.axis_index("det")
    grp = lax.axis_index("grp")
    filt = lax.axis_index("filt")
    mesh_ids = pl.DeviceIdType.MESH

    def position(size, stride):
        if stride == 0:
            return grp
        return lax.rem(filt // stride, size)

    def peer(size, stride, target):
        if stride == 0:
            return (det, target, filt)
        here = position(size, stride)
        return (det, grp, filt + (target - here) * stride)

    live = [(size, stride) for size, stride in stages if size > 1]
    barrier = pltpu.get_barrier_semaphore()
    for size, stride in live:
        here = position(size, stride)
        for i in range(size - 1):
            target = lax.rem(here + 1 + i, size)
            pl.semaphore_signal(
                barrier, inc=1, device_id=peer(size, stride, target), device_id_type=mesh_ids
            )
    pl.semaphore_wait(barrier, sum(size - 1 for size, _ in live))
    value = local_ref[...]
    source = local_ref
    for k, (size, stride) in enumerate(live):
        held, send_sems, recv_sems = scratch[3 * k:3 * k + 3]
        here = position(size, stride)
        copies = []
        for i in range(size - 1):
            target = lax.rem(here + 1 + i, size)
            row = size - 2 - i
            copy = pltpu.make_async_remote_copy(
                src_ref=source,
                dst_ref=held.at[row],
                send_sem=send_sems.at[i],
                recv_sem=recv_sems.at[row],
                device_id=peer(size, stride, target),
                device_id_type=mesh_ids,
            )
            copy.start()
            copies.append(copy)
        for copy in copies:
            copy.wait_send()
            copy.wait_recv()
        value = jnp.maximum(value, jnp.max(held[...], axis=0))
        if k + 1 < len(live):
            acc_ref[k] = value
            source = acc_ref.at[k]
    out_ref[...] = value


def group_max(local_max):
    stages = stage_layout(lax.axis_size("grp"), lax.axis_size("filt"))
    live = [size for size, _ in stages if size > 1]
    width = local_max.shape[-1]
    scratch = [pltpu.VMEM((max(len(live), 1), 1, width), jnp.float32)]
    for size in live:
        scratch += [
            pltpu.VMEM((size - 1, 1, width), jnp.float32),
            pltpu.SemaphoreType.DMA((size - 1,)),
            pltpu.SemaphoreType.DMA((size - 1,)),
        ]
    out = pl.pallas_call(
        functools.partial(loudest_kernel, stages),
        out_shape=jax.ShapeDtypeStruct((1, width), jnp.float32),
        in_specs=[pl.BlockSpec(memory_space=pltpu.VMEM)],
        out_specs=pl.BlockSpec(memory_space=pltpu.VMEM),
        scratch_shapes=scratch,
        compiler_params=pltpu.CompilerParams(collective_id=0, has_side_effects=True),
    )(local_max.reshape(1, width))
    return out.reshape(width)


def dot_nt(left, right):
    return lax.dot_general(
        left, right, (((1,), (1,)), ((), ())), preferred_element_type=jnp.float32
    )


def filter_kernel(
    scalar_ref, x_ref, cfn_ref, sfn_ref, ct_ref, st_ref, cs_ref, ss_ref, cf_ref, sf_ref,
    cfr_ref, sfr_ref, sown_ref, soth_ref, wown_ref, woth_ref, out_ref,
    er_ref, ei_ref, pr_ref, pi_ref, w2_ref,
):
    f32 = jnp.float32
    bf16 = jnp.bfloat16

    def first_stage(cos_rows, sin_rows, x):
        cos_twist = ct_ref[...]
        sin_twist = st_ref[...]
        real_a = jnp.dot(cos_rows, x, preferred_element_type=f32)
        imag_a = -jnp.dot(sin_rows, x, preferred_element_type=f32)
        real_b = (real_a * cos_twist + imag_a * sin_twist).astype(bf16)
        imag_b = (imag_a * cos_twist - real_a * sin_twist).astype(bf16)
        cos_second = cs_ref[...]
        sin_second = ss_ref[...]
        real_x = jnp.dot(real_b, cos_second, preferred_element_type=f32) + jnp.dot(
            imag_b, sin_second, preferred_element_type=f32
        )
        imag_x = jnp.dot(imag_b, cos_second, preferred_element_type=f32) - jnp.dot(
            real_b, sin_second, preferred_element_type=f32
        )
        return real_x, imag_x

    @pl.when(pl.program_id(0) == 0)
    def _():
        det = scalar_ref[1]
        for slot, sig_ref, w_ref in ((det, sown_ref, wown_ref), (1 - det, soth_ref, woth_ref)):
            real_s, imag_s = first_stage(cf_ref[...], sf_ref[...], sig_ref[...])
            weight = jnp.transpose(w_ref[...])
            pr_ref[slot] = weight * real_s
            pi_ref[slot] = weight * imag_s
            w2_ref[slot] = weight * weight

    temp_real, temp_imag = first_stage(cfn_ref[...], sfn_ref[...], x_ref[0])
    power = temp_real * temp_real + temp_imag * temp_imag
    cos_back = cs_ref[...]
    sin_back = ss_ref[...]

    def back_half(d):
        cos_twist = ct_ref[...]
        sin_twist = st_ref[...]
        sigma = jnp.sum(w2_ref[d] * power, axis=(0, 1), keepdims=True)
        data_real = pr_ref[d]
        data_imag = pi_ref[d]
        q_real = (temp_real * data_real + temp_imag * data_imag).astype(bf16)
        q_imag = (temp_real * data_imag - temp_imag * data_real).astype(bf16)
        d_real = dot_nt(q_real, cos_back) - dot_nt(q_imag, sin_back)
        d_imag = dot_nt(q_real, sin_back) + dot_nt(q_imag, cos_back)
        e_real = (d_real * cos_twist - d_imag * sin_twist).astype(bf16)
        e_imag = (d_real * sin_twist + d_imag * cos_twist).astype(bf16)
        return sigma, e_real, e_imag

    sigma0, e_real, e_imag = back_half(0)
    cos_first = cf_ref[...]
    sin_first = sf_ref[...]
    z_real = jnp.dot(cos_first, e_real, preferred_element_type=f32) - jnp.dot(
        sin_first, e_imag, preferred_element_type=f32
    )
    z_imag = jnp.dot(sin_first, e_real, preferred_element_type=f32) + jnp.dot(
        cos_first, e_imag, preferred_element_type=f32
    )
    first = (z_real * z_real + z_imag * z_imag) / (NFFT * sigma0)
    sigma1, e_real, e_imag = back_half(1)
    er_ref[...] = e_real
    ei_ref[...] = e_imag
    rem = scalar_ref[0]
    tiles = first.shape[1] // BLK
    for col in range(tiles):
        src = lax.rem(col + rem, tiles)
        carry = (col + rem) // tiles
        cols = pl.ds(pl.multiple_of(src * BLK, BLK), BLK)
        e_r = er_ref[:, cols]
        e_i = ei_ref[:, cols]
        cos_rows = cfr_ref[carry]
        sin_rows = sfr_ref[carry]
        z_real = jnp.dot(cos_rows, e_r, preferred_element_type=f32) - jnp.dot(
            sin_rows, e_i, preferred_element_type=f32
        )
        z_imag = jnp.dot(sin_rows, e_r, preferred_element_type=f32) + jnp.dot(
            cos_rows, e_i, preferred_element_type=f32
        )
        second = (z_real * z_real + z_imag * z_imag) / (NFFT * sigma1)
        network = first[:, col * BLK:(col + 1) * BLK] + second
        out_ref[0, :, col:col + 1] = jnp.max(network, axis=1, keepdims=True)


def filter_bank(windowed, tables, signals, weights, shift, det):
    cos_first, sin_first, cos_twist, sin_twist, cos_second, sin_second = tables
    count, rows_used, width = windowed.shape
    pad_rows = 128
    x = jnp.concatenate(
        [windowed, jnp.zeros((count, pad_rows - rows_used, width), windowed.dtype)], axis=1
    )
    tiles = N2 // BLK
    quot = shift // tiles
    scalars = jnp.stack([lax.rem(shift, tiles), det]).astype(jnp.int32)
    doubled_cos = jnp.concatenate([cos_first, cos_first], axis=0)
    doubled_sin = jnp.concatenate([sin_first, sin_first], axis=0)
    cos_rolled = jnp.stack(
        [lax.dynamic_slice_in_dim(doubled_cos, quot + v, N1) for v in range(2)]
    )
    sin_rolled = jnp.stack(
        [lax.dynamic_slice_in_dim(doubled_sin, quot + v, N1) for v in range(2)]
    )
    operands = [
        cos_first[:, :pad_rows], sin_first[:, :pad_rows], cos_twist, sin_twist,
        cos_second, sin_second, cos_first, sin_first, cos_rolled, sin_rolled,
        signals[0], signals[1], weights[0], weights[1],
    ]

    def whole(array):
        nd = array.ndim
        return pl.BlockSpec(array.shape, lambda i, r, nd=nd: (0,) * nd)

    grid_spec = pltpu.PrefetchScalarGridSpec(
        num_scalar_prefetch=1,
        grid=(count,),
        in_specs=[pl.BlockSpec((1, pad_rows, width), lambda i, r: (i, 0, 0))]
        + [whole(a) for a in operands],
        out_specs=pl.BlockSpec((1, N1, tiles), lambda i, r: (i, 0, 0)),
        scratch_shapes=[
            pltpu.VMEM((N1, N2), jnp.bfloat16),
            pltpu.VMEM((N1, N2), jnp.bfloat16),
            pltpu.VMEM((2, N1, N2 // 2), jnp.float32),
            pltpu.VMEM((2, N1, N2 // 2), jnp.float32),
            pltpu.VMEM((2, N1, N2 // 2), jnp.float32),
        ],
    )
    matmuls = 2 * N1 * pad_rows * N2 + 4 * N1 * N2 * (N2 // 2) + 16 * N1 * (N2 // 2) * N2
    out = pl.pallas_call(
        filter_kernel,
        out_shape=jax.ShapeDtypeStruct((count, N1, tiles), jnp.float32),
        grid_spec=grid_spec,
        compiler_params=pltpu.CompilerParams(vmem_limit_bytes=48 * 1024 * 1024),
        cost_estimate=pl.CostEstimate(
            flops=2 * matmuls * count, transcendentals=0, bytes_accessed=8 * 1024 * 1024
        ),
    )(scalars, x, *operands)
    return out.reshape(count, N1 * tiles)


def shards(strain, inv_asd, templates, chirp_blocks, owner, slide):
    tables = lax.optimization_barrier(make_tables())
    detector = lax.axis_index("det")
    per_dev = templates.shape[0]
    mine = per_dev // 2
    n_blk = NFFT // BLK
    half_blk = n_blk // 2
    filt_count = lax.axis_size("filt")
    capacity = (per_dev + filt_count - 1) // filt_count
    positions = jnp.arange(per_dev, dtype=jnp.int32)
    same_owner = owner[:, None] == owner[None, :]
    earlier = positions[None, :] < positions[:, None]
    owner_rank = jnp.sum(jnp.logical_and(same_owner, earlier).astype(jnp.int32), axis=1)
    dest_slot = owner * capacity + owner_rank
    slot_ids = jnp.arange(filt_count * capacity, dtype=jnp.int32)[:, None]
    placing = slot_ids == dest_slot[None, :]
    samples = jnp.arange(TL, dtype=jnp.int32)
    windowed = jnp.where(
        samples[None, :] < BLK * chirp_blocks[:, None], templates, jnp.zeros_like(templates)
    )
    payload = jnp.concatenate([windowed, jnp.ones((per_dev, 128), jnp.bfloat16)], axis=1)
    send_rows = jnp.dot(
        placing.astype(jnp.bfloat16), payload, preferred_element_type=jnp.float32
    ).astype(jnp.bfloat16)
    recv_rows = lax.all_to_all(send_rows, "filt", split_axis=0, concat_axis=0, tiled=True)
    valid = recv_rows[:, TL] > 0.5
    wanted = detector * mine + jnp.arange(mine, dtype=jnp.int32)
    my_rows = compact(recv_rows[:, :TL], valid, wanted)
    windowed = my_rows.reshape(mine, TL // N2, N2)
    swap = [(0, 1), (1, 0)]
    own_signal = strain[0].astype(jnp.bfloat16).reshape(N1, N2)
    own_weight = inv_asd[0].reshape(N2 // 2, N1)
    other_signal = lax.ppermute(own_signal, "det", swap)
    other_weight = lax.ppermute(own_weight, "det", swap)
    full = filter_bank(
        windowed, tables, (own_signal, other_signal), (own_weight, other_weight),
        slide[0], detector,
    )
    keep = lax.dynamic_slice_in_dim(full, detector * half_blk, half_blk, axis=1)
    give = lax.dynamic_slice_in_dim(full, (1 - detector) * half_blk, half_blk, axis=1)
    got = lax.ppermute(give, "det", swap)
    peaks = jnp.where(
        detector == 0, jnp.concatenate([keep, got], axis=0), jnp.concatenate([got, keep], axis=0)
    )
    local_max = jnp.max(peaks, axis=0)
    loudest = group_max(local_max)
    return (peaks, loudest)


def solution(mesh):
    return jax.shard_map(
        shards,
        mesh=mesh,
        in_specs=(
            P("det", None),
            P("det", None),
            P(("grp", "filt"), None),
            P(("grp", "filt")),
            P(("grp", "filt")),
            P("grp"),
        ),
        out_specs=(P(("grp", "filt"), "det"), P("det")),
        check_vma=False,
    )
```

```python
import functools

import jax
import ml_dtypes
import numpy as np
import jax.numpy as jnp
from jax import lax
from jax.experimental import pallas as pl
from jax.experimental.pallas import tpu as pltpu
from jax.sharding import PartitionSpec as P

N1 = 256
N2 = 512
NFFT = 131072
BLK = 128
TL = 4096


TWO_PI = 6.283185307179586


def partner_2(value, axis, stride):
    mask = 2**stride
    pairs = [(source, source ^ mask) for source in range(lax.axis_size(axis))]
    return lax.ppermute(value, axis, pairs)


def angle_table(rows, cols, period):
    left = np.arange(rows, dtype=np.int64)[:, None]
    right = np.arange(cols, dtype=np.int64)[None, :]
    turns = (left * right % period).astype(np.float32)
    return np.float32(TWO_PI / period) * turns


def make_tables():
    twist = angle_table(N1, N2, NFFT).astype(np.float64)
    second = angle_table(N2, N2 // 2, N2).astype(np.float64)
    cos_second = np.cos(second).astype(np.float32).astype(ml_dtypes.bfloat16)
    sin_second = np.sin(second).astype(np.float32).astype(ml_dtypes.bfloat16)
    return tuple(
        jnp.asarray(table)
        for table in (
            cos_second[0::2],
            sin_second[0::2],
            np.cos(twist).astype(np.float32),
            np.sin(twist).astype(np.float32),
            cos_second,
            sin_second,
        )
    )


def compact(rows, valid, wanted):
    slot_rank = jnp.cumsum(valid.astype(jnp.int32)) - 1
    picker = jnp.logical_and(valid[None, :], slot_rank[None, :] == wanted[:, None])
    return jnp.dot(picker.astype(jnp.bfloat16), rows, preferred_element_type=jnp.float32).astype(
        jnp.bfloat16
    )


def stage_layout(n_grp, n_filt):
    inner = 8 if n_filt % 8 == 0 else n_filt
    return ((inner, 1), (n_filt // inner, inner), (n_grp, 0))


def loudest_kernel(stages, local_ref, out_ref, acc_ref, *scratch):
    det = lax.axis_index("det")
    grp = lax.axis_index("grp")
    filt = lax.axis_index("filt")
    mesh_ids = pl.DeviceIdType.MESH

    def position(size, stride):
        if stride == 0:
            return grp
        return lax.rem(filt // stride, size)

    def peer(size, stride, target):
        if stride == 0:
            return (det, target, filt)
        here = position(size, stride)
        return (det, grp, filt + (target - here) * stride)

    live = [(size, stride) for size, stride in stages if size > 1]
    barrier = pltpu.get_barrier_semaphore()
    for size, stride in live:
        here = position(size, stride)
        for i in range(size - 1):
            target = lax.rem(here + 1 + i, size)
            pl.semaphore_signal(
                barrier, inc=1, device_id=peer(size, stride, target), device_id_type=mesh_ids
            )
    pl.semaphore_wait(barrier, sum(size - 1 for size, _ in live))
    value = local_ref[...]
    source = local_ref
    for k, (size, stride) in enumerate(live):
        held, send_sems, recv_sems = scratch[3 * k:3 * k + 3]
        here = position(size, stride)
        copies = []
        for i in range(size - 1):
            target = lax.rem(here + 1 + i, size)
            row = size - 2 - i
            copy = pltpu.make_async_remote_copy(
                src_ref=source,
                dst_ref=held.at[row],
                send_sem=send_sems.at[i],
                recv_sem=recv_sems.at[row],
                device_id=peer(size, stride, target),
                device_id_type=mesh_ids,
            )
            copy.start()
            copies.append(copy)
        for copy in copies:
            copy.wait_send()
            copy.wait_recv()
        value = jnp.maximum(value, jnp.max(held[...], axis=0))
        if k + 1 < len(live):
            acc_ref[k] = value
            source = acc_ref.at[k]
    out_ref[...] = value


def group_max(local_max):
    stages = stage_layout(lax.axis_size("grp"), lax.axis_size("filt"))
    live = [size for size, _ in stages if size > 1]
    width = local_max.shape[-1]
    scratch = [pltpu.VMEM((max(len(live), 1), 1, width), jnp.float32)]
    for size in live:
        scratch += [
            pltpu.VMEM((size - 1, 1, width), jnp.float32),
            pltpu.SemaphoreType.DMA((size - 1,)),
            pltpu.SemaphoreType.DMA((size - 1,)),
        ]
    out = pl.pallas_call(
        functools.partial(loudest_kernel, stages),
        out_shape=jax.ShapeDtypeStruct((1, width), jnp.float32),
        in_specs=[pl.BlockSpec(memory_space=pltpu.VMEM)],
        out_specs=pl.BlockSpec(memory_space=pltpu.VMEM),
        scratch_shapes=scratch,
        compiler_params=pltpu.CompilerParams(collective_id=0, has_side_effects=True),
    )(local_max.reshape(1, width))
    return out.reshape(width)


def dot_nt(left, right):
    return lax.dot_general(
        left, right, (((1,), (1,)), ((), ())), preferred_element_type=jnp.float32
    )


def filter_kernel(
    scalar_ref, x_ref, cfn_ref, sfn_ref, ct_ref, st_ref, cs_ref, ss_ref, cf_ref, sf_ref,
    cfr_ref, sfr_ref, sown_ref, soth_ref, wown_ref, woth_ref, out_ref,
    er_ref, ei_ref, pr_ref, pi_ref, w2_ref,
):
    f32 = jnp.float32
    bf16 = jnp.bfloat16

    def first_stage(cos_rows, sin_rows, x):
        cos_twist = ct_ref[...]
        sin_twist = st_ref[...]
        real_a = jnp.dot(cos_rows, x, preferred_element_type=f32)
        imag_a = -jnp.dot(sin_rows, x, preferred_element_type=f32)
        real_b = (real_a * cos_twist + imag_a * sin_twist).astype(bf16)
        imag_b = (imag_a * cos_twist - real_a * sin_twist).astype(bf16)
        cos_second = cs_ref[...]
        sin_second = ss_ref[...]
        real_x = jnp.dot(real_b, cos_second, preferred_element_type=f32) + jnp.dot(
            imag_b, sin_second, preferred_element_type=f32
        )
        imag_x = jnp.dot(imag_b, cos_second, preferred_element_type=f32) - jnp.dot(
            real_b, sin_second, preferred_element_type=f32
        )
        return real_x, imag_x

    @pl.when(pl.program_id(0) == 0)
    def _():
        det = scalar_ref[1]
        for slot, sig_ref, w_ref in ((det, sown_ref, wown_ref), (1 - det, soth_ref, woth_ref)):
            real_s, imag_s = first_stage(cf_ref[...], sf_ref[...], sig_ref[...])
            weight = jnp.transpose(w_ref[...])
            pr_ref[slot] = weight * real_s
            pi_ref[slot] = weight * imag_s
            w2_ref[slot] = weight * weight

    temp_real, temp_imag = first_stage(cfn_ref[...], sfn_ref[...], x_ref[0])
    power = temp_real * temp_real + temp_imag * temp_imag
    cos_back = cs_ref[...]
    sin_back = ss_ref[...]

    def back_half(d):
        cos_twist = ct_ref[...]
        sin_twist = st_ref[...]
        sigma = jnp.sum(w2_ref[d] * power, axis=(0, 1), keepdims=True)
        data_real = pr_ref[d]
        data_imag = pi_ref[d]
        q_real = (temp_real * data_real + temp_imag * data_imag).astype(bf16)
        q_imag = (temp_real * data_imag - temp_imag * data_real).astype(bf16)
        d_real = dot_nt(q_real, cos_back) - dot_nt(q_imag, sin_back)
        d_imag = dot_nt(q_real, sin_back) + dot_nt(q_imag, cos_back)
        e_real = (d_real * cos_twist - d_imag * sin_twist).astype(bf16)
        e_imag = (d_real * sin_twist + d_imag * cos_twist).astype(bf16)
        return sigma, e_real, e_imag

    sigma0, e_real, e_imag = back_half(0)
    cos_first = cf_ref[...]
    sin_first = sf_ref[...]
    z_real = jnp.dot(cos_first, e_real, preferred_element_type=f32) - jnp.dot(
        sin_first, e_imag, preferred_element_type=f32
    )
    z_imag = jnp.dot(sin_first, e_real, preferred_element_type=f32) + jnp.dot(
        cos_first, e_imag, preferred_element_type=f32
    )
    first = (z_real * z_real + z_imag * z_imag) / (NFFT * sigma0)
    sigma1, e_real, e_imag = back_half(1)
    er_ref[...] = e_real
    ei_ref[...] = e_imag
    rem = scalar_ref[0]
    tiles = first.shape[1] // BLK
    for col in range(tiles):
        src = lax.rem(col + rem, tiles)
        carry = (col + rem) // tiles
        cols = pl.ds(pl.multiple_of(src * BLK, BLK), BLK)
        e_r = er_ref[:, cols]
        e_i = ei_ref[:, cols]
        cos_rows = cfr_ref[carry]
        sin_rows = sfr_ref[carry]
        z_real = jnp.dot(cos_rows, e_r, preferred_element_type=f32) - jnp.dot(
            sin_rows, e_i, preferred_element_type=f32
        )
        z_imag = jnp.dot(sin_rows, e_r, preferred_element_type=f32) + jnp.dot(
            cos_rows, e_i, preferred_element_type=f32
        )
        second = (z_real * z_real + z_imag * z_imag) / (NFFT * sigma1)
        network = first[:, col * BLK:(col + 1) * BLK] + second
        out_ref[0, :, col:col + 1] = jnp.max(network, axis=1, keepdims=True)


def filter_bank(windowed, tables, signals, weights, shift, det):
    cos_first, sin_first, cos_twist, sin_twist, cos_second, sin_second = tables
    count, rows_used, width = windowed.shape
    pad_rows = 128
    x = jnp.concatenate(
        [windowed, jnp.zeros((count, pad_rows - rows_used, width), windowed.dtype)], axis=1
    )
    tiles = N2 // BLK
    quot = shift // tiles
    scalars = jnp.stack([lax.rem(shift, tiles), det]).astype(jnp.int32)
    doubled_cos = jnp.concatenate([cos_first, cos_first], axis=0)
    doubled_sin = jnp.concatenate([sin_first, sin_first], axis=0)
    cos_rolled = jnp.stack(
        [lax.dynamic_slice_in_dim(doubled_cos, quot + v, N1) for v in range(2)]
    )
    sin_rolled = jnp.stack(
        [lax.dynamic_slice_in_dim(doubled_sin, quot + v, N1) for v in range(2)]
    )
    operands = [
        cos_first[:, :pad_rows], sin_first[:, :pad_rows], cos_twist, sin_twist,
        cos_second, sin_second, cos_first, sin_first, cos_rolled, sin_rolled,
        signals[0], signals[1], weights[0], weights[1],
    ]

    def whole(array):
        nd = array.ndim
        return pl.BlockSpec(array.shape, lambda i, r, nd=nd: (0,) * nd)

    grid_spec = pltpu.PrefetchScalarGridSpec(
        num_scalar_prefetch=1,
        grid=(count,),
        in_specs=[pl.BlockSpec((1, pad_rows, width), lambda i, r: (i, 0, 0))]
        + [whole(a) for a in operands],
        out_specs=pl.BlockSpec((1, N1, tiles), lambda i, r: (i, 0, 0)),
        scratch_shapes=[
            pltpu.VMEM((N1, N2), jnp.bfloat16),
            pltpu.VMEM((N1, N2), jnp.bfloat16),
            pltpu.VMEM((2, N1, N2 // 2), jnp.float32),
            pltpu.VMEM((2, N1, N2 // 2), jnp.float32),
            pltpu.VMEM((2, N1, N2 // 2), jnp.float32),
        ],
    )
    matmuls = 2 * N1 * pad_rows * N2 + 4 * N1 * N2 * (N2 // 2) + 16 * N1 * (N2 // 2) * N2
    out = pl.pallas_call(
        filter_kernel,
        out_shape=jax.ShapeDtypeStruct((count, N1, tiles), jnp.float32),
        grid_spec=grid_spec,
        compiler_params=pltpu.CompilerParams(vmem_limit_bytes=48 * 1024 * 1024),
        cost_estimate=pl.CostEstimate(
            flops=2 * matmuls * count, transcendentals=0, bytes_accessed=8 * 1024 * 1024
        ),
    )(scalars, x, *operands)
    return out.reshape(count, N1 * tiles)


def shards(strain, inv_asd, templates, chirp_blocks, owner, slide):
    tables = make_tables()
    detector = lax.axis_index("det")
    per_dev = templates.shape[0]
    mine = per_dev // 2
    n_blk = NFFT // BLK
    half_blk = n_blk // 2
    filt_count = lax.axis_size("filt")
    capacity = (per_dev + filt_count - 1) // filt_count
    positions = jnp.arange(per_dev, dtype=jnp.int32)
    same_owner = owner[:, None] == owner[None, :]
    earlier = positions[None, :] < positions[:, None]
    owner_rank = jnp.sum(jnp.logical_and(same_owner, earlier).astype(jnp.int32), axis=1)
    dest_slot = owner * capacity + owner_rank
    slot_ids = jnp.arange(filt_count * capacity, dtype=jnp.int32)[:, None]
    placing = slot_ids == dest_slot[None, :]
    samples = jnp.arange(TL, dtype=jnp.int32)
    windowed = jnp.where(
        samples[None, :] < BLK * chirp_blocks[:, None], templates, jnp.zeros_like(templates)
    )
    payload = jnp.concatenate([windowed, jnp.ones((per_dev, 128), jnp.bfloat16)], axis=1)
    send_rows = jnp.dot(
        placing.astype(jnp.bfloat16), payload, preferred_element_type=jnp.float32
    ).astype(jnp.bfloat16)
    recv_rows = lax.all_to_all(send_rows, "filt", split_axis=0, concat_axis=0, tiled=True)
    valid = recv_rows[:, TL] > 0.5
    wanted = detector * mine + jnp.arange(mine, dtype=jnp.int32)
    my_rows = compact(recv_rows[:, :TL], valid, wanted)
    windowed = my_rows.reshape(mine, TL // N2, N2)
    swap = [(0, 1), (1, 0)]
    own_signal = strain[0].astype(jnp.bfloat16).reshape(N1, N2)
    own_weight = inv_asd[0].reshape(N2 // 2, N1)
    other_signal = lax.ppermute(own_signal, "det", swap)
    other_weight = lax.ppermute(own_weight, "det", swap)
    full = filter_bank(
        windowed, tables, (own_signal, other_signal), (own_weight, other_weight),
        slide[0], detector,
    )
    keep = lax.dynamic_slice_in_dim(full, detector * half_blk, half_blk, axis=1)
    give = lax.dynamic_slice_in_dim(full, (1 - detector) * half_blk, half_blk, axis=1)
    got = lax.ppermute(give, "det", swap)
    peaks = jnp.where(
        detector == 0, jnp.concatenate([keep, got], axis=0), jnp.concatenate([got, keep], axis=0)
    )
    local_max = jnp.max(peaks, axis=0)
    loudest = group_max(local_max)
    return (peaks, loudest)


def solution(mesh):
    return jax.shard_map(
        shards,
        mesh=mesh,
        in_specs=(
            P("det", None),
            P("det", None),
            P(("grp", "filt"), None),
            P(("grp", "filt")),
            P(("grp", "filt")),
            P("grp"),
        ),
        out_specs=(P(("grp", "filt"), "det"), P("det")),
        check_vma=False,
    )
```

```python
import functools

import jax
import ml_dtypes
import numpy as np
import jax.numpy as jnp
from jax import lax
from jax.experimental import pallas as pl
from jax.experimental.pallas import tpu as pltpu
from jax.sharding import PartitionSpec as P

N1 = 256
N2 = 512
NFFT = 131072
BLK = 128
TL = 4096


TWO_PI = 6.283185307179586


def partner_2(value, axis, stride):
    mask = 2**stride
    pairs = [(source, source ^ mask) for source in range(lax.axis_size(axis))]
    return lax.ppermute(value, axis, pairs)


def angle_table(rows, cols, period):
    left = np.arange(rows, dtype=np.int64)[:, None]
    right = np.arange(cols, dtype=np.int64)[None, :]
    turns = (left * right % period).astype(np.float32)
    return np.float32(TWO_PI / period) * turns


def make_tables():
    twist = angle_table(N1, N2, NFFT).astype(np.float64)
    second = angle_table(N2, N2 // 2, N2).astype(np.float64)
    cos_second = np.cos(second).astype(np.float32).astype(ml_dtypes.bfloat16)
    sin_second = np.sin(second).astype(np.float32).astype(ml_dtypes.bfloat16)
    return tuple(
        jnp.asarray(table)
        for table in (
            cos_second[0::2],
            sin_second[0::2],
            np.cos(twist).astype(np.float32),
            np.sin(twist).astype(np.float32),
            cos_second,
            sin_second,
        )
    )


def compact(rows, valid, wanted):
    slot_rank = jnp.cumsum(valid.astype(jnp.int32)) - 1
    picker = jnp.logical_and(valid[None, :], slot_rank[None, :] == wanted[:, None])
    return jnp.dot(picker.astype(jnp.bfloat16), rows, preferred_element_type=jnp.float32).astype(
        jnp.bfloat16
    )


def stage_layout(n_grp, n_filt):
    inner = 8 if n_filt % 8 == 0 else n_filt
    return ((inner, 1), (n_filt // inner, inner), (n_grp, 0))


def loudest_kernel(stages, local_ref, out_ref, acc_ref, *scratch):
    det = lax.axis_index("det")
    grp = lax.axis_index("grp")
    filt = lax.axis_index("filt")
    mesh_ids = pl.DeviceIdType.MESH

    def position(size, stride):
        if stride == 0:
            return grp
        return lax.rem(filt // stride, size)

    def peer(size, stride, target):
        if stride == 0:
            return (det, target, filt)
        here = position(size, stride)
        return (det, grp, filt + (target - here) * stride)

    live = [(size, stride) for size, stride in stages if size > 1]
    barrier = pltpu.get_barrier_semaphore()
    for size, stride in live:
        here = position(size, stride)
        for i in range(size - 1):
            target = lax.rem(here + 1 + i, size)
            pl.semaphore_signal(
                barrier, inc=1, device_id=peer(size, stride, target), device_id_type=mesh_ids
            )
    pl.semaphore_wait(barrier, sum(size - 1 for size, _ in live))
    value = local_ref[...]
    source = local_ref
    for k, (size, stride) in enumerate(live):
        held, send_sems, recv_sems = scratch[3 * k:3 * k + 3]
        here = position(size, stride)
        copies = []
        for i in range(size - 1):
            target = lax.rem(here + 1 + i, size)
            row = size - 2 - i
            copy = pltpu.make_async_remote_copy(
                src_ref=source,
                dst_ref=held.at[row],
                send_sem=send_sems.at[i],
                recv_sem=recv_sems.at[row],
                device_id=peer(size, stride, target),
                device_id_type=mesh_ids,
            )
            copy.start()
            copies.append(copy)
        for copy in copies:
            copy.wait_send()
            copy.wait_recv()
        value = jnp.maximum(value, jnp.max(held[...], axis=0))
        if k + 1 < len(live):
            acc_ref[k] = value
            source = acc_ref.at[k]
    out_ref[...] = value


def group_max(local_max):
    stages = stage_layout(lax.axis_size("grp"), lax.axis_size("filt"))
    live = [size for size, _ in stages if size > 1]
    width = local_max.shape[-1]
    scratch = [pltpu.VMEM((max(len(live), 1), 1, width), jnp.float32)]
    for size in live:
        scratch += [
            pltpu.VMEM((size - 1, 1, width), jnp.float32),
            pltpu.SemaphoreType.DMA((size - 1,)),
            pltpu.SemaphoreType.DMA((size - 1,)),
        ]
    out = pl.pallas_call(
        functools.partial(loudest_kernel, stages),
        out_shape=jax.ShapeDtypeStruct((1, width), jnp.float32),
        in_specs=[pl.BlockSpec(memory_space=pltpu.VMEM)],
        out_specs=pl.BlockSpec(memory_space=pltpu.VMEM),
        scratch_shapes=scratch,
        compiler_params=pltpu.CompilerParams(collective_id=0, has_side_effects=True),
    )(local_max.reshape(1, width))
    return out.reshape(width)


def exchange_kernel(
    n_filt, send_ref, sig_ref, w_ref, recv_out, sig_out, w_out,
    recv_buf, sig_buf, w_buf, send_sems, recv_sems, pair_sems,
):
    det = lax.axis_index("det")
    grp = lax.axis_index("grp")
    me = lax.axis_index("filt")
    mesh_ids = pl.DeviceIdType.MESH
    partner = (1 - det, grp, me)
    barrier = pltpu.get_barrier_semaphore()
    for i in range(n_filt - 1):
        target = lax.rem(me + 1 + i, n_filt)
        pl.semaphore_signal(barrier, inc=1, device_id=(det, grp, target), device_id_type=mesh_ids)
    pl.semaphore_signal(barrier, inc=1, device_id=partner, device_id_type=mesh_ids)
    pl.semaphore_wait(barrier, n_filt)
    sends = []
    for i in range(n_filt - 1):
        target = lax.rem(me + 1 + i, n_filt)
        copy = pltpu.make_async_remote_copy(
            src_ref=send_ref.at[target],
            dst_ref=recv_buf.at[me],
            send_sem=send_sems.at[i],
            recv_sem=recv_sems.at[me],
            device_id=(det, grp, target),
            device_id_type=mesh_ids,
        )
        copy.start()
        sends.append(copy)
    pair = []
    for k, (src, dst) in enumerate(((sig_ref, sig_buf), (w_ref, w_buf))):
        copy = pltpu.make_async_remote_copy(
            src_ref=src,
            dst_ref=dst,
            send_sem=pair_sems.at[2 * k],
            recv_sem=pair_sems.at[2 * k + 1],
            device_id=partner,
            device_id_type=mesh_ids,
        )
        copy.start()
        pair.append(copy)
    for copy in sends:
        copy.wait_send()
    for i in range(n_filt - 1):
        source = lax.rem(me + 1 + i, n_filt)
        pltpu.make_async_remote_copy(
            src_ref=send_ref.at[source],
            dst_ref=recv_buf.at[source],
            send_sem=send_sems.at[i],
            recv_sem=recv_sems.at[source],
            device_id=(det, grp, source),
            device_id_type=mesh_ids,
        ).wait_recv()
    for copy in pair:
        copy.wait_send()
        copy.wait_recv()
    recv_buf[me] = send_ref[me]
    recv_out[...] = recv_buf[...]
    sig_out[...] = sig_buf[...]
    w_out[...] = w_buf[...]


def exchange(send_rows, signal, weight):
    n_filt = send_rows.shape[0]
    vmem = pl.BlockSpec(memory_space=pltpu.VMEM)
    return pl.pallas_call(
        functools.partial(exchange_kernel, n_filt),
        out_shape=(
            jax.ShapeDtypeStruct(send_rows.shape, send_rows.dtype),
            jax.ShapeDtypeStruct(signal.shape, signal.dtype),
            jax.ShapeDtypeStruct(weight.shape, weight.dtype),
        ),
        in_specs=[vmem, vmem, vmem],
        out_specs=(vmem, vmem, vmem),
        scratch_shapes=[
            pltpu.VMEM(send_rows.shape, send_rows.dtype),
            pltpu.VMEM(signal.shape, signal.dtype),
            pltpu.VMEM(weight.shape, weight.dtype),
            pltpu.SemaphoreType.DMA((n_filt,)),
            pltpu.SemaphoreType.DMA((n_filt,)),
            pltpu.SemaphoreType.DMA((4,)),
        ],
        compiler_params=pltpu.CompilerParams(collective_id=1, has_side_effects=True),
    )(send_rows, signal, weight)


def dot_nt(left, right):
    return lax.dot_general(
        left, right, (((1,), (1,)), ((), ())), preferred_element_type=jnp.float32
    )


def filter_kernel(
    scalar_ref, x_ref, cfn_ref, sfn_ref, ct_ref, st_ref, cs_ref, ss_ref, cf_ref, sf_ref,
    cfr_ref, sfr_ref, sown_ref, soth_ref, wown_ref, woth_ref, out_ref,
    er_ref, ei_ref, pr_ref, pi_ref, w2_ref,
):
    f32 = jnp.float32
    bf16 = jnp.bfloat16

    def first_stage(cos_rows, sin_rows, x):
        cos_twist = ct_ref[...]
        sin_twist = st_ref[...]
        real_a = jnp.dot(cos_rows, x, preferred_element_type=f32)
        imag_a = -jnp.dot(sin_rows, x, preferred_element_type=f32)
        real_b = (real_a * cos_twist + imag_a * sin_twist).astype(bf16)
        imag_b = (imag_a * cos_twist - real_a * sin_twist).astype(bf16)
        cos_second = cs_ref[...]
        sin_second = ss_ref[...]
        real_x = jnp.dot(real_b, cos_second, preferred_element_type=f32) + jnp.dot(
            imag_b, sin_second, preferred_element_type=f32
        )
        imag_x = jnp.dot(imag_b, cos_second, preferred_element_type=f32) - jnp.dot(
            real_b, sin_second, preferred_element_type=f32
        )
        return real_x, imag_x

    @pl.when(pl.program_id(0) == 0)
    def _():
        det = scalar_ref[1]
        for slot, sig_ref, w_ref in ((det, sown_ref, wown_ref), (1 - det, soth_ref, woth_ref)):
            real_s, imag_s = first_stage(cf_ref[...], sf_ref[...], sig_ref[...])
            weight = jnp.transpose(w_ref[...])
            pr_ref[slot] = weight * real_s
            pi_ref[slot] = weight * imag_s
            w2_ref[slot] = weight * weight

    temp_real, temp_imag = first_stage(cfn_ref[...], sfn_ref[...], x_ref[0])
    power = temp_real * temp_real + temp_imag * temp_imag
    cos_back = cs_ref[...]
    sin_back = ss_ref[...]

    def back_half(d):
        cos_twist = ct_ref[...]
        sin_twist = st_ref[...]
        sigma = jnp.sum(w2_ref[d] * power, axis=(0, 1), keepdims=True)
        data_real = pr_ref[d]
        data_imag = pi_ref[d]
        q_real = (temp_real * data_real + temp_imag * data_imag).astype(bf16)
        q_imag = (temp_real * data_imag - temp_imag * data_real).astype(bf16)
        d_real = dot_nt(q_real, cos_back) - dot_nt(q_imag, sin_back)
        d_imag = dot_nt(q_real, sin_back) + dot_nt(q_imag, cos_back)
        e_real = (d_real * cos_twist - d_imag * sin_twist).astype(bf16)
        e_imag = (d_real * sin_twist + d_imag * cos_twist).astype(bf16)
        return sigma, e_real, e_imag

    sigma0, e_real, e_imag = back_half(0)
    cos_first = cf_ref[...]
    sin_first = sf_ref[...]
    z_real = jnp.dot(cos_first, e_real, preferred_element_type=f32) - jnp.dot(
        sin_first, e_imag, preferred_element_type=f32
    )
    z_imag = jnp.dot(sin_first, e_real, preferred_element_type=f32) + jnp.dot(
        cos_first, e_imag, preferred_element_type=f32
    )
    first = (z_real * z_real + z_imag * z_imag) / (NFFT * sigma0)
    sigma1, e_real, e_imag = back_half(1)
    er_ref[...] = e_real
    ei_ref[...] = e_imag
    rem = scalar_ref[0]
    tiles = first.shape[1] // BLK
    for col in range(tiles):
        src = lax.rem(col + rem, tiles)
        carry = (col + rem) // tiles
        cols = pl.ds(pl.multiple_of(src * BLK, BLK), BLK)
        e_r = er_ref[:, cols]
        e_i = ei_ref[:, cols]
        cos_rows = cfr_ref[carry]
        sin_rows = sfr_ref[carry]
        z_real = jnp.dot(cos_rows, e_r, preferred_element_type=f32) - jnp.dot(
            sin_rows, e_i, preferred_element_type=f32
        )
        z_imag = jnp.dot(sin_rows, e_r, preferred_element_type=f32) + jnp.dot(
            cos_rows, e_i, preferred_element_type=f32
        )
        second = (z_real * z_real + z_imag * z_imag) / (NFFT * sigma1)
        network = first[:, col * BLK:(col + 1) * BLK] + second
        out_ref[0, :, col:col + 1] = jnp.max(network, axis=1, keepdims=True)


def filter_bank(windowed, tables, signals, weights, shift, det):
    cos_first, sin_first, cos_twist, sin_twist, cos_second, sin_second = tables
    count, rows_used, width = windowed.shape
    pad_rows = 128
    x = jnp.concatenate(
        [windowed, jnp.zeros((count, pad_rows - rows_used, width), windowed.dtype)], axis=1
    )
    tiles = N2 // BLK
    quot = shift // tiles
    scalars = jnp.stack([lax.rem(shift, tiles), det]).astype(jnp.int32)
    doubled_cos = jnp.concatenate([cos_first, cos_first], axis=0)
    doubled_sin = jnp.concatenate([sin_first, sin_first], axis=0)
    cos_rolled = jnp.stack(
        [lax.dynamic_slice_in_dim(doubled_cos, quot + v, N1) for v in range(2)]
    )
    sin_rolled = jnp.stack(
        [lax.dynamic_slice_in_dim(doubled_sin, quot + v, N1) for v in range(2)]
    )
    operands = [
        cos_first[:, :pad_rows], sin_first[:, :pad_rows], cos_twist, sin_twist,
        cos_second, sin_second, cos_first, sin_first, cos_rolled, sin_rolled,
        signals[0], signals[1], weights[0], weights[1],
    ]

    def whole(array):
        nd = array.ndim
        return pl.BlockSpec(array.shape, lambda i, r, nd=nd: (0,) * nd)

    grid_spec = pltpu.PrefetchScalarGridSpec(
        num_scalar_prefetch=1,
        grid=(count,),
        in_specs=[pl.BlockSpec((1, pad_rows, width), lambda i, r: (i, 0, 0))]
        + [whole(a) for a in operands],
        out_specs=pl.BlockSpec((1, N1, tiles), lambda i, r: (i, 0, 0)),
        scratch_shapes=[
            pltpu.VMEM((N1, N2), jnp.bfloat16),
            pltpu.VMEM((N1, N2), jnp.bfloat16),
            pltpu.VMEM((2, N1, N2 // 2), jnp.float32),
            pltpu.VMEM((2, N1, N2 // 2), jnp.float32),
            pltpu.VMEM((2, N1, N2 // 2), jnp.float32),
        ],
    )
    matmuls = 2 * N1 * pad_rows * N2 + 4 * N1 * N2 * (N2 // 2) + 16 * N1 * (N2 // 2) * N2
    out = pl.pallas_call(
        filter_kernel,
        out_shape=jax.ShapeDtypeStruct((count, N1, tiles), jnp.float32),
        grid_spec=grid_spec,
        compiler_params=pltpu.CompilerParams(vmem_limit_bytes=48 * 1024 * 1024),
        cost_estimate=pl.CostEstimate(
            flops=2 * matmuls * count, transcendentals=0, bytes_accessed=8 * 1024 * 1024
        ),
    )(scalars, x, *operands)
    return out.reshape(count, N1 * tiles)


def shards(strain, inv_asd, templates, chirp_blocks, owner, slide):
    tables = make_tables()
    detector = lax.axis_index("det")
    per_dev = templates.shape[0]
    mine = per_dev // 2
    n_blk = NFFT // BLK
    half_blk = n_blk // 2
    filt_count = lax.axis_size("filt")
    capacity = (per_dev + filt_count - 1) // filt_count
    positions = jnp.arange(per_dev, dtype=jnp.int32)
    same_owner = owner[:, None] == owner[None, :]
    earlier = positions[None, :] < positions[:, None]
    owner_rank = jnp.sum(jnp.logical_and(same_owner, earlier).astype(jnp.int32), axis=1)
    dest_slot = owner * capacity + owner_rank
    slot_ids = jnp.arange(filt_count * capacity, dtype=jnp.int32)[:, None]
    placing = slot_ids == dest_slot[None, :]
    samples = jnp.arange(TL, dtype=jnp.int32)
    windowed = jnp.where(
        samples[None, :] < BLK * chirp_blocks[:, None], templates, jnp.zeros_like(templates)
    )
    lanes = 128
    body_rows = TL // lanes
    slot_rows = 48
    payload = jnp.concatenate(
        [
            windowed.reshape(per_dev, body_rows, lanes),
            jnp.ones((per_dev, 1, lanes), jnp.bfloat16),
            jnp.zeros((per_dev, slot_rows - body_rows - 1, lanes), jnp.bfloat16),
        ],
        axis=1,
    )
    send_rows = jnp.einsum(
        "js,srl->jrl", placing.astype(jnp.bfloat16), payload, preferred_element_type=jnp.float32
    ).astype(jnp.bfloat16)
    own_signal = strain[0].astype(jnp.bfloat16).reshape(N1, N2)
    own_weight = inv_asd[0].reshape(N2 // 2, N1)
    recv_rows, other_signal, other_weight = exchange(send_rows, own_signal, own_weight)
    valid = recv_rows[:, body_rows, 0] > 0.5
    wanted = detector * mine + jnp.arange(mine, dtype=jnp.int32)
    my_rows = compact(recv_rows[:, :body_rows, :].reshape(filt_count * capacity, TL), valid, wanted)
    windowed = my_rows.reshape(mine, TL // N2, N2)
    swap = [(0, 1), (1, 0)]
    full = filter_bank(
        windowed, tables, (own_signal, other_signal), (own_weight, other_weight),
        slide[0], detector,
    )
    keep = lax.dynamic_slice_in_dim(full, detector * half_blk, half_blk, axis=1)
    give = lax.dynamic_slice_in_dim(full, (1 - detector) * half_blk, half_blk, axis=1)
    got = lax.ppermute(give, "det", swap)
    peaks = jnp.where(
        detector == 0, jnp.concatenate([keep, got], axis=0), jnp.concatenate([got, keep], axis=0)
    )
    local_max = jnp.max(peaks, axis=0)
    loudest = group_max(local_max)
    return (peaks, loudest)


def solution(mesh):
    return jax.shard_map(
        shards,
        mesh=mesh,
        in_specs=(
            P("det", None),
            P("det", None),
            P(("grp", "filt"), None),
            P(("grp", "filt")),
            P(("grp", "filt")),
            P("grp"),
        ),
        out_specs=(P(("grp", "filt"), "det"), P("det")),
        check_vma=False,
    )
```

```python
import functools

import jax
import ml_dtypes
import numpy as np
import jax.numpy as jnp
from jax import lax
from jax.experimental import pallas as pl
from jax.experimental.pallas import tpu as pltpu
from jax.sharding import PartitionSpec as P

N1 = 256
N2 = 512
NFFT = 131072
BLK = 128
TL = 4096


TWO_PI = 6.283185307179586


def partner_2(value, axis, stride):
    mask = 2**stride
    pairs = [(source, source ^ mask) for source in range(lax.axis_size(axis))]
    return lax.ppermute(value, axis, pairs)


def angle_table(rows, cols, period):
    left = np.arange(rows, dtype=np.int64)[:, None]
    right = np.arange(cols, dtype=np.int64)[None, :]
    turns = (left * right % period).astype(np.float32)
    return np.float32(TWO_PI / period) * turns


def make_tables():
    twist = angle_table(N1, N2, NFFT).astype(np.float64)
    second = angle_table(N2, N2 // 2, N2).astype(np.float64)
    cos_second = np.cos(second).astype(np.float32).astype(ml_dtypes.bfloat16)
    sin_second = np.sin(second).astype(np.float32).astype(ml_dtypes.bfloat16)
    return tuple(
        jnp.asarray(table)
        for table in (
            cos_second[0::2],
            sin_second[0::2],
            np.cos(twist).astype(np.float32),
            np.sin(twist).astype(np.float32),
            cos_second,
            sin_second,
        )
    )


def compact(rows, valid, wanted):
    slot_rank = jnp.cumsum(valid.astype(jnp.int32)) - 1
    picker = jnp.logical_and(valid[None, :], slot_rank[None, :] == wanted[:, None])
    return jnp.dot(picker.astype(jnp.bfloat16), rows, preferred_element_type=jnp.float32).astype(
        jnp.bfloat16
    )


def stage_layout(n_grp, n_filt):
    inner = 8 if n_filt % 8 == 0 else n_filt
    return ((inner, 1), (n_filt // inner, inner), (n_grp, 0))


def loudest_kernel(stages, local_ref, out_ref, acc_ref, *scratch):
    det = lax.axis_index("det")
    grp = lax.axis_index("grp")
    filt = lax.axis_index("filt")
    mesh_ids = pl.DeviceIdType.MESH

    def position(size, stride):
        if stride == 0:
            return grp
        return lax.rem(filt // stride, size)

    def peer(size, stride, target):
        if stride == 0:
            return (det, target, filt)
        here = position(size, stride)
        return (det, grp, filt + (target - here) * stride)

    live = [(size, stride) for size, stride in stages if size > 1]
    barrier = pltpu.get_barrier_semaphore()
    for size, stride in live:
        here = position(size, stride)
        for i in range(size - 1):
            target = lax.rem(here + 1 + i, size)
            pl.semaphore_signal(
                barrier, inc=1, device_id=peer(size, stride, target), device_id_type=mesh_ids
            )
    pl.semaphore_wait(barrier, sum(size - 1 for size, _ in live))
    value = local_ref[...]
    source = local_ref
    for k, (size, stride) in enumerate(live):
        held, send_sems, recv_sems = scratch[3 * k:3 * k + 3]
        here = position(size, stride)
        copies = []
        for i in range(size - 1):
            target = lax.rem(here + 1 + i, size)
            row = size - 2 - i
            copy = pltpu.make_async_remote_copy(
                src_ref=source,
                dst_ref=held.at[row],
                send_sem=send_sems.at[i],
                recv_sem=recv_sems.at[row],
                device_id=peer(size, stride, target),
                device_id_type=mesh_ids,
            )
            copy.start()
            copies.append(copy)
        for copy in copies:
            copy.wait_send()
            copy.wait_recv()
        value = jnp.maximum(value, jnp.max(held[...], axis=0))
        if k + 1 < len(live):
            acc_ref[k] = value
            source = acc_ref.at[k]
    out_ref[...] = value


def group_max(local_max):
    stages = stage_layout(lax.axis_size("grp"), lax.axis_size("filt"))
    live = [size for size, _ in stages if size > 1]
    width = local_max.shape[-1]
    scratch = [pltpu.VMEM((max(len(live), 1), 1, width), jnp.float32)]
    for size in live:
        scratch += [
            pltpu.VMEM((size - 1, 1, width), jnp.float32),
            pltpu.SemaphoreType.DMA((size - 1,)),
            pltpu.SemaphoreType.DMA((size - 1,)),
        ]
    out = pl.pallas_call(
        functools.partial(loudest_kernel, stages),
        out_shape=jax.ShapeDtypeStruct((1, width), jnp.float32),
        in_specs=[pl.BlockSpec(memory_space=pltpu.VMEM)],
        out_specs=pl.BlockSpec(memory_space=pltpu.VMEM),
        scratch_shapes=scratch,
        compiler_params=pltpu.CompilerParams(collective_id=0, has_side_effects=True),
    )(local_max.reshape(1, width))
    return out.reshape(width)


def dot_nt(left, right):
    return lax.dot_general(
        left, right, (((1,), (1,)), ((), ())), preferred_element_type=jnp.float32
    )


def first_transform(ct_ref, st_ref, cs_ref, ss_ref, cos_rows, sin_rows, x):
    f32 = jnp.float32
    bf16 = jnp.bfloat16
    cos_twist = ct_ref[...]
    sin_twist = st_ref[...]
    real_a = jnp.dot(cos_rows, x, preferred_element_type=f32)
    imag_a = -jnp.dot(sin_rows, x, preferred_element_type=f32)
    real_b = (real_a * cos_twist + imag_a * sin_twist).astype(bf16)
    imag_b = (imag_a * cos_twist - real_a * sin_twist).astype(bf16)
    cos_second = cs_ref[...]
    sin_second = ss_ref[...]
    real_x = jnp.dot(real_b, cos_second, preferred_element_type=f32) + jnp.dot(
        imag_b, sin_second, preferred_element_type=f32
    )
    imag_x = jnp.dot(imag_b, cos_second, preferred_element_type=f32) - jnp.dot(
        real_b, sin_second, preferred_element_type=f32
    )
    return real_x, imag_x


def spectrum_kernel(
    det_ref, ct_ref, st_ref, cs_ref, ss_ref, cf_ref, sf_ref,
    sown_ref, soth_ref, wown_ref, woth_ref, pr_ref, pi_ref, w2_ref,
):
    det = det_ref[0]
    for slot, sig_ref, w_ref in ((det, sown_ref, wown_ref), (1 - det, soth_ref, woth_ref)):
        real_s, imag_s = first_transform(
            ct_ref, st_ref, cs_ref, ss_ref, cf_ref[...], sf_ref[...], sig_ref[...]
        )
        weight = jnp.transpose(w_ref[...])
        pr_ref[slot] = weight * real_s
        pi_ref[slot] = weight * imag_s
        w2_ref[slot] = weight * weight


def spectra(tables, signals, weights, det):
    cos_first, sin_first, cos_twist, sin_twist, cos_second, sin_second = tables
    vmem = pl.BlockSpec(memory_space=pltpu.VMEM)
    smem = pl.BlockSpec(memory_space=pltpu.SMEM)
    part = jax.ShapeDtypeStruct((2, N1, N2 // 2), jnp.float32)
    flops = 2 * 2 * (2 * N1 * N1 * N2 + 4 * N1 * N2 * (N2 // 2))
    return pl.pallas_call(
        spectrum_kernel,
        out_shape=(part, part, part),
        in_specs=[smem] + [vmem] * 10,
        out_specs=(vmem, vmem, vmem),
        cost_estimate=pl.CostEstimate(
            flops=flops, transcendentals=0, bytes_accessed=4 * 1024 * 1024
        ),
    )(
        det.reshape(1).astype(jnp.int32), cos_twist, sin_twist, cos_second, sin_second,
        cos_first, sin_first, signals[0], signals[1], weights[0], weights[1],
    )


def filter_kernel(
    scalar_ref, x_ref, cfn_ref, sfn_ref, ct_ref, st_ref, cs_ref, ss_ref, cf_ref, sf_ref,
    cfr_ref, sfr_ref, pr_ref, pi_ref, w2_ref, out_ref, er_ref, ei_ref,
):
    f32 = jnp.float32
    bf16 = jnp.bfloat16

    f32 = jnp.float32
    bf16 = jnp.bfloat16
    temp_real, temp_imag = first_transform(
        ct_ref, st_ref, cs_ref, ss_ref, cfn_ref[...], sfn_ref[...], x_ref[0]
    )
    power = temp_real * temp_real + temp_imag * temp_imag
    cos_back = cs_ref[...]
    sin_back = ss_ref[...]

    def back_half(d):
        cos_twist = ct_ref[...]
        sin_twist = st_ref[...]
        sigma = jnp.sum(w2_ref[d] * power, axis=(0, 1), keepdims=True)
        data_real = pr_ref[d]
        data_imag = pi_ref[d]
        q_real = (temp_real * data_real + temp_imag * data_imag).astype(bf16)
        q_imag = (temp_real * data_imag - temp_imag * data_real).astype(bf16)
        d_real = dot_nt(q_real, cos_back) - dot_nt(q_imag, sin_back)
        d_imag = dot_nt(q_real, sin_back) + dot_nt(q_imag, cos_back)
        e_real = (d_real * cos_twist - d_imag * sin_twist).astype(bf16)
        e_imag = (d_real * sin_twist + d_imag * cos_twist).astype(bf16)
        return sigma, e_real, e_imag

    sigma0, e_real, e_imag = back_half(0)
    cos_first = cf_ref[...]
    sin_first = sf_ref[...]
    z_real = jnp.dot(cos_first, e_real, preferred_element_type=f32) - jnp.dot(
        sin_first, e_imag, preferred_element_type=f32
    )
    z_imag = jnp.dot(sin_first, e_real, preferred_element_type=f32) + jnp.dot(
        cos_first, e_imag, preferred_element_type=f32
    )
    first = (z_real * z_real + z_imag * z_imag) * (1.0 / (NFFT * sigma0))
    sigma1, e_real, e_imag = back_half(1)
    scale1 = 1.0 / (NFFT * sigma1)
    er_ref[...] = e_real
    ei_ref[...] = e_imag
    rem = scalar_ref[0]
    tiles = first.shape[1] // BLK
    for col in range(tiles):
        src = lax.rem(col + rem, tiles)
        carry = (col + rem) // tiles
        cols = pl.ds(pl.multiple_of(src * BLK, BLK), BLK)
        e_r = er_ref[:, cols]
        e_i = ei_ref[:, cols]
        cos_rows = cfr_ref[carry]
        sin_rows = sfr_ref[carry]
        z_real = jnp.dot(cos_rows, e_r, preferred_element_type=f32) - jnp.dot(
            sin_rows, e_i, preferred_element_type=f32
        )
        z_imag = jnp.dot(sin_rows, e_r, preferred_element_type=f32) + jnp.dot(
            cos_rows, e_i, preferred_element_type=f32
        )
        second = (z_real * z_real + z_imag * z_imag) * scale1
        network = first[:, col * BLK:(col + 1) * BLK] + second
        out_ref[0, :, col:col + 1] = jnp.max(network, axis=1, keepdims=True)


def filter_bank(windowed, tables, spectrum, shift):
    cos_first, sin_first, cos_twist, sin_twist, cos_second, sin_second = tables
    count, rows_used, width = windowed.shape
    pad_rows = 128
    x = jnp.concatenate(
        [windowed, jnp.zeros((count, pad_rows - rows_used, width), windowed.dtype)], axis=1
    )
    tiles = N2 // BLK
    quot = shift // tiles
    scalars = lax.rem(shift, tiles).reshape(1).astype(jnp.int32)
    doubled_cos = jnp.concatenate([cos_first, cos_first], axis=0)
    doubled_sin = jnp.concatenate([sin_first, sin_first], axis=0)
    cos_rolled = jnp.stack(
        [lax.dynamic_slice_in_dim(doubled_cos, quot + v, N1) for v in range(2)]
    )
    sin_rolled = jnp.stack(
        [lax.dynamic_slice_in_dim(doubled_sin, quot + v, N1) for v in range(2)]
    )
    operands = [
        cos_first[:, :pad_rows], sin_first[:, :pad_rows], cos_twist, sin_twist,
        cos_second, sin_second, cos_first, sin_first, cos_rolled, sin_rolled,
        *spectrum,
    ]

    def whole(array):
        nd = array.ndim
        return pl.BlockSpec(array.shape, lambda i, r, nd=nd: (0,) * nd)

    grid_spec = pltpu.PrefetchScalarGridSpec(
        num_scalar_prefetch=1,
        grid=(count,),
        in_specs=[pl.BlockSpec((1, pad_rows, width), lambda i, r: (i, 0, 0))]
        + [whole(a) for a in operands],
        out_specs=pl.BlockSpec((1, N1, tiles), lambda i, r: (i, 0, 0)),
        scratch_shapes=[pltpu.VMEM((N1, N2), jnp.bfloat16), pltpu.VMEM((N1, N2), jnp.bfloat16)],
    )
    matmuls = 2 * N1 * pad_rows * N2 + 4 * N1 * N2 * (N2 // 2) + 16 * N1 * (N2 // 2) * N2
    out = pl.pallas_call(
        filter_kernel,
        out_shape=jax.ShapeDtypeStruct((count, N1, tiles), jnp.float32),
        grid_spec=grid_spec,
        compiler_params=pltpu.CompilerParams(vmem_limit_bytes=48 * 1024 * 1024),
        cost_estimate=pl.CostEstimate(
            flops=2 * matmuls * count, transcendentals=0, bytes_accessed=8 * 1024 * 1024
        ),
    )(scalars, x, *operands)
    return out.reshape(count, N1 * tiles)


def shards(strain, inv_asd, templates, chirp_blocks, owner, slide):
    tables = make_tables()
    detector = lax.axis_index("det")
    per_dev = templates.shape[0]
    mine = per_dev // 2
    n_blk = NFFT // BLK
    half_blk = n_blk // 2
    filt_count = lax.axis_size("filt")
    capacity = (per_dev + filt_count - 1) // filt_count
    positions = jnp.arange(per_dev, dtype=jnp.int32)
    same_owner = owner[:, None] == owner[None, :]
    earlier = positions[None, :] < positions[:, None]
    owner_rank = jnp.sum(jnp.logical_and(same_owner, earlier).astype(jnp.int32), axis=1)
    dest_slot = owner * capacity + owner_rank
    slot_ids = jnp.arange(filt_count * capacity, dtype=jnp.int32)[:, None]
    placing = slot_ids == dest_slot[None, :]
    samples = jnp.arange(TL, dtype=jnp.int32)
    windowed = jnp.where(
        samples[None, :] < BLK * chirp_blocks[:, None], templates, jnp.zeros_like(templates)
    )
    payload = jnp.concatenate([windowed, jnp.ones((per_dev, 128), jnp.bfloat16)], axis=1)
    send_rows = jnp.dot(
        placing.astype(jnp.bfloat16), payload, preferred_element_type=jnp.float32
    ).astype(jnp.bfloat16)
    recv_rows = lax.all_to_all(send_rows, "filt", split_axis=0, concat_axis=0, tiled=True)
    valid = recv_rows[:, TL] > 0.5
    wanted = detector * mine + jnp.arange(mine, dtype=jnp.int32)
    my_rows = compact(recv_rows[:, :TL], valid, wanted)
    windowed = my_rows.reshape(mine, TL // N2, N2)
    swap = [(0, 1), (1, 0)]
    own_signal = strain[0].astype(jnp.bfloat16).reshape(N1, N2)
    own_weight = inv_asd[0].reshape(N2 // 2, N1)
    other_signal = lax.ppermute(own_signal, "det", swap)
    other_weight = lax.ppermute(own_weight, "det", swap)
    spectrum = spectra(tables, (own_signal, other_signal), (own_weight, other_weight), detector)
    full = filter_bank(windowed, tables, spectrum, slide[0])
    keep = lax.dynamic_slice_in_dim(full, detector * half_blk, half_blk, axis=1)
    give = lax.dynamic_slice_in_dim(full, (1 - detector) * half_blk, half_blk, axis=1)
    got = lax.ppermute(give, "det", swap)
    peaks = jnp.where(
        detector == 0, jnp.concatenate([keep, got], axis=0), jnp.concatenate([got, keep], axis=0)
    )
    local_max = jnp.max(peaks, axis=0)
    loudest = group_max(local_max)
    return (peaks, loudest)


def solution(mesh):
    return jax.shard_map(
        shards,
        mesh=mesh,
        in_specs=(
            P("det", None),
            P("det", None),
            P(("grp", "filt"), None),
            P(("grp", "filt")),
            P(("grp", "filt")),
            P("grp"),
        ),
        out_specs=(P(("grp", "filt"), "det"), P("det")),
        check_vma=False,
    )
```

```python
import functools

import jax
import ml_dtypes
import numpy as np
import jax.numpy as jnp
from jax import lax
from jax.experimental import pallas as pl
from jax.experimental.pallas import tpu as pltpu
from jax.sharding import PartitionSpec as P

N1 = 256
N2 = 512
NFFT = 131072
BLK = 128
TL = 4096


TWO_PI = 6.283185307179586


def partner_2(value, axis, stride):
    mask = 2**stride
    pairs = [(source, source ^ mask) for source in range(lax.axis_size(axis))]
    return lax.ppermute(value, axis, pairs)


def angle_table(rows, cols, period):
    left = np.arange(rows, dtype=np.int64)[:, None]
    right = np.arange(cols, dtype=np.int64)[None, :]
    turns = (left * right % period).astype(np.float32)
    return np.float32(TWO_PI / period) * turns


def make_tables():
    twist = angle_table(N1, N2, NFFT).astype(np.float64)
    second = angle_table(N2, N2 // 2, N2).astype(np.float64)
    cos_second = np.cos(second).astype(np.float32).astype(ml_dtypes.bfloat16)
    sin_second = np.sin(second).astype(np.float32).astype(ml_dtypes.bfloat16)
    return tuple(
        jnp.asarray(table)
        for table in (
            cos_second[0::2],
            sin_second[0::2],
            np.cos(twist).astype(np.float32),
            np.sin(twist).astype(np.float32),
            cos_second,
            sin_second,
        )
    )


def compact(rows, valid, wanted):
    slot_rank = jnp.cumsum(valid.astype(jnp.int32)) - 1
    picker = jnp.logical_and(valid[None, :], slot_rank[None, :] == wanted[:, None])
    return jnp.dot(picker.astype(jnp.bfloat16), rows, preferred_element_type=jnp.float32).astype(
        jnp.bfloat16
    )


def stage_layout(n_grp, n_filt):
    inner = 8 if n_filt % 8 == 0 else n_filt
    return ((inner, 1), (n_filt // inner, inner), (n_grp, 0))


def loudest_kernel(stages, local_ref, out_ref, acc_ref, *scratch):
    det = lax.axis_index("det")
    grp = lax.axis_index("grp")
    filt = lax.axis_index("filt")
    mesh_ids = pl.DeviceIdType.MESH

    def position(size, stride):
        if stride == 0:
            return grp
        return lax.rem(filt // stride, size)

    def peer(size, stride, target):
        if stride == 0:
            return (det, target, filt)
        here = position(size, stride)
        return (det, grp, filt + (target - here) * stride)

    live = [(size, stride) for size, stride in stages if size > 1]
    barrier = pltpu.get_barrier_semaphore()
    for size, stride in live:
        here = position(size, stride)
        for i in range(size - 1):
            target = lax.rem(here + 1 + i, size)
            pl.semaphore_signal(
                barrier, inc=1, device_id=peer(size, stride, target), device_id_type=mesh_ids
            )
    pl.semaphore_wait(barrier, sum(size - 1 for size, _ in live))
    value = local_ref[...]
    source = local_ref
    for k, (size, stride) in enumerate(live):
        held, send_sems, recv_sems = scratch[3 * k:3 * k + 3]
        here = position(size, stride)
        copies = []
        for i in range(size - 1):
            target = lax.rem(here + 1 + i, size)
            row = size - 2 - i
            copy = pltpu.make_async_remote_copy(
                src_ref=source,
                dst_ref=held.at[row],
                send_sem=send_sems.at[i],
                recv_sem=recv_sems.at[row],
                device_id=peer(size, stride, target),
                device_id_type=mesh_ids,
            )
            copy.start()
            copies.append(copy)
        for copy in copies:
            copy.wait_send()
            copy.wait_recv()
        value = jnp.maximum(value, jnp.max(held[...], axis=0))
        if k + 1 < len(live):
            acc_ref[k] = value
            source = acc_ref.at[k]
    out_ref[...] = value


def group_max(local_max):
    stages = stage_layout(lax.axis_size("grp"), lax.axis_size("filt"))
    live = [size for size, _ in stages if size > 1]
    width = local_max.shape[-1]
    scratch = [pltpu.VMEM((max(len(live), 1), 1, width), jnp.float32)]
    for size in live:
        scratch += [
            pltpu.VMEM((size - 1, 1, width), jnp.float32),
            pltpu.SemaphoreType.DMA((size - 1,)),
            pltpu.SemaphoreType.DMA((size - 1,)),
        ]
    out = pl.pallas_call(
        functools.partial(loudest_kernel, stages),
        out_shape=jax.ShapeDtypeStruct((1, width), jnp.float32),
        in_specs=[pl.BlockSpec(memory_space=pltpu.VMEM)],
        out_specs=pl.BlockSpec(memory_space=pltpu.VMEM),
        scratch_shapes=scratch,
        compiler_params=pltpu.CompilerParams(collective_id=0, has_side_effects=True),
    )(local_max.reshape(1, width))
    return out.reshape(width)


def dot_nt(left, right):
    return lax.dot_general(
        left, right, (((1,), (1,)), ((), ())), preferred_element_type=jnp.float32
    )


def first_transform(ct_ref, st_ref, cs_ref, ss_ref, cos_rows, sin_rows, x):
    f32 = jnp.float32
    bf16 = jnp.bfloat16
    cos_twist = ct_ref[...]
    sin_twist = st_ref[...]
    real_a = jnp.dot(cos_rows, x, preferred_element_type=f32)
    imag_a = -jnp.dot(sin_rows, x, preferred_element_type=f32)
    real_b = (real_a * cos_twist + imag_a * sin_twist).astype(bf16)
    imag_b = (imag_a * cos_twist - real_a * sin_twist).astype(bf16)
    cos_second = cs_ref[...]
    sin_second = ss_ref[...]
    real_x = jnp.dot(real_b, cos_second, preferred_element_type=f32) + jnp.dot(
        imag_b, sin_second, preferred_element_type=f32
    )
    imag_x = jnp.dot(imag_b, cos_second, preferred_element_type=f32) - jnp.dot(
        real_b, sin_second, preferred_element_type=f32
    )
    return real_x, imag_x


def spectrum_kernel(
    det_ref, ct_ref, st_ref, cs_ref, ss_ref, cf_ref, sf_ref,
    sown_ref, soth_ref, wown_ref, woth_ref, pr_ref, pi_ref, w2_ref,
):
    det = det_ref[0]
    for slot, sig_ref, w_ref in ((det, sown_ref, wown_ref), (1 - det, soth_ref, woth_ref)):
        real_s, imag_s = first_transform(
            ct_ref, st_ref, cs_ref, ss_ref, cf_ref[...], sf_ref[...], sig_ref[...]
        )
        weight = jnp.transpose(w_ref[...])
        pr_ref[slot] = weight * real_s
        pi_ref[slot] = weight * imag_s
        w2_ref[slot] = weight * weight


def spectra(tables, signals, weights, det):
    cos_first, sin_first, cos_twist, sin_twist, cos_second, sin_second = tables
    vmem = pl.BlockSpec(memory_space=pltpu.VMEM)
    smem = pl.BlockSpec(memory_space=pltpu.SMEM)
    part = jax.ShapeDtypeStruct((2, N1, N2 // 2), jnp.float32)
    flops = 2 * 2 * (2 * N1 * N1 * N2 + 4 * N1 * N2 * (N2 // 2))
    return pl.pallas_call(
        spectrum_kernel,
        out_shape=(part, part, part),
        in_specs=[smem] + [vmem] * 10,
        out_specs=(vmem, vmem, vmem),
        cost_estimate=pl.CostEstimate(
            flops=flops, transcendentals=0, bytes_accessed=4 * 1024 * 1024
        ),
    )(
        det.reshape(1).astype(jnp.int32), cos_twist, sin_twist, cos_second, sin_second,
        cos_first, sin_first, signals[0], signals[1], weights[0], weights[1],
    )


def filter_kernel(
    scalar_ref, x_ref, cfn_ref, sfn_ref, ct_ref, st_ref, cs_ref, ss_ref, cf_ref, sf_ref,
    cfr_ref, sfr_ref, pr_ref, pi_ref, w2_ref, out_ref, er_ref, ei_ref,
):
    f32 = jnp.float32
    bf16 = jnp.bfloat16

    f32 = jnp.float32
    bf16 = jnp.bfloat16
    temp_real, temp_imag = first_transform(
        ct_ref, st_ref, cs_ref, ss_ref, cfn_ref[...], sfn_ref[...], x_ref[0]
    )
    power = temp_real * temp_real + temp_imag * temp_imag
    cos_back = cs_ref[...]
    sin_back = ss_ref[...]

    def back_half(d):
        cos_twist = ct_ref[...]
        sin_twist = st_ref[...]
        sigma = jnp.sum(w2_ref[d] * power, axis=(0, 1), keepdims=True)
        data_real = pr_ref[d]
        data_imag = pi_ref[d]
        q_real = (temp_real * data_real + temp_imag * data_imag).astype(bf16)
        q_imag = (temp_real * data_imag - temp_imag * data_real).astype(bf16)
        d_real = dot_nt(q_real, cos_back) - dot_nt(q_imag, sin_back)
        d_imag = dot_nt(q_real, sin_back) + dot_nt(q_imag, cos_back)
        e_real = (d_real * cos_twist - d_imag * sin_twist).astype(bf16)
        e_imag = (d_real * sin_twist + d_imag * cos_twist).astype(bf16)
        return sigma, e_real, e_imag

    sigma0, e_real, e_imag = back_half(0)
    cos_first = cf_ref[...]
    sin_first = sf_ref[...]
    z_real = jnp.dot(cos_first, e_real, preferred_element_type=f32) - jnp.dot(
        sin_first, e_imag, preferred_element_type=f32
    )
    z_imag = jnp.dot(sin_first, e_real, preferred_element_type=f32) + jnp.dot(
        cos_first, e_imag, preferred_element_type=f32
    )
    first = (z_real * z_real + z_imag * z_imag) * (1.0 / (NFFT * sigma0))
    sigma1, e_real, e_imag = back_half(1)
    scale1 = 1.0 / (NFFT * sigma1)
    er_ref[...] = e_real
    ei_ref[...] = e_imag
    rem = scalar_ref[0]
    tiles = first.shape[1] // BLK
    for col in range(tiles):
        src = lax.rem(col + rem, tiles)
        carry = (col + rem) // tiles
        cols = pl.ds(pl.multiple_of(src * BLK, BLK), BLK)
        e_r = er_ref[:, cols]
        e_i = ei_ref[:, cols]
        cos_rows = cfr_ref[carry]
        sin_rows = sfr_ref[carry]
        z_real = jnp.dot(cos_rows, e_r, preferred_element_type=f32) - jnp.dot(
            sin_rows, e_i, preferred_element_type=f32
        )
        z_imag = jnp.dot(sin_rows, e_r, preferred_element_type=f32) + jnp.dot(
            cos_rows, e_i, preferred_element_type=f32
        )
        second = (z_real * z_real + z_imag * z_imag) * scale1
        network = first[:, col * BLK:(col + 1) * BLK] + second
        out_ref[0, :, col:col + 1] = jnp.max(network, axis=1, keepdims=True)


def filter_bank(windowed, tables, spectrum, shift):
    cos_first, sin_first, cos_twist, sin_twist, cos_second, sin_second = tables
    count, rows_used, width = windowed.shape
    pad_rows = 128
    x = jnp.concatenate(
        [windowed, jnp.zeros((count, pad_rows - rows_used, width), windowed.dtype)], axis=1
    )
    tiles = N2 // BLK
    quot = shift // tiles
    scalars = lax.rem(shift, tiles).reshape(1).astype(jnp.int32)
    doubled_cos = jnp.concatenate([cos_first, cos_first], axis=0)
    doubled_sin = jnp.concatenate([sin_first, sin_first], axis=0)
    cos_rolled = jnp.stack(
        [lax.dynamic_slice_in_dim(doubled_cos, quot + v, N1) for v in range(2)]
    )
    sin_rolled = jnp.stack(
        [lax.dynamic_slice_in_dim(doubled_sin, quot + v, N1) for v in range(2)]
    )
    operands = [
        cos_first[:, :pad_rows], sin_first[:, :pad_rows], cos_twist, sin_twist,
        cos_second, sin_second, cos_first, sin_first, cos_rolled, sin_rolled,
        *spectrum,
    ]

    def whole(array):
        nd = array.ndim
        return pl.BlockSpec(array.shape, lambda i, r, nd=nd: (0,) * nd)

    grid_spec = pltpu.PrefetchScalarGridSpec(
        num_scalar_prefetch=1,
        grid=(count,),
        in_specs=[pl.BlockSpec((1, pad_rows, width), lambda i, r: (i, 0, 0))]
        + [whole(a) for a in operands],
        out_specs=pl.BlockSpec((1, N1, tiles), lambda i, r: (i, 0, 0)),
        scratch_shapes=[pltpu.VMEM((N1, N2), jnp.bfloat16), pltpu.VMEM((N1, N2), jnp.bfloat16)],
    )
    matmuls = 2 * N1 * pad_rows * N2 + 4 * N1 * N2 * (N2 // 2) + 16 * N1 * (N2 // 2) * N2
    out = pl.pallas_call(
        filter_kernel,
        out_shape=jax.ShapeDtypeStruct((count, N1, tiles), jnp.float32),
        grid_spec=grid_spec,
        compiler_params=pltpu.CompilerParams(vmem_limit_bytes=48 * 1024 * 1024),
        cost_estimate=pl.CostEstimate(
            flops=2 * matmuls * count, transcendentals=0, bytes_accessed=8 * 1024 * 1024
        ),
    )(scalars, x, *operands)
    return out.reshape(count, N1 * tiles)


def shards(strain, inv_asd, templates, chirp_blocks, owner, slide):
    tables = make_tables()
    detector = lax.axis_index("det")
    per_dev = templates.shape[0]
    mine = per_dev // 2
    n_blk = NFFT // BLK
    half_blk = n_blk // 2
    filt_count = lax.axis_size("filt")
    swap = [(0, 1), (1, 0)]
    own_signal = strain[0].astype(jnp.bfloat16).reshape(N1, N2)
    own_weight = inv_asd[0].reshape(N2 // 2, N1)
    other_signal = lax.ppermute(own_signal, "det", swap)
    other_weight = lax.ppermute(own_weight, "det", swap)
    samples = jnp.arange(TL, dtype=jnp.int32)
    my_rows = lax.dynamic_slice_in_dim(templates, detector * mine, mine)
    my_blocks = lax.dynamic_slice_in_dim(chirp_blocks, detector * mine, mine)
    windowed = jnp.where(
        samples[None, :] < BLK * my_blocks[:, None], my_rows, jnp.zeros_like(my_rows)
    )
    windowed = windowed.reshape(mine, TL // N2, N2)
    spectrum = spectra(tables, (own_signal, other_signal), (own_weight, other_weight), detector)
    full = filter_bank(windowed, tables, spectrum, slide[0])
    keep = lax.dynamic_slice_in_dim(full, detector * half_blk, half_blk, axis=1)
    give = lax.dynamic_slice_in_dim(full, (1 - detector) * half_blk, half_blk, axis=1)
    got = lax.ppermute(give, "det", swap)
    local = jnp.where(
        detector == 0, jnp.concatenate([keep, got], axis=0), jnp.concatenate([got, keep], axis=0)
    )
    local_max = jnp.max(local, axis=0)
    loudest = group_max(local_max)
    positions = jnp.arange(per_dev, dtype=jnp.int32)
    slots = jnp.arange(filt_count, dtype=jnp.int32)
    placing = owner[None, :] == slots[:, None]
    source = jnp.sum(jnp.where(placing, positions[None, :], 0), axis=1)
    used = jnp.any(placing, axis=1)
    flagged = jnp.concatenate([local, jnp.ones((per_dev, 128), jnp.float32)], axis=1)
    send_rows = jnp.where(used[:, None], jnp.take(flagged, source, axis=0), 0.0)
    recv_rows = lax.all_to_all(send_rows, "filt", split_axis=0, concat_axis=0, tiled=True)
    valid = recv_rows[:, half_blk] > 0.5
    rank = jnp.cumsum(valid.astype(jnp.int32)) - 1
    hits = jnp.logical_and(valid[None, :], rank[None, :] == positions[:, None])
    pick = jnp.sum(jnp.where(hits, slots[None, :], 0), axis=1)
    peaks = jnp.take(recv_rows[:, :half_blk], pick, axis=0)
    return (peaks, loudest)


def solution(mesh):
    return jax.shard_map(
        shards,
        mesh=mesh,
        in_specs=(
            P("det", None),
            P("det", None),
            P(("grp", "filt"), None),
            P(("grp", "filt")),
            P(("grp", "filt")),
            P("grp"),
        ),
        out_specs=(P(("grp", "filt"), "det"), P("det")),
        check_vma=False,
    )
```

```python
import functools

import jax
import ml_dtypes
import numpy as np
import jax.numpy as jnp
from jax import lax
from jax.experimental import pallas as pl
from jax.experimental.pallas import tpu as pltpu
from jax.sharding import PartitionSpec as P

N1 = 256
N2 = 512
NFFT = 131072
BLK = 128
TL = 4096


TWO_PI = 6.283185307179586


def angle_table(rows, cols, period):
    left = np.arange(rows, dtype=np.int64)[:, None]
    right = np.arange(cols, dtype=np.int64)[None, :]
    turns = (left * right % period).astype(np.float32)
    return np.float32(TWO_PI / period) * turns


def make_tables():
    twist = angle_table(N1, N2, NFFT).astype(np.float64)
    second = angle_table(N2, N2 // 2, N2).astype(np.float64)
    cos_second = np.cos(second).astype(np.float32).astype(ml_dtypes.bfloat16)
    sin_second = np.sin(second).astype(np.float32).astype(ml_dtypes.bfloat16)
    return tuple(
        jnp.asarray(table)
        for table in (
            cos_second[0::2],
            sin_second[0::2],
            np.cos(twist).astype(np.float32),
            np.sin(twist).astype(np.float32),
            cos_second,
            sin_second,
        )
    )


def route_kernel(
    stages, send_ref, local_ref, recv_out, out_ref, recv_buf, slot_send, slot_recv, acc_ref,
    *scratch,
):
    det = lax.axis_index("det")
    grp = lax.axis_index("grp")
    filt = lax.axis_index("filt")
    n_grp = lax.axis_size("grp")
    n_filt = send_ref.shape[0]
    mesh_ids = pl.DeviceIdType.MESH

    def position(size, stride):
        if stride == 0:
            return grp
        return lax.rem(filt // stride, size)

    def peer(size, stride, target):
        if stride == 0:
            return (det, target, filt)
        here = position(size, stride)
        return (det, grp, filt + (target - here) * stride)

    barrier = pltpu.get_barrier_semaphore()
    for i in range(n_filt - 1):
        target = lax.rem(filt + 1 + i, n_filt)
        pl.semaphore_signal(barrier, inc=1, device_id=(det, grp, target), device_id_type=mesh_ids)
    for i in range(n_grp - 1):
        target = lax.rem(grp + 1 + i, n_grp)
        pl.semaphore_signal(barrier, inc=1, device_id=(det, target, filt), device_id_type=mesh_ids)
    pl.semaphore_wait(barrier, n_filt - 1 + n_grp - 1)
    slots = []
    for i in range(n_filt - 1):
        target = lax.rem(filt + 1 + i, n_filt)
        copy = pltpu.make_async_remote_copy(
            src_ref=send_ref.at[target],
            dst_ref=recv_buf.at[filt],
            send_sem=slot_send.at[i],
            recv_sem=slot_recv.at[filt],
            device_id=(det, grp, target),
            device_id_type=mesh_ids,
        )
        copy.start()
        slots.append(copy)
    live = [(size, stride) for size, stride in stages if size > 1]
    value = local_ref[...]
    source = local_ref
    for k, (size, stride) in enumerate(live):
        held, send_sems, recv_sems = scratch[3 * k:3 * k + 3]
        here = position(size, stride)
        copies = []
        for i in range(size - 1):
            target = lax.rem(here + 1 + i, size)
            row = size - 2 - i
            copy = pltpu.make_async_remote_copy(
                src_ref=source,
                dst_ref=held.at[row],
                send_sem=send_sems.at[i],
                recv_sem=recv_sems.at[row],
                device_id=peer(size, stride, target),
                device_id_type=mesh_ids,
            )
            copy.start()
            copies.append(copy)
        for copy in copies:
            copy.wait_send()
            copy.wait_recv()
        value = jnp.maximum(value, jnp.max(held[...], axis=0))
        if k + 1 < len(live):
            acc_ref[k] = value
            source = acc_ref.at[k]
    out_ref[...] = value
    for copy in slots:
        copy.wait_send()
    for i in range(n_filt - 1):
        origin = lax.rem(filt + 1 + i, n_filt)
        pltpu.make_async_remote_copy(
            src_ref=send_ref.at[origin],
            dst_ref=recv_buf.at[origin],
            send_sem=slot_send.at[i],
            recv_sem=slot_recv.at[origin],
            device_id=(det, grp, origin),
            device_id_type=mesh_ids,
        ).wait_recv()
    recv_buf[filt] = send_ref[filt]
    recv_out[...] = recv_buf[...]


def stage_layout(n_grp, n_filt):
    inner = 8 if n_filt % 8 == 0 else n_filt
    return ((inner, 1), (n_filt // inner, inner), (n_grp, 0))


def route_and_max(send_rows, local_max):
    stages = stage_layout(lax.axis_size("grp"), lax.axis_size("filt"))
    live = [size for size, _ in stages if size > 1]
    width = local_max.shape[-1]
    n_filt = send_rows.shape[0]
    scratch = [
        pltpu.VMEM(send_rows.shape, send_rows.dtype),
        pltpu.SemaphoreType.DMA((n_filt,)),
        pltpu.SemaphoreType.DMA((n_filt,)),
        pltpu.VMEM((max(len(live), 1), 1, width), jnp.float32),
    ]
    for size in live:
        scratch += [
            pltpu.VMEM((size - 1, 1, width), jnp.float32),
            pltpu.SemaphoreType.DMA((size - 1,)),
            pltpu.SemaphoreType.DMA((size - 1,)),
        ]
    vmem = pl.BlockSpec(memory_space=pltpu.VMEM)
    recv, out = pl.pallas_call(
        functools.partial(route_kernel, stages),
        out_shape=(
            jax.ShapeDtypeStruct(send_rows.shape, send_rows.dtype),
            jax.ShapeDtypeStruct((1, width), jnp.float32),
        ),
        in_specs=[vmem, vmem],
        out_specs=(vmem, vmem),
        scratch_shapes=scratch,
        compiler_params=pltpu.CompilerParams(collective_id=0, has_side_effects=True),
    )(send_rows, local_max.reshape(1, width))
    return recv, out.reshape(width)


def dot_nt(left, right):
    return lax.dot_general(
        left, right, (((1,), (1,)), ((), ())), preferred_element_type=jnp.float32
    )


def filter_kernel(
    scalar_ref, x_ref, cfn_ref, sfn_ref, ct_ref, st_ref, cs_ref, ss_ref, cf_ref, sf_ref,
    cfr_ref, sfr_ref, sown_ref, soth_ref, wown_ref, woth_ref, out_ref,
    er_ref, ei_ref, pr_ref, pi_ref, w2_ref,
):
    f32 = jnp.float32
    bf16 = jnp.bfloat16

    def first_stage(cos_rows, sin_rows, x):
        cos_twist = ct_ref[...]
        sin_twist = st_ref[...]
        real_a = jnp.dot(cos_rows, x, preferred_element_type=f32)
        imag_a = -jnp.dot(sin_rows, x, preferred_element_type=f32)
        real_b = (real_a * cos_twist + imag_a * sin_twist).astype(bf16)
        imag_b = (imag_a * cos_twist - real_a * sin_twist).astype(bf16)
        cos_second = cs_ref[...]
        sin_second = ss_ref[...]
        real_x = jnp.dot(real_b, cos_second, preferred_element_type=f32) + jnp.dot(
            imag_b, sin_second, preferred_element_type=f32
        )
        imag_x = jnp.dot(imag_b, cos_second, preferred_element_type=f32) - jnp.dot(
            real_b, sin_second, preferred_element_type=f32
        )
        return real_x, imag_x

    @pl.when(pl.program_id(0) == 0)
    def _():
        det = scalar_ref[1]
        for slot, sig_ref, w_ref in ((det, sown_ref, wown_ref), (1 - det, soth_ref, woth_ref)):
            real_s, imag_s = first_stage(cf_ref[...], sf_ref[...], sig_ref[...])
            weight = jnp.transpose(w_ref[...])
            pr_ref[slot] = weight * real_s
            pi_ref[slot] = weight * imag_s
            w2_ref[slot] = weight * weight

    temp_real, temp_imag = first_stage(cfn_ref[...], sfn_ref[...], x_ref[0])
    power = temp_real * temp_real + temp_imag * temp_imag
    cos_back = cs_ref[...]
    sin_back = ss_ref[...]

    def back_half(d):
        cos_twist = ct_ref[...]
        sin_twist = st_ref[...]
        sigma = jnp.sum(w2_ref[d] * power, axis=(0, 1), keepdims=True)
        data_real = pr_ref[d]
        data_imag = pi_ref[d]
        q_real = (temp_real * data_real + temp_imag * data_imag).astype(bf16)
        q_imag = (temp_real * data_imag - temp_imag * data_real).astype(bf16)
        d_real = dot_nt(q_real, cos_back) - dot_nt(q_imag, sin_back)
        d_imag = dot_nt(q_real, sin_back) + dot_nt(q_imag, cos_back)
        e_real = (d_real * cos_twist - d_imag * sin_twist).astype(bf16)
        e_imag = (d_real * sin_twist + d_imag * cos_twist).astype(bf16)
        return sigma, e_real, e_imag

    sigma0, e_real, e_imag = back_half(0)
    cos_first = cf_ref[...]
    sin_first = sf_ref[...]
    z_real = jnp.dot(cos_first, e_real, preferred_element_type=f32) - jnp.dot(
        sin_first, e_imag, preferred_element_type=f32
    )
    z_imag = jnp.dot(sin_first, e_real, preferred_element_type=f32) + jnp.dot(
        cos_first, e_imag, preferred_element_type=f32
    )
    first = (z_real * z_real + z_imag * z_imag) / (NFFT * sigma0)
    sigma1, e_real, e_imag = back_half(1)
    er_ref[...] = e_real
    ei_ref[...] = e_imag
    rem = scalar_ref[0]
    tiles = first.shape[1] // BLK
    for col in range(tiles):
        src = lax.rem(col + rem, tiles)
        carry = (col + rem) // tiles
        cols = pl.ds(pl.multiple_of(src * BLK, BLK), BLK)
        e_r = er_ref[:, cols]
        e_i = ei_ref[:, cols]
        cos_rows = cfr_ref[carry]
        sin_rows = sfr_ref[carry]
        z_real = jnp.dot(cos_rows, e_r, preferred_element_type=f32) - jnp.dot(
            sin_rows, e_i, preferred_element_type=f32
        )
        z_imag = jnp.dot(sin_rows, e_r, preferred_element_type=f32) + jnp.dot(
            cos_rows, e_i, preferred_element_type=f32
        )
        second = (z_real * z_real + z_imag * z_imag) / (NFFT * sigma1)
        network = first[:, col * BLK:(col + 1) * BLK] + second
        out_ref[0, :, col:col + 1] = jnp.max(network, axis=1, keepdims=True)


def filter_bank(windowed, tables, signals, weights, shift, det):
    cos_first, sin_first, cos_twist, sin_twist, cos_second, sin_second = tables
    count, rows_used, width = windowed.shape
    pad_rows = 128
    x = jnp.concatenate(
        [windowed, jnp.zeros((count, pad_rows - rows_used, width), windowed.dtype)], axis=1
    )
    tiles = N2 // BLK
    quot = shift // tiles
    scalars = jnp.stack([lax.rem(shift, tiles), det]).astype(jnp.int32)
    doubled_cos = jnp.concatenate([cos_first, cos_first], axis=0)
    doubled_sin = jnp.concatenate([sin_first, sin_first], axis=0)
    cos_rolled = jnp.stack(
        [lax.dynamic_slice_in_dim(doubled_cos, quot + v, N1) for v in range(2)]
    )
    sin_rolled = jnp.stack(
        [lax.dynamic_slice_in_dim(doubled_sin, quot + v, N1) for v in range(2)]
    )
    operands = [
        cos_first[:, :pad_rows], sin_first[:, :pad_rows], cos_twist, sin_twist,
        cos_second, sin_second, cos_first, sin_first, cos_rolled, sin_rolled,
        signals[0], signals[1], weights[0], weights[1],
    ]

    def whole(array):
        nd = array.ndim
        return pl.BlockSpec(array.shape, lambda i, r, nd=nd: (0,) * nd)

    grid_spec = pltpu.PrefetchScalarGridSpec(
        num_scalar_prefetch=1,
        grid=(count,),
        in_specs=[pl.BlockSpec((1, pad_rows, width), lambda i, r: (i, 0, 0))]
        + [whole(a) for a in operands],
        out_specs=pl.BlockSpec((1, N1, tiles), lambda i, r: (i, 0, 0)),
        scratch_shapes=[
            pltpu.VMEM((N1, N2), jnp.bfloat16),
            pltpu.VMEM((N1, N2), jnp.bfloat16),
            pltpu.VMEM((2, N1, N2 // 2), jnp.float32),
            pltpu.VMEM((2, N1, N2 // 2), jnp.float32),
            pltpu.VMEM((2, N1, N2 // 2), jnp.float32),
        ],
    )
    matmuls = 2 * N1 * pad_rows * N2 + 4 * N1 * N2 * (N2 // 2) + 16 * N1 * (N2 // 2) * N2
    out = pl.pallas_call(
        filter_kernel,
        out_shape=jax.ShapeDtypeStruct((count, N1, tiles), jnp.float32),
        grid_spec=grid_spec,
        compiler_params=pltpu.CompilerParams(vmem_limit_bytes=48 * 1024 * 1024),
        cost_estimate=pl.CostEstimate(
            flops=2 * matmuls * count, transcendentals=0, bytes_accessed=8 * 1024 * 1024
        ),
    )(scalars, x, *operands)
    return out.reshape(count, N1 * tiles)


def shards(strain, inv_asd, templates, chirp_blocks, owner, slide):
    tables = make_tables()
    detector = lax.axis_index("det")
    per_dev = templates.shape[0]
    mine = per_dev // 2
    n_blk = NFFT // BLK
    half_blk = n_blk // 2
    filt_count = lax.axis_size("filt")
    swap = [(0, 1), (1, 0)]
    own_signal = strain[0].astype(jnp.bfloat16).reshape(N1, N2)
    own_weight = inv_asd[0].reshape(N2 // 2, N1)
    other_signal = lax.ppermute(own_signal, "det", swap)
    other_weight = lax.ppermute(own_weight, "det", swap)
    samples = jnp.arange(TL, dtype=jnp.int32)
    my_rows = lax.dynamic_slice_in_dim(templates, detector * mine, mine)
    my_blocks = lax.dynamic_slice_in_dim(chirp_blocks, detector * mine, mine)
    windowed = jnp.where(
        samples[None, :] < BLK * my_blocks[:, None], my_rows, jnp.zeros_like(my_rows)
    )
    windowed = windowed.reshape(mine, TL // N2, N2)
    full = filter_bank(
        windowed, tables, (own_signal, other_signal), (own_weight, other_weight),
        slide[0], detector,
    )
    keep = lax.dynamic_slice_in_dim(full, detector * half_blk, half_blk, axis=1)
    give = lax.dynamic_slice_in_dim(full, (1 - detector) * half_blk, half_blk, axis=1)
    got = lax.ppermute(give, "det", swap)
    local = jnp.where(
        detector == 0, jnp.concatenate([keep, got], axis=0), jnp.concatenate([got, keep], axis=0)
    )
    local_max = jnp.max(local, axis=0)
    positions = jnp.arange(per_dev, dtype=jnp.int32)
    slots = jnp.arange(filt_count, dtype=jnp.int32)
    placing = owner[None, :] == slots[:, None]
    source = jnp.sum(jnp.where(placing, positions[None, :], 0), axis=1)
    used = jnp.any(placing, axis=1)
    flagged = jnp.concatenate([local, jnp.ones((per_dev, 128), jnp.float32)], axis=1)
    send_rows = jnp.where(used[:, None], jnp.take(flagged, source, axis=0), 0.0)
    recv_rows, loudest = route_and_max(send_rows[:, None, :], local_max)
    recv_rows = recv_rows.reshape(filt_count, half_blk + 128)
    valid = recv_rows[:, half_blk] > 0.5
    rank = jnp.cumsum(valid.astype(jnp.int32)) - 1
    hits = jnp.logical_and(valid[None, :], rank[None, :] == positions[:, None])
    pick = jnp.sum(jnp.where(hits, slots[None, :], 0), axis=1)
    peaks = jnp.take(recv_rows[:, :half_blk], pick, axis=0)
    return (peaks, loudest)


def solution(mesh):
    return jax.shard_map(
        shards,
        mesh=mesh,
        in_specs=(
            P("det", None),
            P("det", None),
            P(("grp", "filt"), None),
            P(("grp", "filt")),
            P(("grp", "filt")),
            P("grp"),
        ),
        out_specs=(P(("grp", "filt"), "det"), P("det")),
        check_vma=False,
    )
```

```python
import functools

import jax
import ml_dtypes
import numpy as np
import jax.numpy as jnp
from jax import lax
from jax.experimental import pallas as pl
from jax.experimental.pallas import tpu as pltpu
from jax.sharding import PartitionSpec as P

N1 = 256
N2 = 512
NFFT = 131072
BLK = 128
TL = 4096


TWO_PI = 6.283185307179586


def angle_table(rows, cols, period):
    left = np.arange(rows, dtype=np.int64)[:, None]
    right = np.arange(cols, dtype=np.int64)[None, :]
    turns = (left * right % period).astype(np.float32)
    return np.float32(TWO_PI / period) * turns


def make_tables():
    twist = angle_table(N1, N2, NFFT).astype(np.float64)
    second = angle_table(N2, N2 // 2, N2).astype(np.float64)
    cos_second = np.cos(second).astype(np.float32).astype(ml_dtypes.bfloat16)
    sin_second = np.sin(second).astype(np.float32).astype(ml_dtypes.bfloat16)
    return tuple(
        jnp.asarray(table)
        for table in (
            cos_second[0::2],
            sin_second[0::2],
            np.cos(twist).astype(np.float32),
            np.sin(twist).astype(np.float32),
            cos_second,
            sin_second,
        )
    )


def route_kernel(
    stages, send_ref, local_ref, recv_out, out_ref, recv_buf, slot_send, slot_recv, acc_ref,
    *scratch,
):
    det = lax.axis_index("det")
    grp = lax.axis_index("grp")
    filt = lax.axis_index("filt")
    n_grp = lax.axis_size("grp")
    n_filt = send_ref.shape[0]
    mesh_ids = pl.DeviceIdType.MESH

    def position(size, stride):
        if stride == 0:
            return grp
        return lax.rem(filt // stride, size)

    def peer(size, stride, target):
        if stride == 0:
            return (det, target, filt)
        here = position(size, stride)
        return (det, grp, filt + (target - here) * stride)

    barrier = pltpu.get_barrier_semaphore()
    for i in range(n_filt - 1):
        target = lax.rem(filt + 1 + i, n_filt)
        pl.semaphore_signal(barrier, inc=1, device_id=(det, grp, target), device_id_type=mesh_ids)
    for i in range(n_grp - 1):
        target = lax.rem(grp + 1 + i, n_grp)
        pl.semaphore_signal(barrier, inc=1, device_id=(det, target, filt), device_id_type=mesh_ids)
    pl.semaphore_wait(barrier, n_filt - 1 + n_grp - 1)
    slots = []
    for i in range(n_filt - 1):
        target = lax.rem(filt + 1 + i, n_filt)
        copy = pltpu.make_async_remote_copy(
            src_ref=send_ref.at[target],
            dst_ref=recv_buf.at[filt],
            send_sem=slot_send.at[i],
            recv_sem=slot_recv.at[filt],
            device_id=(det, grp, target),
            device_id_type=mesh_ids,
        )
        copy.start()
        slots.append(copy)
    live = [(size, stride) for size, stride in stages if size > 1]
    value = local_ref[...]
    source = local_ref
    for k, (size, stride) in enumerate(live):
        held, send_sems, recv_sems = scratch[3 * k:3 * k + 3]
        here = position(size, stride)
        copies = []
        for i in range(size - 1):
            target = lax.rem(here + 1 + i, size)
            row = size - 2 - i
            copy = pltpu.make_async_remote_copy(
                src_ref=source,
                dst_ref=held.at[row],
                send_sem=send_sems.at[i],
                recv_sem=recv_sems.at[row],
                device_id=peer(size, stride, target),
                device_id_type=mesh_ids,
            )
            copy.start()
            copies.append(copy)
        for copy in copies:
            copy.wait_send()
            copy.wait_recv()
        value = jnp.maximum(value, jnp.max(held[...], axis=0))
        if k + 1 < len(live):
            acc_ref[k] = value
            source = acc_ref.at[k]
    out_ref[...] = value
    for copy in slots:
        copy.wait_send()
    for i in range(n_filt - 1):
        origin = lax.rem(filt + 1 + i, n_filt)
        pltpu.make_async_remote_copy(
            src_ref=send_ref.at[origin],
            dst_ref=recv_buf.at[origin],
            send_sem=slot_send.at[i],
            recv_sem=slot_recv.at[origin],
            device_id=(det, grp, origin),
            device_id_type=mesh_ids,
        ).wait_recv()
    recv_buf[filt] = send_ref[filt]
    recv_out[...] = recv_buf[...]


def stage_layout(n_grp, n_filt):
    inner = 8 if n_filt % 8 == 0 else n_filt
    return ((inner, 1), (n_filt // inner, inner), (n_grp, 0))


def route_and_max(send_rows, local_max):
    stages = stage_layout(lax.axis_size("grp"), lax.axis_size("filt"))
    live = [size for size, _ in stages if size > 1]
    width = local_max.shape[-1]
    n_filt = send_rows.shape[0]
    scratch = [
        pltpu.VMEM(send_rows.shape, send_rows.dtype),
        pltpu.SemaphoreType.DMA((n_filt,)),
        pltpu.SemaphoreType.DMA((n_filt,)),
        pltpu.VMEM((max(len(live), 1), 1, width), jnp.float32),
    ]
    for size in live:
        scratch += [
            pltpu.VMEM((size - 1, 1, width), jnp.float32),
            pltpu.SemaphoreType.DMA((size - 1,)),
            pltpu.SemaphoreType.DMA((size - 1,)),
        ]
    vmem = pl.BlockSpec(memory_space=pltpu.VMEM)
    recv, out = pl.pallas_call(
        functools.partial(route_kernel, stages),
        out_shape=(
            jax.ShapeDtypeStruct(send_rows.shape, send_rows.dtype),
            jax.ShapeDtypeStruct((1, width), jnp.float32),
        ),
        in_specs=[vmem, vmem],
        out_specs=(vmem, vmem),
        scratch_shapes=scratch,
        compiler_params=pltpu.CompilerParams(collective_id=0, has_side_effects=True),
    )(send_rows, local_max.reshape(1, width))
    return recv, out.reshape(width)


def dot_nt(left, right):
    return lax.dot_general(
        left, right, (((1,), (1,)), ((), ())), preferred_element_type=jnp.float32
    )


def filter_kernel(scalar_ref, x_ref, *refs):
    count = 14
    sources = refs[:count]
    out_ref, er_ref, ei_ref, pr_ref, pi_ref, w2_ref = refs[count:count + 6]
    held = refs[count + 6:2 * count + 6]
    fetch_sems = refs[2 * count + 6]
    (cfn_ref, sfn_ref, ct_ref, st_ref, cs_ref, ss_ref, cf_ref, sf_ref,
     cfr_ref, sfr_ref, sown_ref, soth_ref, wown_ref, woth_ref) = held
    f32 = jnp.float32
    bf16 = jnp.bfloat16

    def first_stage(cos_rows, sin_rows, x):
        cos_twist = ct_ref[...]
        sin_twist = st_ref[...]
        real_a = jnp.dot(cos_rows, x, preferred_element_type=f32)
        imag_a = -jnp.dot(sin_rows, x, preferred_element_type=f32)
        real_b = (real_a * cos_twist + imag_a * sin_twist).astype(bf16)
        imag_b = (imag_a * cos_twist - real_a * sin_twist).astype(bf16)
        cos_second = cs_ref[...]
        sin_second = ss_ref[...]
        real_x = jnp.dot(real_b, cos_second, preferred_element_type=f32) + jnp.dot(
            imag_b, sin_second, preferred_element_type=f32
        )
        imag_x = jnp.dot(imag_b, cos_second, preferred_element_type=f32) - jnp.dot(
            real_b, sin_second, preferred_element_type=f32
        )
        return real_x, imag_x

    @pl.when(pl.program_id(0) == 0)
    def _():
        fetches = [
            pltpu.make_async_copy(src, dst, fetch_sems.at[k])
            for k, (src, dst) in enumerate(zip(sources, held))
        ]
        for fetch in fetches:
            fetch.start()
        for fetch in fetches:
            fetch.wait()
        det = scalar_ref[1]
        for slot, sig_ref, w_ref in ((det, sown_ref, wown_ref), (1 - det, soth_ref, woth_ref)):
            real_s, imag_s = first_stage(cf_ref[...], sf_ref[...], sig_ref[...])
            weight = jnp.transpose(w_ref[...])
            pr_ref[slot] = weight * real_s
            pi_ref[slot] = weight * imag_s
            w2_ref[slot] = weight * weight

    temp_real, temp_imag = first_stage(cfn_ref[...], sfn_ref[...], x_ref[0])
    power = temp_real * temp_real + temp_imag * temp_imag
    cos_back = cs_ref[...]
    sin_back = ss_ref[...]

    def back_half(d):
        cos_twist = ct_ref[...]
        sin_twist = st_ref[...]
        sigma = jnp.sum(w2_ref[d] * power, axis=(0, 1), keepdims=True)
        data_real = pr_ref[d]
        data_imag = pi_ref[d]
        q_real = (temp_real * data_real + temp_imag * data_imag).astype(bf16)
        q_imag = (temp_real * data_imag - temp_imag * data_real).astype(bf16)
        d_real = dot_nt(q_real, cos_back) - dot_nt(q_imag, sin_back)
        d_imag = dot_nt(q_real, sin_back) + dot_nt(q_imag, cos_back)
        e_real = (d_real * cos_twist - d_imag * sin_twist).astype(bf16)
        e_imag = (d_real * sin_twist + d_imag * cos_twist).astype(bf16)
        return sigma, e_real, e_imag

    sigma0, e_real, e_imag = back_half(0)
    cos_first = cf_ref[...]
    sin_first = sf_ref[...]
    z_real = jnp.dot(cos_first, e_real, preferred_element_type=f32) - jnp.dot(
        sin_first, e_imag, preferred_element_type=f32
    )
    z_imag = jnp.dot(sin_first, e_real, preferred_element_type=f32) + jnp.dot(
        cos_first, e_imag, preferred_element_type=f32
    )
    first = (z_real * z_real + z_imag * z_imag) / (NFFT * sigma0)
    sigma1, e_real, e_imag = back_half(1)
    er_ref[...] = e_real
    ei_ref[...] = e_imag
    rem = scalar_ref[0]
    tiles = first.shape[1] // BLK
    for col in range(tiles):
        src = lax.rem(col + rem, tiles)
        carry = (col + rem) // tiles
        cols = pl.ds(pl.multiple_of(src * BLK, BLK), BLK)
        e_r = er_ref[:, cols]
        e_i = ei_ref[:, cols]
        cos_rows = cfr_ref[carry]
        sin_rows = sfr_ref[carry]
        z_real = jnp.dot(cos_rows, e_r, preferred_element_type=f32) - jnp.dot(
            sin_rows, e_i, preferred_element_type=f32
        )
        z_imag = jnp.dot(sin_rows, e_r, preferred_element_type=f32) + jnp.dot(
            cos_rows, e_i, preferred_element_type=f32
        )
        second = (z_real * z_real + z_imag * z_imag) / (NFFT * sigma1)
        network = first[:, col * BLK:(col + 1) * BLK] + second
        out_ref[0, :, col:col + 1] = jnp.max(network, axis=1, keepdims=True)


def filter_bank(windowed, tables, signals, weights, shift, det):
    cos_first, sin_first, cos_twist, sin_twist, cos_second, sin_second = tables
    count, rows_used, width = windowed.shape
    pad_rows = 128
    x = jnp.concatenate(
        [windowed, jnp.zeros((count, pad_rows - rows_used, width), windowed.dtype)], axis=1
    )
    tiles = N2 // BLK
    quot = shift // tiles
    scalars = jnp.stack([lax.rem(shift, tiles), det]).astype(jnp.int32)
    doubled_cos = jnp.concatenate([cos_first, cos_first], axis=0)
    doubled_sin = jnp.concatenate([sin_first, sin_first], axis=0)
    cos_rolled = jnp.stack(
        [lax.dynamic_slice_in_dim(doubled_cos, quot + v, N1) for v in range(2)]
    )
    sin_rolled = jnp.stack(
        [lax.dynamic_slice_in_dim(doubled_sin, quot + v, N1) for v in range(2)]
    )
    operands = [
        cos_first[:, :pad_rows], sin_first[:, :pad_rows], cos_twist, sin_twist,
        cos_second, sin_second, cos_first, sin_first, cos_rolled, sin_rolled,
        signals[0], signals[1], weights[0], weights[1],
    ]


    grid_spec = pltpu.PrefetchScalarGridSpec(
        num_scalar_prefetch=1,
        grid=(count,),
        in_specs=[pl.BlockSpec((1, pad_rows, width), lambda i, r: (i, 0, 0))]
        + [pl.BlockSpec(memory_space=pl.ANY)] * len(operands),
        out_specs=pl.BlockSpec((1, N1, tiles), lambda i, r: (i, 0, 0)),
        scratch_shapes=[
            pltpu.VMEM((N1, N2), jnp.bfloat16),
            pltpu.VMEM((N1, N2), jnp.bfloat16),
            pltpu.VMEM((2, N1, N2 // 2), jnp.float32),
            pltpu.VMEM((2, N1, N2 // 2), jnp.float32),
            pltpu.VMEM((2, N1, N2 // 2), jnp.float32),
        ]
        + [pltpu.VMEM(a.shape, a.dtype) for a in operands]
        + [pltpu.SemaphoreType.DMA((len(operands),))],
    )
    matmuls = 2 * N1 * pad_rows * N2 + 4 * N1 * N2 * (N2 // 2) + 16 * N1 * (N2 // 2) * N2
    out = pl.pallas_call(
        filter_kernel,
        out_shape=jax.ShapeDtypeStruct((count, N1, tiles), jnp.float32),
        grid_spec=grid_spec,
        compiler_params=pltpu.CompilerParams(vmem_limit_bytes=56 * 1024 * 1024),
        cost_estimate=pl.CostEstimate(
            flops=2 * matmuls * count, transcendentals=0, bytes_accessed=8 * 1024 * 1024
        ),
    )(scalars, x, *operands)
    return out.reshape(count, N1 * tiles)


def shards(strain, inv_asd, templates, chirp_blocks, owner, slide):
    tables = make_tables()
    detector = lax.axis_index("det")
    per_dev = templates.shape[0]
    mine = per_dev // 2
    n_blk = NFFT // BLK
    half_blk = n_blk // 2
    filt_count = lax.axis_size("filt")
    swap = [(0, 1), (1, 0)]
    own_signal = strain[0].astype(jnp.bfloat16).reshape(N1, N2)
    own_weight = inv_asd[0].reshape(N2 // 2, N1)
    other_signal = lax.ppermute(own_signal, "det", swap)
    other_weight = lax.ppermute(own_weight, "det", swap)
    samples = jnp.arange(TL, dtype=jnp.int32)
    my_rows = lax.dynamic_slice_in_dim(templates, detector * mine, mine)
    my_blocks = lax.dynamic_slice_in_dim(chirp_blocks, detector * mine, mine)
    windowed = jnp.where(
        samples[None, :] < BLK * my_blocks[:, None], my_rows, jnp.zeros_like(my_rows)
    )
    windowed = windowed.reshape(mine, TL // N2, N2)
    full = filter_bank(
        windowed, tables, (own_signal, other_signal), (own_weight, other_weight),
        slide[0], detector,
    )
    keep = lax.dynamic_slice_in_dim(full, detector * half_blk, half_blk, axis=1)
    give = lax.dynamic_slice_in_dim(full, (1 - detector) * half_blk, half_blk, axis=1)
    got = lax.ppermute(give, "det", swap)
    local = jnp.where(
        detector == 0, jnp.concatenate([keep, got], axis=0), jnp.concatenate([got, keep], axis=0)
    )
    local_max = jnp.max(local, axis=0)
    positions = jnp.arange(per_dev, dtype=jnp.int32)
    slots = jnp.arange(filt_count, dtype=jnp.int32)
    placing = owner[None, :] == slots[:, None]
    source = jnp.sum(jnp.where(placing, positions[None, :], 0), axis=1)
    used = jnp.any(placing, axis=1)
    flagged = jnp.concatenate([local, jnp.ones((per_dev, 128), jnp.float32)], axis=1)
    send_rows = jnp.where(used[:, None], jnp.take(flagged, source, axis=0), 0.0)
    recv_rows, loudest = route_and_max(send_rows[:, None, :], local_max)
    recv_rows = recv_rows.reshape(filt_count, half_blk + 128)
    valid = recv_rows[:, half_blk] > 0.5
    rank = jnp.cumsum(valid.astype(jnp.int32)) - 1
    hits = jnp.logical_and(valid[None, :], rank[None, :] == positions[:, None])
    pick = jnp.sum(jnp.where(hits, slots[None, :], 0), axis=1)
    peaks = jnp.take(recv_rows[:, :half_blk], pick, axis=0)
    return (peaks, loudest)


def solution(mesh):
    return jax.shard_map(
        shards,
        mesh=mesh,
        in_specs=(
            P("det", None),
            P("det", None),
            P(("grp", "filt"), None),
            P(("grp", "filt")),
            P(("grp", "filt")),
            P("grp"),
        ),
        out_specs=(P(("grp", "filt"), "det"), P("det")),
        check_vma=False,
    )
```

```python
import functools

import jax
import ml_dtypes
import numpy as np
import jax.numpy as jnp
from jax import lax
from jax.experimental import pallas as pl
from jax.experimental.pallas import tpu as pltpu
from jax.sharding import PartitionSpec as P

N1 = 256
N2 = 512
NFFT = 131072
BLK = 128
TL = 4096


TWO_PI = 6.283185307179586


def angle_table(rows, cols, period):
    left = np.arange(rows, dtype=np.int64)[:, None]
    right = np.arange(cols, dtype=np.int64)[None, :]
    turns = (left * right % period).astype(np.float32)
    return np.float32(TWO_PI / period) * turns


def make_tables():
    twist = angle_table(N1, N2, NFFT).astype(np.float64)
    second = angle_table(N2, N2 // 2, N2).astype(np.float64)
    cos_second = np.cos(second).astype(np.float32).astype(ml_dtypes.bfloat16)
    sin_second = np.sin(second).astype(np.float32).astype(ml_dtypes.bfloat16)
    return tuple(
        jnp.asarray(table)
        for table in (
            cos_second[0::2],
            sin_second[0::2],
            np.cos(twist).astype(np.float32),
            np.sin(twist).astype(np.float32),
            cos_second,
            sin_second,
        )
    )


def route_kernel(
    split, send_ref, recv_out, out_ref, recv_buf, slot_send, slot_recv, acc_ref,
    held, grp_send, grp_recv,
):
    det = lax.axis_index("det")
    grp = lax.axis_index("grp")
    filt = lax.axis_index("filt")
    n_grp = lax.axis_size("grp")
    n_filt = send_ref.shape[0]
    mesh_ids = pl.DeviceIdType.MESH
    barrier = pltpu.get_barrier_semaphore()
    for i in range(n_filt - 1):
        target = lax.rem(filt + 1 + i, n_filt)
        pl.semaphore_signal(barrier, inc=1, device_id=(det, grp, target), device_id_type=mesh_ids)
    for i in range(n_grp - 1):
        target = lax.rem(grp + 1 + i, n_grp)
        pl.semaphore_signal(barrier, inc=1, device_id=(det, target, filt), device_id_type=mesh_ids)
    pl.semaphore_wait(barrier, n_filt - 1 + n_grp - 1)
    slots = []
    for i in range(n_filt - 1):
        target = lax.rem(filt + 1 + i, n_filt)
        copy = pltpu.make_async_remote_copy(
            src_ref=send_ref.at[target],
            dst_ref=recv_buf.at[filt],
            send_sem=slot_send.at[i],
            recv_sem=slot_recv.at[filt],
            device_id=(det, grp, target),
            device_id_type=mesh_ids,
        )
        copy.start()
        slots.append(copy)
    for copy in slots:
        copy.wait_send()
    for i in range(n_filt - 1):
        origin = lax.rem(filt + 1 + i, n_filt)
        pltpu.make_async_remote_copy(
            src_ref=send_ref.at[origin],
            dst_ref=recv_buf.at[origin],
            send_sem=slot_send.at[i],
            recv_sem=slot_recv.at[origin],
            device_id=(det, grp, origin),
            device_id_type=mesh_ids,
        ).wait_recv()
    recv_buf[filt] = send_ref[filt]
    rows = recv_buf[...]
    recv_out[...] = rows
    value = jnp.max(rows[:, :, split:], axis=0)
    if n_grp > 1:
        acc_ref[...] = value
        copies = []
        for i in range(n_grp - 1):
            target = lax.rem(grp + 1 + i, n_grp)
            row = n_grp - 2 - i
            copy = pltpu.make_async_remote_copy(
                src_ref=acc_ref,
                dst_ref=held.at[row],
                send_sem=grp_send.at[i],
                recv_sem=grp_recv.at[row],
                device_id=(det, target, filt),
                device_id_type=mesh_ids,
            )
            copy.start()
            copies.append(copy)
        for copy in copies:
            copy.wait_send()
            copy.wait_recv()
        value = jnp.maximum(value, jnp.max(held[...], axis=0))
    out_ref[...] = value


def route_and_max(send_rows, split):
    n_grp = lax.axis_size("grp")
    n_filt = send_rows.shape[0]
    width = send_rows.shape[-1] - split
    vmem = pl.BlockSpec(memory_space=pltpu.VMEM)
    recv, out = pl.pallas_call(
        functools.partial(route_kernel, split),
        out_shape=(
            jax.ShapeDtypeStruct(send_rows.shape, send_rows.dtype),
            jax.ShapeDtypeStruct((1, width), jnp.float32),
        ),
        in_specs=[vmem],
        out_specs=(vmem, vmem),
        scratch_shapes=[
            pltpu.VMEM(send_rows.shape, send_rows.dtype),
            pltpu.SemaphoreType.DMA((n_filt,)),
            pltpu.SemaphoreType.DMA((n_filt,)),
            pltpu.VMEM((1, width), jnp.float32),
            pltpu.VMEM((max(n_grp - 1, 1), 1, width), jnp.float32),
            pltpu.SemaphoreType.DMA((max(n_grp - 1, 1),)),
            pltpu.SemaphoreType.DMA((max(n_grp - 1, 1),)),
        ],
        compiler_params=pltpu.CompilerParams(collective_id=0, has_side_effects=True),
    )(send_rows)
    return recv, out.reshape(width)


def dot_nt(left, right):
    return lax.dot_general(
        left, right, (((1,), (1,)), ((), ())), preferred_element_type=jnp.float32
    )


def filter_kernel(
    scalar_ref, x_ref, cfn_ref, sfn_ref, ct_ref, st_ref, cs_ref, ss_ref, cf_ref, sf_ref,
    cfr_ref, sfr_ref, sown_ref, soth_ref, wown_ref, woth_ref, out_ref,
    er_ref, ei_ref, pr_ref, pi_ref, w2_ref,
):
    f32 = jnp.float32
    bf16 = jnp.bfloat16

    def first_stage(cos_rows, sin_rows, x):
        cos_twist = ct_ref[...]
        sin_twist = st_ref[...]
        real_a = jnp.dot(cos_rows, x, preferred_element_type=f32)
        imag_a = -jnp.dot(sin_rows, x, preferred_element_type=f32)
        real_b = (real_a * cos_twist + imag_a * sin_twist).astype(bf16)
        imag_b = (imag_a * cos_twist - real_a * sin_twist).astype(bf16)
        cos_second = cs_ref[...]
        sin_second = ss_ref[...]
        real_x = jnp.dot(real_b, cos_second, preferred_element_type=f32) + jnp.dot(
            imag_b, sin_second, preferred_element_type=f32
        )
        imag_x = jnp.dot(imag_b, cos_second, preferred_element_type=f32) - jnp.dot(
            real_b, sin_second, preferred_element_type=f32
        )
        return real_x, imag_x

    @pl.when(pl.program_id(0) == 0)
    def _():
        det = scalar_ref[1]
        for slot, sig_ref, w_ref in ((det, sown_ref, wown_ref), (1 - det, soth_ref, woth_ref)):
            real_s, imag_s = first_stage(cf_ref[...], sf_ref[...], sig_ref[...])
            weight = jnp.transpose(w_ref[...])
            pr_ref[slot] = weight * real_s
            pi_ref[slot] = weight * imag_s
            w2_ref[slot] = weight * weight

    temp_real, temp_imag = first_stage(cfn_ref[...], sfn_ref[...], x_ref[0])
    power = temp_real * temp_real + temp_imag * temp_imag
    cos_back = cs_ref[...]
    sin_back = ss_ref[...]

    def back_half(d):
        cos_twist = ct_ref[...]
        sin_twist = st_ref[...]
        sigma = jnp.sum(w2_ref[d] * power, axis=(0, 1), keepdims=True)
        data_real = pr_ref[d]
        data_imag = pi_ref[d]
        q_real = (temp_real * data_real + temp_imag * data_imag).astype(bf16)
        q_imag = (temp_real * data_imag - temp_imag * data_real).astype(bf16)
        d_real = dot_nt(q_real, cos_back) - dot_nt(q_imag, sin_back)
        d_imag = dot_nt(q_real, sin_back) + dot_nt(q_imag, cos_back)
        e_real = (d_real * cos_twist - d_imag * sin_twist).astype(bf16)
        e_imag = (d_real * sin_twist + d_imag * cos_twist).astype(bf16)
        return sigma, e_real, e_imag

    sigma0, e_real, e_imag = back_half(0)
    cos_first = cf_ref[...]
    sin_first = sf_ref[...]
    z_real = jnp.dot(cos_first, e_real, preferred_element_type=f32) - jnp.dot(
        sin_first, e_imag, preferred_element_type=f32
    )
    z_imag = jnp.dot(sin_first, e_real, preferred_element_type=f32) + jnp.dot(
        cos_first, e_imag, preferred_element_type=f32
    )
    first = (z_real * z_real + z_imag * z_imag) / (NFFT * sigma0)
    sigma1, e_real, e_imag = back_half(1)
    er_ref[...] = e_real
    ei_ref[...] = e_imag
    rem = scalar_ref[0]
    tiles = first.shape[1] // BLK
    for col in range(tiles):
        src = lax.rem(col + rem, tiles)
        carry = (col + rem) // tiles
        cols = pl.ds(pl.multiple_of(src * BLK, BLK), BLK)
        e_r = er_ref[:, cols]
        e_i = ei_ref[:, cols]
        cos_rows = cfr_ref[carry]
        sin_rows = sfr_ref[carry]
        z_real = jnp.dot(cos_rows, e_r, preferred_element_type=f32) - jnp.dot(
            sin_rows, e_i, preferred_element_type=f32
        )
        z_imag = jnp.dot(sin_rows, e_r, preferred_element_type=f32) + jnp.dot(
            cos_rows, e_i, preferred_element_type=f32
        )
        second = (z_real * z_real + z_imag * z_imag) / (NFFT * sigma1)
        network = first[:, col * BLK:(col + 1) * BLK] + second
        out_ref[0, :, col:col + 1] = jnp.max(network, axis=1, keepdims=True)


def filter_bank(windowed, tables, signals, weights, shift, det):
    cos_first, sin_first, cos_twist, sin_twist, cos_second, sin_second = tables
    count, rows_used, width = windowed.shape
    pad_rows = 128
    x = jnp.concatenate(
        [windowed, jnp.zeros((count, pad_rows - rows_used, width), windowed.dtype)], axis=1
    )
    tiles = N2 // BLK
    quot = shift // tiles
    scalars = jnp.stack([lax.rem(shift, tiles), det]).astype(jnp.int32)
    doubled_cos = jnp.concatenate([cos_first, cos_first], axis=0)
    doubled_sin = jnp.concatenate([sin_first, sin_first], axis=0)
    cos_rolled = jnp.stack(
        [lax.dynamic_slice_in_dim(doubled_cos, quot + v, N1) for v in range(2)]
    )
    sin_rolled = jnp.stack(
        [lax.dynamic_slice_in_dim(doubled_sin, quot + v, N1) for v in range(2)]
    )
    operands = [
        cos_first[:, :pad_rows], sin_first[:, :pad_rows], cos_twist, sin_twist,
        cos_second, sin_second, cos_first, sin_first, cos_rolled, sin_rolled,
        signals[0], signals[1], weights[0], weights[1],
    ]

    def whole(array):
        nd = array.ndim
        return pl.BlockSpec(array.shape, lambda i, r, nd=nd: (0,) * nd)

    grid_spec = pltpu.PrefetchScalarGridSpec(
        num_scalar_prefetch=1,
        grid=(count,),
        in_specs=[pl.BlockSpec((1, pad_rows, width), lambda i, r: (i, 0, 0))]
        + [whole(a) for a in operands],
        out_specs=pl.BlockSpec((1, N1, tiles), lambda i, r: (i, 0, 0)),
        scratch_shapes=[
            pltpu.VMEM((N1, N2), jnp.bfloat16),
            pltpu.VMEM((N1, N2), jnp.bfloat16),
            pltpu.VMEM((2, N1, N2 // 2), jnp.float32),
            pltpu.VMEM((2, N1, N2 // 2), jnp.float32),
            pltpu.VMEM((2, N1, N2 // 2), jnp.float32),
        ],
    )
    matmuls = 2 * N1 * pad_rows * N2 + 4 * N1 * N2 * (N2 // 2) + 16 * N1 * (N2 // 2) * N2
    out = pl.pallas_call(
        filter_kernel,
        out_shape=jax.ShapeDtypeStruct((count, N1, tiles), jnp.float32),
        grid_spec=grid_spec,
        compiler_params=pltpu.CompilerParams(vmem_limit_bytes=48 * 1024 * 1024),
        cost_estimate=pl.CostEstimate(
            flops=2 * matmuls * count, transcendentals=0, bytes_accessed=8 * 1024 * 1024
        ),
    )(scalars, x, *operands)
    return out.reshape(count, N1 * tiles)


def shards(strain, inv_asd, templates, chirp_blocks, owner, slide):
    tables = make_tables()
    detector = lax.axis_index("det")
    per_dev = templates.shape[0]
    mine = per_dev // 2
    n_blk = NFFT // BLK
    half_blk = n_blk // 2
    filt_count = lax.axis_size("filt")
    swap = [(0, 1), (1, 0)]
    own_signal = strain.reshape(N1, N2).astype(jnp.bfloat16)
    own_weight = inv_asd.reshape(N2 // 2, N1)
    other_signal = lax.ppermute(own_signal, "det", swap)
    other_weight = lax.ppermute(own_weight, "det", swap)
    samples = jnp.arange(TL, dtype=jnp.int32)
    my_rows = lax.dynamic_slice_in_dim(templates, detector * mine, mine)
    my_blocks = lax.dynamic_slice_in_dim(chirp_blocks, detector * mine, mine)
    windowed = jnp.where(
        samples[None, :] < BLK * my_blocks[:, None], my_rows, jnp.zeros_like(my_rows)
    )
    windowed = windowed.reshape(mine, TL // N2, N2)
    full = filter_bank(
        windowed, tables, (own_signal, other_signal), (own_weight, other_weight),
        slide[0], detector,
    )
    keep = lax.dynamic_slice_in_dim(full, detector * half_blk, half_blk, axis=1)
    give = lax.dynamic_slice_in_dim(full, (1 - detector) * half_blk, half_blk, axis=1)
    got = lax.ppermute(give, "det", swap)
    local = jnp.where(
        detector == 0, jnp.concatenate([keep, got], axis=0), jnp.concatenate([got, keep], axis=0)
    )
    local_max = jnp.max(local, axis=0)
    positions = jnp.arange(per_dev, dtype=jnp.int32)
    slots = jnp.arange(filt_count, dtype=jnp.int32)
    placing = owner[None, :] == slots[:, None]
    source = jnp.sum(jnp.where(placing, positions[None, :], 0), axis=1)
    used = jnp.any(placing, axis=1)
    flagged = jnp.concatenate([local, jnp.ones((per_dev, 128), jnp.float32)], axis=1)
    send_rows = jnp.where(used[:, None], jnp.take(flagged, source, axis=0), 0.0)
    split = half_blk + 128
    send_rows = jnp.concatenate(
        [send_rows, jnp.broadcast_to(local_max[None, :], (filt_count, half_blk))], axis=1
    )
    recv_rows, loudest = route_and_max(send_rows[:, None, :], split)
    recv_rows = recv_rows.reshape(filt_count, split + half_blk)
    valid = recv_rows[:, half_blk] > 0.5
    rank = jnp.cumsum(valid.astype(jnp.int32)) - 1
    hits = jnp.logical_and(valid[None, :], rank[None, :] == positions[:, None])
    pick = jnp.sum(jnp.where(hits, slots[None, :], 0), axis=1)
    peaks = jnp.take(recv_rows[:, :half_blk], pick, axis=0)
    return (peaks, loudest)


def solution(mesh):
    return jax.shard_map(
        shards,
        mesh=mesh,
        in_specs=(
            P("det", None),
            P("det", None),
            P(("grp", "filt"), None),
            P(("grp", "filt")),
            P(("grp", "filt")),
            P("grp"),
        ),
        out_specs=(P(("grp", "filt"), "det"), P("det")),
        check_vma=False,
    )
```

```python
import functools

import jax
import ml_dtypes
import numpy as np
import jax.numpy as jnp
from jax import lax
from jax.experimental import pallas as pl
from jax.experimental.pallas import tpu as pltpu
from jax.sharding import PartitionSpec as P

N1 = 256
N2 = 512
NFFT = 131072
BLK = 128
TL = 4096


TWO_PI = 6.283185307179586


def angle_table(rows, cols, period):
    left = np.arange(rows, dtype=np.int64)[:, None]
    right = np.arange(cols, dtype=np.int64)[None, :]
    turns = (left * right % period).astype(np.float32)
    return np.float32(TWO_PI / period) * turns


def make_tables():
    twist = angle_table(N1, N2, NFFT).astype(np.float64)
    second = angle_table(N2, N2 // 2, N2).astype(np.float64)
    cos_second = np.cos(second).astype(np.float32).astype(ml_dtypes.bfloat16)
    sin_second = np.sin(second).astype(np.float32).astype(ml_dtypes.bfloat16)
    return tuple(
        jnp.asarray(table)
        for table in (
            cos_second[0::2],
            sin_second[0::2],
            np.cos(twist).astype(np.float32),
            np.sin(twist).astype(np.float32),
            cos_second,
            sin_second,
        )
    )


def route_kernel(
    split, send_ref, recv_out, out_ref, recv_buf, slot_send, slot_recv, acc_ref,
    held, grp_send, grp_recv,
):
    det = lax.axis_index("det")
    grp = lax.axis_index("grp")
    filt = lax.axis_index("filt")
    n_grp = lax.axis_size("grp")
    n_filt = send_ref.shape[0]
    mesh_ids = pl.DeviceIdType.MESH
    barrier = pltpu.get_barrier_semaphore()
    for i in range(n_filt - 1):
        target = lax.rem(filt + 1 + i, n_filt)
        pl.semaphore_signal(barrier, inc=1, device_id=(det, grp, target), device_id_type=mesh_ids)
    for i in range(n_grp - 1):
        target = lax.rem(grp + 1 + i, n_grp)
        pl.semaphore_signal(barrier, inc=1, device_id=(det, target, filt), device_id_type=mesh_ids)
    pl.semaphore_wait(barrier, n_filt - 1 + n_grp - 1)
    slots = []
    for i in range(n_filt - 1):
        target = lax.rem(filt + 1 + i, n_filt)
        copy = pltpu.make_async_remote_copy(
            src_ref=send_ref.at[target],
            dst_ref=recv_buf.at[filt],
            send_sem=slot_send.at[i],
            recv_sem=slot_recv.at[filt],
            device_id=(det, grp, target),
            device_id_type=mesh_ids,
        )
        copy.start()
        slots.append(copy)
    for copy in slots:
        copy.wait_send()
    for i in range(n_filt - 1):
        origin = lax.rem(filt + 1 + i, n_filt)
        pltpu.make_async_remote_copy(
            src_ref=send_ref.at[origin],
            dst_ref=recv_buf.at[origin],
            send_sem=slot_send.at[i],
            recv_sem=slot_recv.at[origin],
            device_id=(det, grp, origin),
            device_id_type=mesh_ids,
        ).wait_recv()
    recv_buf[filt] = send_ref[filt]
    rows = recv_buf[...]
    recv_out[...] = rows
    value = jnp.max(rows[:, :, split:], axis=0)
    if n_grp > 1:
        acc_ref[...] = value
        copies = []
        for i in range(n_grp - 1):
            target = lax.rem(grp + 1 + i, n_grp)
            row = n_grp - 2 - i
            copy = pltpu.make_async_remote_copy(
                src_ref=acc_ref,
                dst_ref=held.at[row],
                send_sem=grp_send.at[i],
                recv_sem=grp_recv.at[row],
                device_id=(det, target, filt),
                device_id_type=mesh_ids,
            )
            copy.start()
            copies.append(copy)
        for copy in copies:
            copy.wait_send()
            copy.wait_recv()
        value = jnp.maximum(value, jnp.max(held[...], axis=0))
    out_ref[...] = value


def route_and_max(send_rows, split):
    n_grp = lax.axis_size("grp")
    n_filt = send_rows.shape[0]
    width = send_rows.shape[-1] - split
    vmem = pl.BlockSpec(memory_space=pltpu.VMEM)
    recv, out = pl.pallas_call(
        functools.partial(route_kernel, split),
        out_shape=(
            jax.ShapeDtypeStruct(send_rows.shape, send_rows.dtype),
            jax.ShapeDtypeStruct((1, width), jnp.float32),
        ),
        in_specs=[vmem],
        out_specs=(vmem, vmem),
        scratch_shapes=[
            pltpu.VMEM(send_rows.shape, send_rows.dtype),
            pltpu.SemaphoreType.DMA((n_filt,)),
            pltpu.SemaphoreType.DMA((n_filt,)),
            pltpu.VMEM((1, width), jnp.float32),
            pltpu.VMEM((max(n_grp - 1, 1), 1, width), jnp.float32),
            pltpu.SemaphoreType.DMA((max(n_grp - 1, 1),)),
            pltpu.SemaphoreType.DMA((max(n_grp - 1, 1),)),
        ],
        compiler_params=pltpu.CompilerParams(collective_id=0, has_side_effects=True),
    )(send_rows)
    return recv, out.reshape(width)


def dot_nt(left, right):
    return lax.dot_general(
        left, right, (((1,), (1,)), ((), ())), preferred_element_type=jnp.float32
    )


def filter_kernel(scalar_ref, x_ref, *refs):
    sources = refs[:8]
    cfr_ref, sfr_ref, sown_ref, soth_ref, wown_ref, woth_ref = refs[8:14]
    out_ref, er_ref, ei_ref, pr_ref, pi_ref, w2_ref = refs[14:20]
    held = refs[20:28]
    fetch_sems = refs[28]
    cfn_ref, sfn_ref, ct_ref, st_ref, cs_ref, ss_ref, cf_ref, sf_ref = held
    f32 = jnp.float32
    bf16 = jnp.bfloat16

    def first_stage(cos_rows, sin_rows, x):
        cos_twist = ct_ref[...]
        sin_twist = st_ref[...]
        real_a = jnp.dot(cos_rows, x, preferred_element_type=f32)
        imag_a = -jnp.dot(sin_rows, x, preferred_element_type=f32)
        real_b = (real_a * cos_twist + imag_a * sin_twist).astype(bf16)
        imag_b = (imag_a * cos_twist - real_a * sin_twist).astype(bf16)
        cos_second = cs_ref[...]
        sin_second = ss_ref[...]
        real_x = jnp.dot(real_b, cos_second, preferred_element_type=f32) + jnp.dot(
            imag_b, sin_second, preferred_element_type=f32
        )
        imag_x = jnp.dot(imag_b, cos_second, preferred_element_type=f32) - jnp.dot(
            real_b, sin_second, preferred_element_type=f32
        )
        return real_x, imag_x

    @pl.when(pl.program_id(0) == 0)
    def _():
        fetches = [
            pltpu.make_async_copy(src, dst, fetch_sems.at[k])
            for k, (src, dst) in enumerate(zip(sources, held))
        ]
        for fetch in fetches:
            fetch.start()
        for fetch in fetches:
            fetch.wait()
        det = scalar_ref[1]
        for slot, sig_ref, w_ref in ((det, sown_ref, wown_ref), (1 - det, soth_ref, woth_ref)):
            real_s, imag_s = first_stage(cf_ref[...], sf_ref[...], sig_ref[...])
            weight = jnp.transpose(w_ref[...])
            pr_ref[slot] = weight * real_s
            pi_ref[slot] = weight * imag_s
            w2_ref[slot] = weight * weight

    temp_real, temp_imag = first_stage(cfn_ref[...], sfn_ref[...], x_ref[0])
    power = temp_real * temp_real + temp_imag * temp_imag
    cos_back = cs_ref[...]
    sin_back = ss_ref[...]

    def back_half(d):
        cos_twist = ct_ref[...]
        sin_twist = st_ref[...]
        sigma = jnp.sum(w2_ref[d] * power, axis=(0, 1), keepdims=True)
        data_real = pr_ref[d]
        data_imag = pi_ref[d]
        q_real = (temp_real * data_real + temp_imag * data_imag).astype(bf16)
        q_imag = (temp_real * data_imag - temp_imag * data_real).astype(bf16)
        d_real = dot_nt(q_real, cos_back) - dot_nt(q_imag, sin_back)
        d_imag = dot_nt(q_real, sin_back) + dot_nt(q_imag, cos_back)
        e_real = (d_real * cos_twist - d_imag * sin_twist).astype(bf16)
        e_imag = (d_real * sin_twist + d_imag * cos_twist).astype(bf16)
        return sigma, e_real, e_imag

    sigma0, e_real, e_imag = back_half(0)
    cos_first = cf_ref[...]
    sin_first = sf_ref[...]
    z_real = jnp.dot(cos_first, e_real, preferred_element_type=f32) - jnp.dot(
        sin_first, e_imag, preferred_element_type=f32
    )
    z_imag = jnp.dot(sin_first, e_real, preferred_element_type=f32) + jnp.dot(
        cos_first, e_imag, preferred_element_type=f32
    )
    first = (z_real * z_real + z_imag * z_imag) / (NFFT * sigma0)
    sigma1, e_real, e_imag = back_half(1)
    er_ref[...] = e_real
    ei_ref[...] = e_imag
    rem = scalar_ref[0]
    tiles = first.shape[1] // BLK
    for col in range(tiles):
        src = lax.rem(col + rem, tiles)
        carry = (col + rem) // tiles
        cols = pl.ds(pl.multiple_of(src * BLK, BLK), BLK)
        e_r = er_ref[:, cols]
        e_i = ei_ref[:, cols]
        cos_rows = cfr_ref[carry]
        sin_rows = sfr_ref[carry]
        z_real = jnp.dot(cos_rows, e_r, preferred_element_type=f32) - jnp.dot(
            sin_rows, e_i, preferred_element_type=f32
        )
        z_imag = jnp.dot(sin_rows, e_r, preferred_element_type=f32) + jnp.dot(
            cos_rows, e_i, preferred_element_type=f32
        )
        second = (z_real * z_real + z_imag * z_imag) / (NFFT * sigma1)
        network = first[:, col * BLK:(col + 1) * BLK] + second
        out_ref[0, :, col:col + 1] = jnp.max(network, axis=1, keepdims=True)


def filter_bank(windowed, tables, signals, weights, shift, det):
    cos_first, sin_first, cos_twist, sin_twist, cos_second, sin_second = tables
    count, rows_used, width = windowed.shape
    pad_rows = 128
    x = jnp.concatenate(
        [windowed, jnp.zeros((count, pad_rows - rows_used, width), windowed.dtype)], axis=1
    )
    tiles = N2 // BLK
    quot = shift // tiles
    scalars = jnp.stack([lax.rem(shift, tiles), det]).astype(jnp.int32)
    doubled_cos = jnp.concatenate([cos_first, cos_first], axis=0)
    doubled_sin = jnp.concatenate([sin_first, sin_first], axis=0)
    cos_rolled = jnp.stack(
        [lax.dynamic_slice_in_dim(doubled_cos, quot + v, N1) for v in range(2)]
    )
    sin_rolled = jnp.stack(
        [lax.dynamic_slice_in_dim(doubled_sin, quot + v, N1) for v in range(2)]
    )
    operands = [
        cos_first[:, :pad_rows], sin_first[:, :pad_rows], cos_twist, sin_twist,
        cos_second, sin_second, cos_first, sin_first, cos_rolled, sin_rolled,
        signals[0], signals[1], weights[0], weights[1],
    ]

    def whole(array):
        nd = array.ndim
        return pl.BlockSpec(array.shape, lambda i, r, nd=nd: (0,) * nd)

    grid_spec = pltpu.PrefetchScalarGridSpec(
        num_scalar_prefetch=1,
        grid=(count,),
        in_specs=[pl.BlockSpec((1, pad_rows, width), lambda i, r: (i, 0, 0))]
        + [pl.BlockSpec(memory_space=pl.ANY)] * 8
        + [whole(a) for a in operands[8:]],
        out_specs=pl.BlockSpec((1, N1, tiles), lambda i, r: (i, 0, 0)),
        scratch_shapes=[
            pltpu.VMEM((N1, N2), jnp.bfloat16),
            pltpu.VMEM((N1, N2), jnp.bfloat16),
            pltpu.VMEM((2, N1, N2 // 2), jnp.float32),
            pltpu.VMEM((2, N1, N2 // 2), jnp.float32),
            pltpu.VMEM((2, N1, N2 // 2), jnp.float32),
        ]
        + [pltpu.VMEM(a.shape, a.dtype) for a in operands[:8]]
        + [pltpu.SemaphoreType.DMA((8,))],
    )
    matmuls = 2 * N1 * pad_rows * N2 + 4 * N1 * N2 * (N2 // 2) + 16 * N1 * (N2 // 2) * N2
    out = pl.pallas_call(
        filter_kernel,
        out_shape=jax.ShapeDtypeStruct((count, N1, tiles), jnp.float32),
        grid_spec=grid_spec,
        compiler_params=pltpu.CompilerParams(vmem_limit_bytes=56 * 1024 * 1024),
        cost_estimate=pl.CostEstimate(
            flops=2 * matmuls * count, transcendentals=0, bytes_accessed=8 * 1024 * 1024
        ),
    )(scalars, x, *operands)
    return out.reshape(count, N1 * tiles)


def shards(strain, inv_asd, templates, chirp_blocks, owner, slide):
    tables = make_tables()
    detector = lax.axis_index("det")
    per_dev = templates.shape[0]
    mine = per_dev // 2
    n_blk = NFFT // BLK
    half_blk = n_blk // 2
    filt_count = lax.axis_size("filt")
    swap = [(0, 1), (1, 0)]
    own_signal = strain.reshape(N1, N2).astype(jnp.bfloat16)
    own_weight = inv_asd.reshape(N2 // 2, N1)
    other_signal = lax.ppermute(own_signal, "det", swap)
    other_weight = lax.ppermute(own_weight, "det", swap)
    samples = jnp.arange(TL, dtype=jnp.int32)
    my_rows = lax.dynamic_slice_in_dim(templates, detector * mine, mine)
    my_blocks = lax.dynamic_slice_in_dim(chirp_blocks, detector * mine, mine)
    windowed = jnp.where(
        samples[None, :] < BLK * my_blocks[:, None], my_rows, jnp.zeros_like(my_rows)
    )
    windowed = windowed.reshape(mine, TL // N2, N2)
    full = filter_bank(
        windowed, tables, (own_signal, other_signal), (own_weight, other_weight),
        slide[0], detector,
    )
    keep = lax.dynamic_slice_in_dim(full, detector * half_blk, half_blk, axis=1)
    give = lax.dynamic_slice_in_dim(full, (1 - detector) * half_blk, half_blk, axis=1)
    got = lax.ppermute(give, "det", swap)
    local = jnp.where(
        detector == 0, jnp.concatenate([keep, got], axis=0), jnp.concatenate([got, keep], axis=0)
    )
    local_max = jnp.max(local, axis=0)
    positions = jnp.arange(per_dev, dtype=jnp.int32)
    slots = jnp.arange(filt_count, dtype=jnp.int32)
    placing = owner[None, :] == slots[:, None]
    source = jnp.sum(jnp.where(placing, positions[None, :], 0), axis=1)
    used = jnp.any(placing, axis=1)
    flagged = jnp.concatenate([local, jnp.ones((per_dev, 128), jnp.float32)], axis=1)
    send_rows = jnp.where(used[:, None], jnp.take(flagged, source, axis=0), 0.0)
    split = half_blk + 128
    send_rows = jnp.concatenate(
        [send_rows, jnp.broadcast_to(local_max[None, :], (filt_count, half_blk))], axis=1
    )
    recv_rows, loudest = route_and_max(send_rows[:, None, :], split)
    recv_rows = recv_rows.reshape(filt_count, split + half_blk)
    valid = recv_rows[:, half_blk] > 0.5
    rank = jnp.cumsum(valid.astype(jnp.int32)) - 1
    hits = jnp.logical_and(valid[None, :], rank[None, :] == positions[:, None])
    pick = jnp.sum(jnp.where(hits, slots[None, :], 0), axis=1)
    peaks = jnp.take(recv_rows[:, :half_blk], pick, axis=0)
    return (peaks, loudest)


def solution(mesh):
    return jax.shard_map(
        shards,
        mesh=mesh,
        in_specs=(
            P("det", None),
            P("det", None),
            P(("grp", "filt"), None),
            P(("grp", "filt")),
            P(("grp", "filt")),
            P("grp"),
        ),
        out_specs=(P(("grp", "filt"), "det"), P("det")),
        check_vma=False,
    )
```

```python
import functools

import jax
import ml_dtypes
import numpy as np
import jax.numpy as jnp
from jax import lax
from jax.experimental import pallas as pl
from jax.experimental.pallas import tpu as pltpu
from jax.sharding import PartitionSpec as P

N1 = 256
N2 = 512
NFFT = 131072
BLK = 128
TL = 4096


TWO_PI = 6.283185307179586


def angle_table(rows, cols, period):
    left = np.arange(rows, dtype=np.int64)[:, None]
    right = np.arange(cols, dtype=np.int64)[None, :]
    turns = (left * right % period).astype(np.float32)
    return np.float32(TWO_PI / period) * turns


def make_tables():
    twist = angle_table(N1, N2, NFFT).astype(np.float64)
    second = angle_table(N2, N2 // 2, N2).astype(np.float64)
    cos_second = np.cos(second).astype(np.float32).astype(ml_dtypes.bfloat16)
    sin_second = np.sin(second).astype(np.float32).astype(ml_dtypes.bfloat16)
    return tuple(
        jnp.asarray(table)
        for table in (
            cos_second[0::2],
            sin_second[0::2],
            np.cos(twist).astype(np.float32),
            np.sin(twist).astype(np.float32),
            cos_second,
            sin_second,
        )
    )


def route_kernel(
    split, send_ref, recv_out, out_ref, recv_buf, slot_send, slot_recv, acc_ref,
    held, grp_send, grp_recv,
):
    det = lax.axis_index("det")
    grp = lax.axis_index("grp")
    filt = lax.axis_index("filt")
    n_grp = lax.axis_size("grp")
    n_filt = send_ref.shape[0]
    mesh_ids = pl.DeviceIdType.MESH
    barrier = pltpu.get_barrier_semaphore()
    for i in range(n_filt - 1):
        target = lax.rem(filt + 1 + i, n_filt)
        pl.semaphore_signal(barrier, inc=1, device_id=(det, grp, target), device_id_type=mesh_ids)
    for i in range(n_grp - 1):
        target = lax.rem(grp + 1 + i, n_grp)
        pl.semaphore_signal(barrier, inc=1, device_id=(det, target, filt), device_id_type=mesh_ids)
    pl.semaphore_wait(barrier, n_filt - 1 + n_grp - 1)
    slots = []
    for i in range(n_filt - 1):
        target = lax.rem(filt + 1 + i, n_filt)
        copy = pltpu.make_async_remote_copy(
            src_ref=send_ref.at[target],
            dst_ref=recv_buf.at[filt],
            send_sem=slot_send.at[i],
            recv_sem=slot_recv.at[filt],
            device_id=(det, grp, target),
            device_id_type=mesh_ids,
        )
        copy.start()
        slots.append(copy)
    for copy in slots:
        copy.wait_send()
    for i in range(n_filt - 1):
        origin = lax.rem(filt + 1 + i, n_filt)
        pltpu.make_async_remote_copy(
            src_ref=send_ref.at[origin],
            dst_ref=recv_buf.at[origin],
            send_sem=slot_send.at[i],
            recv_sem=slot_recv.at[origin],
            device_id=(det, grp, origin),
            device_id_type=mesh_ids,
        ).wait_recv()
    recv_buf[filt] = send_ref[filt]
    rows = recv_buf[...]
    recv_out[...] = rows
    value = jnp.max(rows[:, :, split:], axis=0)
    if n_grp > 1:
        acc_ref[...] = value
        copies = []
        for i in range(n_grp - 1):
            target = lax.rem(grp + 1 + i, n_grp)
            row = n_grp - 2 - i
            copy = pltpu.make_async_remote_copy(
                src_ref=acc_ref,
                dst_ref=held.at[row],
                send_sem=grp_send.at[i],
                recv_sem=grp_recv.at[row],
                device_id=(det, target, filt),
                device_id_type=mesh_ids,
            )
            copy.start()
            copies.append(copy)
        for copy in copies:
            copy.wait_send()
            copy.wait_recv()
        value = jnp.maximum(value, jnp.max(held[...], axis=0))
    out_ref[...] = value


def route_and_max(send_rows, split):
    n_grp = lax.axis_size("grp")
    n_filt = send_rows.shape[0]
    width = send_rows.shape[-1] - split
    vmem = pl.BlockSpec(memory_space=pltpu.VMEM)
    recv, out = pl.pallas_call(
        functools.partial(route_kernel, split),
        out_shape=(
            jax.ShapeDtypeStruct(send_rows.shape, send_rows.dtype),
            jax.ShapeDtypeStruct((1, width), jnp.float32),
        ),
        in_specs=[vmem],
        out_specs=(vmem, vmem),
        scratch_shapes=[
            pltpu.VMEM(send_rows.shape, send_rows.dtype),
            pltpu.SemaphoreType.DMA((n_filt,)),
            pltpu.SemaphoreType.DMA((n_filt,)),
            pltpu.VMEM((1, width), jnp.float32),
            pltpu.VMEM((max(n_grp - 1, 1), 1, width), jnp.float32),
            pltpu.SemaphoreType.DMA((max(n_grp - 1, 1),)),
            pltpu.SemaphoreType.DMA((max(n_grp - 1, 1),)),
        ],
        compiler_params=pltpu.CompilerParams(collective_id=0, has_side_effects=True),
    )(send_rows)
    return recv, out.reshape(width)


def dot_nt(left, right):
    return lax.dot_general(
        left, right, (((1,), (1,)), ((), ())), preferred_element_type=jnp.float32
    )


def filter_kernel(
    scalar_ref, x_ref, cfn_ref, sfn_ref, ct_ref, st_ref, cs_ref, ss_ref, cf_ref, sf_ref,
    sown_ref, soth_ref, wown_ref, woth_ref, out_ref, rho_ref, pr_ref, pi_ref, w2_ref,
):
    f32 = jnp.float32
    bf16 = jnp.bfloat16

    def first_stage(cos_rows, sin_rows, x):
        cos_twist = ct_ref[...]
        sin_twist = st_ref[...]
        real_a = jnp.dot(cos_rows, x, preferred_element_type=f32)
        imag_a = -jnp.dot(sin_rows, x, preferred_element_type=f32)
        real_b = (real_a * cos_twist + imag_a * sin_twist).astype(bf16)
        imag_b = (imag_a * cos_twist - real_a * sin_twist).astype(bf16)
        cos_second = cs_ref[...]
        sin_second = ss_ref[...]
        real_x = jnp.dot(real_b, cos_second, preferred_element_type=f32) + jnp.dot(
            imag_b, sin_second, preferred_element_type=f32
        )
        imag_x = jnp.dot(imag_b, cos_second, preferred_element_type=f32) - jnp.dot(
            real_b, sin_second, preferred_element_type=f32
        )
        return real_x, imag_x

    @pl.when(pl.program_id(0) == 0)
    def _():
        det = scalar_ref[1]
        for slot, sig_ref, w_ref in ((det, sown_ref, wown_ref), (1 - det, soth_ref, woth_ref)):
            real_s, imag_s = first_stage(cf_ref[...], sf_ref[...], sig_ref[...])
            weight = jnp.transpose(w_ref[...])
            pr_ref[slot] = weight * real_s
            pi_ref[slot] = weight * imag_s
            w2_ref[slot] = weight * weight

    temp_real, temp_imag = first_stage(cfn_ref[...], sfn_ref[...], x_ref[0])
    power = temp_real * temp_real + temp_imag * temp_imag
    cos_back = cs_ref[...]
    sin_back = ss_ref[...]

    def back_half(d):
        cos_twist = ct_ref[...]
        sin_twist = st_ref[...]
        sigma = jnp.sum(w2_ref[d] * power, axis=(0, 1), keepdims=True)
        data_real = pr_ref[d]
        data_imag = pi_ref[d]
        q_real = (temp_real * data_real + temp_imag * data_imag).astype(bf16)
        q_imag = (temp_real * data_imag - temp_imag * data_real).astype(bf16)
        d_real = dot_nt(q_real, cos_back) - dot_nt(q_imag, sin_back)
        d_imag = dot_nt(q_real, sin_back) + dot_nt(q_imag, cos_back)
        e_real = (d_real * cos_twist - d_imag * sin_twist).astype(bf16)
        e_imag = (d_real * sin_twist + d_imag * cos_twist).astype(bf16)
        return sigma, e_real, e_imag

    sigma0, e_real, e_imag = back_half(0)
    cos_first = cf_ref[...]
    sin_first = sf_ref[...]
    z_real = jnp.dot(cos_first, e_real, preferred_element_type=f32) - jnp.dot(
        sin_first, e_imag, preferred_element_type=f32
    )
    z_imag = jnp.dot(sin_first, e_real, preferred_element_type=f32) + jnp.dot(
        cos_first, e_imag, preferred_element_type=f32
    )
    first = (z_real * z_real + z_imag * z_imag) / (NFFT * sigma0)
    sigma1, e_real, e_imag = back_half(1)
    z_real = jnp.dot(cos_first, e_real, preferred_element_type=f32) - jnp.dot(
        sin_first, e_imag, preferred_element_type=f32
    )
    z_imag = jnp.dot(sin_first, e_real, preferred_element_type=f32) + jnp.dot(
        cos_first, e_imag, preferred_element_type=f32
    )
    rho_ref[...] = (z_real * z_real + z_imag * z_imag) / (NFFT * sigma1)
    rem = scalar_ref[0]
    quot = scalar_ref[2]
    rows = first.shape[0]
    tiles = first.shape[1] // BLK
    for col in range(tiles):
        src = lax.rem(col + rem, tiles)
        carry = (col + rem) // tiles
        cols = pl.ds(pl.multiple_of(src * BLK, BLK), BLK)
        shift = lax.rem(rows - lax.rem(quot + carry, rows), rows)
        second = pltpu.roll(rho_ref[:, cols], shift, 0)
        network = first[:, col * BLK:(col + 1) * BLK] + second
        out_ref[0, :, col:col + 1] = jnp.max(network, axis=1, keepdims=True)


def filter_bank(windowed, tables, signals, weights, shift, det):
    cos_first, sin_first, cos_twist, sin_twist, cos_second, sin_second = tables
    count, rows_used, width = windowed.shape
    pad_rows = 128
    x = jnp.concatenate(
        [windowed, jnp.zeros((count, pad_rows - rows_used, width), windowed.dtype)], axis=1
    )
    tiles = N2 // BLK
    quot = shift // tiles
    scalars = jnp.stack([lax.rem(shift, tiles), det, quot]).astype(jnp.int32)
    operands = [
        cos_first[:, :pad_rows], sin_first[:, :pad_rows], cos_twist, sin_twist,
        cos_second, sin_second, cos_first, sin_first,
        signals[0], signals[1], weights[0], weights[1],
    ]

    def whole(array):
        nd = array.ndim
        return pl.BlockSpec(array.shape, lambda i, r, nd=nd: (0,) * nd)

    grid_spec = pltpu.PrefetchScalarGridSpec(
        num_scalar_prefetch=1,
        grid=(count,),
        in_specs=[pl.BlockSpec((1, pad_rows, width), lambda i, r: (i, 0, 0))]
        + [whole(a) for a in operands],
        out_specs=pl.BlockSpec((1, N1, tiles), lambda i, r: (i, 0, 0)),
        scratch_shapes=[
            pltpu.VMEM((N1, N2), jnp.float32),
            pltpu.VMEM((2, N1, N2 // 2), jnp.float32),
            pltpu.VMEM((2, N1, N2 // 2), jnp.float32),
            pltpu.VMEM((2, N1, N2 // 2), jnp.float32),
        ],
    )
    matmuls = 2 * N1 * pad_rows * N2 + 4 * N1 * N2 * (N2 // 2) + 16 * N1 * (N2 // 2) * N2
    out = pl.pallas_call(
        filter_kernel,
        out_shape=jax.ShapeDtypeStruct((count, N1, tiles), jnp.float32),
        grid_spec=grid_spec,
        compiler_params=pltpu.CompilerParams(vmem_limit_bytes=48 * 1024 * 1024),
        cost_estimate=pl.CostEstimate(
            flops=2 * matmuls * count, transcendentals=0, bytes_accessed=8 * 1024 * 1024
        ),
    )(scalars, x, *operands)
    return out.reshape(count, N1 * tiles)


def shards(strain, inv_asd, templates, chirp_blocks, owner, slide):
    tables = make_tables()
    detector = lax.axis_index("det")
    per_dev = templates.shape[0]
    mine = per_dev // 2
    n_blk = NFFT // BLK
    half_blk = n_blk // 2
    filt_count = lax.axis_size("filt")
    swap = [(0, 1), (1, 0)]
    own_signal = strain.reshape(N1, N2).astype(jnp.bfloat16)
    own_weight = inv_asd.reshape(N2 // 2, N1)
    other_signal = lax.ppermute(own_signal, "det", swap)
    other_weight = lax.ppermute(own_weight, "det", swap)
    samples = jnp.arange(TL, dtype=jnp.int32)
    my_rows = lax.dynamic_slice_in_dim(templates, detector * mine, mine)
    my_blocks = lax.dynamic_slice_in_dim(chirp_blocks, detector * mine, mine)
    windowed = jnp.where(
        samples[None, :] < BLK * my_blocks[:, None], my_rows, jnp.zeros_like(my_rows)
    )
    windowed = windowed.reshape(mine, TL // N2, N2)
    full = filter_bank(
        windowed, tables, (own_signal, other_signal), (own_weight, other_weight),
        slide[0], detector,
    )
    keep = lax.dynamic_slice_in_dim(full, detector * half_blk, half_blk, axis=1)
    give = lax.dynamic_slice_in_dim(full, (1 - detector) * half_blk, half_blk, axis=1)
    got = lax.ppermute(give, "det", swap)
    local = jnp.where(
        detector == 0, jnp.concatenate([keep, got], axis=0), jnp.concatenate([got, keep], axis=0)
    )
    local_max = jnp.max(local, axis=0)
    positions = jnp.arange(per_dev, dtype=jnp.int32)
    slots = jnp.arange(filt_count, dtype=jnp.int32)
    placing = owner[None, :] == slots[:, None]
    source = jnp.sum(jnp.where(placing, positions[None, :], 0), axis=1)
    used = jnp.any(placing, axis=1)
    flagged = jnp.concatenate([local, jnp.ones((per_dev, 128), jnp.float32)], axis=1)
    send_rows = jnp.where(used[:, None], jnp.take(flagged, source, axis=0), 0.0)
    split = half_blk + 128
    send_rows = jnp.concatenate(
        [send_rows, jnp.broadcast_to(local_max[None, :], (filt_count, half_blk))], axis=1
    )
    recv_rows, loudest = route_and_max(send_rows[:, None, :], split)
    recv_rows = recv_rows.reshape(filt_count, split + half_blk)
    valid = recv_rows[:, half_blk] > 0.5
    rank = jnp.cumsum(valid.astype(jnp.int32)) - 1
    hits = jnp.logical_and(valid[None, :], rank[None, :] == positions[:, None])
    pick = jnp.sum(jnp.where(hits, slots[None, :], 0), axis=1)
    peaks = jnp.take(recv_rows[:, :half_blk], pick, axis=0)
    return (peaks, loudest)


def solution(mesh):
    return jax.shard_map(
        shards,
        mesh=mesh,
        in_specs=(
            P("det", None),
            P("det", None),
            P(("grp", "filt"), None),
            P(("grp", "filt")),
            P(("grp", "filt")),
            P("grp"),
        ),
        out_specs=(P(("grp", "filt"), "det"), P("det")),
        check_vma=False,
    )
```

```python
import functools

import jax
import ml_dtypes
import numpy as np
import jax.numpy as jnp
from jax import lax
from jax.experimental import pallas as pl
from jax.experimental.pallas import tpu as pltpu
from jax.sharding import PartitionSpec as P

N1 = 256
N2 = 512
NFFT = 131072
BLK = 128
TL = 4096


TWO_PI = 6.283185307179586


def angle_table(rows, cols, period):
    left = np.arange(rows, dtype=np.int64)[:, None]
    right = np.arange(cols, dtype=np.int64)[None, :]
    turns = (left * right % period).astype(np.float32)
    return np.float32(TWO_PI / period) * turns


def make_tables():
    twist = angle_table(N1, N2, NFFT).astype(np.float64)
    second = angle_table(N2, N2 // 2, N2).astype(np.float64)
    cos_second = np.cos(second).astype(np.float32).astype(ml_dtypes.bfloat16)
    sin_second = np.sin(second).astype(np.float32).astype(ml_dtypes.bfloat16)
    return tuple(
        jnp.asarray(table)
        for table in (
            cos_second[0::2],
            sin_second[0::2],
            np.cos(twist).astype(np.float32),
            np.sin(twist).astype(np.float32),
            cos_second,
            sin_second,
        )
    )


def route_kernel(
    split, send_ref, recv_out, out_ref, recv_buf, slot_send, slot_recv, acc_ref,
    held, grp_send, grp_recv,
):
    det = lax.axis_index("det")
    grp = lax.axis_index("grp")
    filt = lax.axis_index("filt")
    n_grp = lax.axis_size("grp")
    n_filt = send_ref.shape[0]
    mesh_ids = pl.DeviceIdType.MESH
    barrier = pltpu.get_barrier_semaphore()
    for i in range(n_filt - 1):
        target = lax.rem(filt + 1 + i, n_filt)
        pl.semaphore_signal(barrier, inc=1, device_id=(det, grp, target), device_id_type=mesh_ids)
    for i in range(n_grp - 1):
        target = lax.rem(grp + 1 + i, n_grp)
        pl.semaphore_signal(barrier, inc=1, device_id=(det, target, filt), device_id_type=mesh_ids)
    pl.semaphore_wait(barrier, n_filt - 1 + n_grp - 1)
    slots = []
    for i in range(n_filt - 1):
        target = lax.rem(filt + 1 + i, n_filt)
        copy = pltpu.make_async_remote_copy(
            src_ref=send_ref.at[target],
            dst_ref=recv_buf.at[filt],
            send_sem=slot_send.at[i],
            recv_sem=slot_recv.at[filt],
            device_id=(det, grp, target),
            device_id_type=mesh_ids,
        )
        copy.start()
        slots.append(copy)
    for copy in slots:
        copy.wait_send()
    for i in range(n_filt - 1):
        origin = lax.rem(filt + 1 + i, n_filt)
        pltpu.make_async_remote_copy(
            src_ref=send_ref.at[origin],
            dst_ref=recv_buf.at[origin],
            send_sem=slot_send.at[i],
            recv_sem=slot_recv.at[origin],
            device_id=(det, grp, origin),
            device_id_type=mesh_ids,
        ).wait_recv()
    recv_buf[filt] = send_ref[filt]
    rows = recv_buf[...]
    recv_out[...] = rows
    value = jnp.max(rows[:, :, split:], axis=0)
    if n_grp > 1:
        acc_ref[...] = value
        copies = []
        for i in range(n_grp - 1):
            target = lax.rem(grp + 1 + i, n_grp)
            row = n_grp - 2 - i
            copy = pltpu.make_async_remote_copy(
                src_ref=acc_ref,
                dst_ref=held.at[row],
                send_sem=grp_send.at[i],
                recv_sem=grp_recv.at[row],
                device_id=(det, target, filt),
                device_id_type=mesh_ids,
            )
            copy.start()
            copies.append(copy)
        for copy in copies:
            copy.wait_send()
            copy.wait_recv()
        value = jnp.maximum(value, jnp.max(held[...], axis=0))
    out_ref[...] = value


def route_and_max(send_rows, split):
    n_grp = lax.axis_size("grp")
    n_filt = send_rows.shape[0]
    width = send_rows.shape[-1] - split
    vmem = pl.BlockSpec(memory_space=pltpu.VMEM)
    recv, out = pl.pallas_call(
        functools.partial(route_kernel, split),
        out_shape=(
            jax.ShapeDtypeStruct(send_rows.shape, send_rows.dtype),
            jax.ShapeDtypeStruct((1, width), jnp.float32),
        ),
        in_specs=[vmem],
        out_specs=(vmem, vmem),
        scratch_shapes=[
            pltpu.VMEM(send_rows.shape, send_rows.dtype),
            pltpu.SemaphoreType.DMA((n_filt,)),
            pltpu.SemaphoreType.DMA((n_filt,)),
            pltpu.VMEM((1, width), jnp.float32),
            pltpu.VMEM((max(n_grp - 1, 1), 1, width), jnp.float32),
            pltpu.SemaphoreType.DMA((max(n_grp - 1, 1),)),
            pltpu.SemaphoreType.DMA((max(n_grp - 1, 1),)),
        ],
        compiler_params=pltpu.CompilerParams(collective_id=0, has_side_effects=True),
    )(send_rows)
    return recv, out.reshape(width)


def dot_nt(left, right):
    return lax.dot_general(
        left, right, (((1,), (1,)), ((), ())), preferred_element_type=jnp.float32
    )


def filter_kernel(
    scalar_ref, x_ref, ct_ref, st_ref, cs_ref, ss_ref, cf_ref, sf_ref,
    sown_ref, soth_ref, wown_ref, woth_ref, out_ref, rho_ref, pr_ref, pi_ref, w2_ref,
):
    f32 = jnp.float32
    bf16 = jnp.bfloat16

    def first_stage(cos_rows, sin_rows, x):
        cos_twist = ct_ref[...]
        sin_twist = st_ref[...]
        real_a = jnp.dot(cos_rows, x, preferred_element_type=f32)
        imag_a = -jnp.dot(sin_rows, x, preferred_element_type=f32)
        real_b = (real_a * cos_twist + imag_a * sin_twist).astype(bf16)
        imag_b = (imag_a * cos_twist - real_a * sin_twist).astype(bf16)
        cos_second = cs_ref[...]
        sin_second = ss_ref[...]
        real_x = jnp.dot(real_b, cos_second, preferred_element_type=f32) + jnp.dot(
            imag_b, sin_second, preferred_element_type=f32
        )
        imag_x = jnp.dot(imag_b, cos_second, preferred_element_type=f32) - jnp.dot(
            real_b, sin_second, preferred_element_type=f32
        )
        return real_x, imag_x

    @pl.when(pl.program_id(0) == 0)
    def _():
        det = scalar_ref[1]
        for slot, sig_ref, w_ref in ((det, sown_ref, wown_ref), (1 - det, soth_ref, woth_ref)):
            real_s, imag_s = first_stage(cf_ref[...], sf_ref[...], sig_ref[...])
            weight = jnp.transpose(w_ref[...])
            pr_ref[slot] = weight * real_s
            pi_ref[slot] = weight * imag_s
            w2_ref[slot] = weight * weight

    used = x_ref.shape[1]
    temp_real, temp_imag = first_stage(cf_ref[:, :used], sf_ref[:, :used], x_ref[0])
    power = temp_real * temp_real + temp_imag * temp_imag
    cos_back = cs_ref[...]
    sin_back = ss_ref[...]

    def back_half(d):
        cos_twist = ct_ref[...]
        sin_twist = st_ref[...]
        sigma = jnp.sum(w2_ref[d] * power, axis=(0, 1), keepdims=True)
        data_real = pr_ref[d]
        data_imag = pi_ref[d]
        q_real = (temp_real * data_real + temp_imag * data_imag).astype(bf16)
        q_imag = (temp_real * data_imag - temp_imag * data_real).astype(bf16)
        d_real = dot_nt(q_real, cos_back) - dot_nt(q_imag, sin_back)
        d_imag = dot_nt(q_real, sin_back) + dot_nt(q_imag, cos_back)
        e_real = (d_real * cos_twist - d_imag * sin_twist).astype(bf16)
        e_imag = (d_real * sin_twist + d_imag * cos_twist).astype(bf16)
        return sigma, e_real, e_imag

    sigma0, e_real, e_imag = back_half(0)
    cos_first = cf_ref[...]
    sin_first = sf_ref[...]
    z_real = jnp.dot(cos_first, e_real, preferred_element_type=f32) - jnp.dot(
        sin_first, e_imag, preferred_element_type=f32
    )
    z_imag = jnp.dot(sin_first, e_real, preferred_element_type=f32) + jnp.dot(
        cos_first, e_imag, preferred_element_type=f32
    )
    first = (z_real * z_real + z_imag * z_imag) / (NFFT * sigma0)
    sigma1, e_real, e_imag = back_half(1)
    z_real = jnp.dot(cos_first, e_real, preferred_element_type=f32) - jnp.dot(
        sin_first, e_imag, preferred_element_type=f32
    )
    z_imag = jnp.dot(sin_first, e_real, preferred_element_type=f32) + jnp.dot(
        cos_first, e_imag, preferred_element_type=f32
    )
    rho_ref[...] = (z_real * z_real + z_imag * z_imag) / (NFFT * sigma1)
    rem = scalar_ref[0]
    quot = scalar_ref[2]
    rows = first.shape[0]
    tiles = first.shape[1] // BLK
    for col in range(tiles):
        src = lax.rem(col + rem, tiles)
        carry = (col + rem) // tiles
        cols = pl.ds(pl.multiple_of(src * BLK, BLK), BLK)
        shift = lax.rem(rows - lax.rem(quot + carry, rows), rows)
        second = pltpu.roll(rho_ref[:, cols], shift, 0)
        network = first[:, col * BLK:(col + 1) * BLK] + second
        out_ref[0, :, col:col + 1] = jnp.max(network, axis=1, keepdims=True)


def filter_bank(windowed, tables, signals, weights, shift, det):
    cos_first, sin_first, cos_twist, sin_twist, cos_second, sin_second = tables
    count, rows_used, width = windowed.shape
    pad_rows = 128
    x = jnp.concatenate(
        [windowed, jnp.zeros((count, pad_rows - rows_used, width), windowed.dtype)], axis=1
    )
    tiles = N2 // BLK
    quot = shift // tiles
    scalars = jnp.stack([lax.rem(shift, tiles), det, quot]).astype(jnp.int32)
    operands = [
        cos_twist, sin_twist,
        cos_second, sin_second, cos_first, sin_first,
        signals[0], signals[1], weights[0], weights[1],
    ]

    def whole(array):
        nd = array.ndim
        return pl.BlockSpec(array.shape, lambda i, r, nd=nd: (0,) * nd)

    grid_spec = pltpu.PrefetchScalarGridSpec(
        num_scalar_prefetch=1,
        grid=(count,),
        in_specs=[pl.BlockSpec((1, pad_rows, width), lambda i, r: (i, 0, 0))]
        + [whole(a) for a in operands],
        out_specs=pl.BlockSpec((1, N1, tiles), lambda i, r: (i, 0, 0)),
        scratch_shapes=[
            pltpu.VMEM((N1, N2), jnp.float32),
            pltpu.VMEM((2, N1, N2 // 2), jnp.float32),
            pltpu.VMEM((2, N1, N2 // 2), jnp.float32),
            pltpu.VMEM((2, N1, N2 // 2), jnp.float32),
        ],
    )
    matmuls = 2 * N1 * pad_rows * N2 + 4 * N1 * N2 * (N2 // 2) + 16 * N1 * (N2 // 2) * N2
    out = pl.pallas_call(
        filter_kernel,
        out_shape=jax.ShapeDtypeStruct((count, N1, tiles), jnp.float32),
        grid_spec=grid_spec,
        compiler_params=pltpu.CompilerParams(vmem_limit_bytes=48 * 1024 * 1024),
        cost_estimate=pl.CostEstimate(
            flops=2 * matmuls * count, transcendentals=0, bytes_accessed=8 * 1024 * 1024
        ),
    )(scalars, x, *operands)
    return out.reshape(count, N1 * tiles)


def shards(strain, inv_asd, templates, chirp_blocks, owner, slide):
    tables = make_tables()
    detector = lax.axis_index("det")
    per_dev = templates.shape[0]
    mine = per_dev // 2
    n_blk = NFFT // BLK
    half_blk = n_blk // 2
    filt_count = lax.axis_size("filt")
    swap = [(0, 1), (1, 0)]
    own_signal = strain.reshape(N1, N2).astype(jnp.bfloat16)
    own_weight = inv_asd.reshape(N2 // 2, N1)
    other_signal = lax.ppermute(own_signal, "det", swap)
    other_weight = lax.ppermute(own_weight, "det", swap)
    samples = jnp.arange(TL, dtype=jnp.int32)
    my_rows = lax.dynamic_slice_in_dim(templates, detector * mine, mine)
    my_blocks = lax.dynamic_slice_in_dim(chirp_blocks, detector * mine, mine)
    windowed = jnp.where(
        samples[None, :] < BLK * my_blocks[:, None], my_rows, jnp.zeros_like(my_rows)
    )
    windowed = windowed.reshape(mine, TL // N2, N2)
    full = filter_bank(
        windowed, tables, (own_signal, other_signal), (own_weight, other_weight),
        slide[0], detector,
    )
    keep = lax.dynamic_slice_in_dim(full, detector * half_blk, half_blk, axis=1)
    give = lax.dynamic_slice_in_dim(full, (1 - detector) * half_blk, half_blk, axis=1)
    got = lax.ppermute(give, "det", swap)
    local = jnp.where(
        detector == 0, jnp.concatenate([keep, got], axis=0), jnp.concatenate([got, keep], axis=0)
    )
    local_max = jnp.max(local, axis=0)
    positions = jnp.arange(per_dev, dtype=jnp.int32)
    slots = jnp.arange(filt_count, dtype=jnp.int32)
    placing = owner[None, :] == slots[:, None]
    source = jnp.sum(jnp.where(placing, positions[None, :], 0), axis=1)
    used = jnp.any(placing, axis=1)
    flagged = jnp.concatenate([local, jnp.ones((per_dev, 128), jnp.float32)], axis=1)
    send_rows = jnp.where(used[:, None], jnp.take(flagged, source, axis=0), 0.0)
    split = half_blk + 128
    send_rows = jnp.concatenate(
        [send_rows, jnp.broadcast_to(local_max[None, :], (filt_count, half_blk))], axis=1
    )
    recv_rows, loudest = route_and_max(send_rows[:, None, :], split)
    recv_rows = recv_rows.reshape(filt_count, split + half_blk)
    valid = recv_rows[:, half_blk] > 0.5
    rank = jnp.cumsum(valid.astype(jnp.int32)) - 1
    hits = jnp.logical_and(valid[None, :], rank[None, :] == positions[:, None])
    pick = jnp.sum(jnp.where(hits, slots[None, :], 0), axis=1)
    peaks = jnp.take(recv_rows[:, :half_blk], pick, axis=0)
    return (peaks, loudest)


def solution(mesh):
    return jax.shard_map(
        shards,
        mesh=mesh,
        in_specs=(
            P("det", None),
            P("det", None),
            P(("grp", "filt"), None),
            P(("grp", "filt")),
            P(("grp", "filt")),
            P("grp"),
        ),
        out_specs=(P(("grp", "filt"), "det"), P("det")),
        check_vma=False,
    )
```

```python
import functools

import jax
import ml_dtypes
import numpy as np
import jax.numpy as jnp
from jax import lax
from jax.experimental import pallas as pl
from jax.experimental.pallas import tpu as pltpu
from jax.sharding import PartitionSpec as P

N1 = 256
N2 = 512
NFFT = 131072
BLK = 128
TL = 4096


TWO_PI = 6.283185307179586


def angle_table(rows, cols, period):
    left = np.arange(rows, dtype=np.int64)[:, None]
    right = np.arange(cols, dtype=np.int64)[None, :]
    turns = (left * right % period).astype(np.float32)
    return np.float32(TWO_PI / period) * turns


def make_tables():
    twist = angle_table(N1, N2, NFFT).astype(np.float64)
    second = angle_table(N2, N2 // 2, N2).astype(np.float64)
    cos_second = np.cos(second).astype(np.float32).astype(ml_dtypes.bfloat16)
    sin_second = np.sin(second).astype(np.float32).astype(ml_dtypes.bfloat16)
    return tuple(
        jnp.asarray(table)
        for table in (
            cos_second[0::2],
            sin_second[0::2],
            np.cos(twist).astype(np.float32),
            np.sin(twist).astype(np.float32),
            cos_second,
            sin_second,
        )
    )


def route_kernel(
    split, send_ref, recv_out, out_ref, recv_buf, slot_send, slot_recv, acc_ref,
    held, grp_send, grp_recv,
):
    det = lax.axis_index("det")
    grp = lax.axis_index("grp")
    filt = lax.axis_index("filt")
    n_grp = lax.axis_size("grp")
    n_filt = send_ref.shape[0]
    mesh_ids = pl.DeviceIdType.MESH
    barrier = pltpu.get_barrier_semaphore()
    for i in range(n_filt - 1):
        target = lax.rem(filt + 1 + i, n_filt)
        pl.semaphore_signal(barrier, inc=1, device_id=(det, grp, target), device_id_type=mesh_ids)
    for i in range(n_grp - 1):
        target = lax.rem(grp + 1 + i, n_grp)
        pl.semaphore_signal(barrier, inc=1, device_id=(det, target, filt), device_id_type=mesh_ids)
    pl.semaphore_wait(barrier, n_filt - 1 + n_grp - 1)
    slots = []
    for i in range(n_filt - 1):
        target = lax.rem(filt + 1 + i, n_filt)
        copy = pltpu.make_async_remote_copy(
            src_ref=send_ref.at[target],
            dst_ref=recv_buf.at[filt],
            send_sem=slot_send.at[i],
            recv_sem=slot_recv.at[filt],
            device_id=(det, grp, target),
            device_id_type=mesh_ids,
        )
        copy.start()
        slots.append(copy)
    for copy in slots:
        copy.wait_send()
    for i in range(n_filt - 1):
        origin = lax.rem(filt + 1 + i, n_filt)
        pltpu.make_async_remote_copy(
            src_ref=send_ref.at[origin],
            dst_ref=recv_buf.at[origin],
            send_sem=slot_send.at[i],
            recv_sem=slot_recv.at[origin],
            device_id=(det, grp, origin),
            device_id_type=mesh_ids,
        ).wait_recv()
    recv_buf[filt] = send_ref[filt]
    rows = recv_buf[...]
    recv_out[...] = rows
    value = jnp.max(rows[:, :, split:], axis=0)
    if n_grp > 1:
        acc_ref[...] = value
        copies = []
        for i in range(n_grp - 1):
            target = lax.rem(grp + 1 + i, n_grp)
            row = n_grp - 2 - i
            copy = pltpu.make_async_remote_copy(
                src_ref=acc_ref,
                dst_ref=held.at[row],
                send_sem=grp_send.at[i],
                recv_sem=grp_recv.at[row],
                device_id=(det, target, filt),
                device_id_type=mesh_ids,
            )
            copy.start()
            copies.append(copy)
        for copy in copies:
            copy.wait_send()
            copy.wait_recv()
        value = jnp.maximum(value, jnp.max(held[...], axis=0))
    out_ref[...] = value


def route_and_max(send_rows, split):
    n_grp = lax.axis_size("grp")
    n_filt = send_rows.shape[0]
    width = send_rows.shape[-1] - split
    vmem = pl.BlockSpec(memory_space=pltpu.VMEM)
    recv, out = pl.pallas_call(
        functools.partial(route_kernel, split),
        out_shape=(
            jax.ShapeDtypeStruct(send_rows.shape, send_rows.dtype),
            jax.ShapeDtypeStruct((1, width), jnp.float32),
        ),
        in_specs=[vmem],
        out_specs=(vmem, vmem),
        scratch_shapes=[
            pltpu.VMEM(send_rows.shape, send_rows.dtype),
            pltpu.SemaphoreType.DMA((n_filt,)),
            pltpu.SemaphoreType.DMA((n_filt,)),
            pltpu.VMEM((1, width), jnp.float32),
            pltpu.VMEM((max(n_grp - 1, 1), 1, width), jnp.float32),
            pltpu.SemaphoreType.DMA((max(n_grp - 1, 1),)),
            pltpu.SemaphoreType.DMA((max(n_grp - 1, 1),)),
        ],
        compiler_params=pltpu.CompilerParams(collective_id=0, has_side_effects=True),
    )(send_rows)
    return recv, out.reshape(width)


def dot_nt(left, right):
    return lax.dot_general(
        left, right, (((1,), (1,)), ((), ())), preferred_element_type=jnp.float32
    )


def filter_kernel(
    scalar_ref, x_ref, ct_ref, st_ref, cs_ref, ss_ref, cf_ref, sf_ref,
    sown_ref, soth_ref, wown_ref, woth_ref, out_ref, rho_ref, pr_ref, pi_ref, w2_ref,
):
    f32 = jnp.float32
    bf16 = jnp.bfloat16

    def first_stage(cos_rows, sin_rows, x):
        cos_twist = ct_ref[...]
        sin_twist = st_ref[...]
        real_a = jnp.dot(cos_rows, x, preferred_element_type=f32)
        imag_a = -jnp.dot(sin_rows, x, preferred_element_type=f32)
        real_b = (real_a * cos_twist + imag_a * sin_twist).astype(bf16)
        imag_b = (imag_a * cos_twist - real_a * sin_twist).astype(bf16)
        cos_second = cs_ref[...]
        sin_second = ss_ref[...]
        real_x = jnp.dot(real_b, cos_second, preferred_element_type=f32) + jnp.dot(
            imag_b, sin_second, preferred_element_type=f32
        )
        imag_x = jnp.dot(imag_b, cos_second, preferred_element_type=f32) - jnp.dot(
            real_b, sin_second, preferred_element_type=f32
        )
        return real_x, imag_x

    @pl.when(pl.program_id(0) == 0)
    def _():
        det = scalar_ref[1]
        for slot, sig_ref, w_ref in ((det, sown_ref, wown_ref), (1 - det, soth_ref, woth_ref)):
            rows = sig_ref.shape[0] // (N2 // BLK)
            signal = jnp.concatenate(
                [sig_ref[pl.ds(c, rows, stride=N2 // BLK), :] for c in range(N2 // BLK)], axis=1
            ).astype(bf16)
            real_s, imag_s = first_stage(cf_ref[...], sf_ref[...], signal)
            halves = N1 // BLK
            raw = jnp.concatenate(
                [w_ref[pl.ds(h, N2 // 2, stride=halves), :] for h in range(halves)], axis=1
            )
            weight = jnp.transpose(raw)
            pr_ref[slot] = weight * real_s
            pi_ref[slot] = weight * imag_s
            w2_ref[slot] = weight * weight

    used = x_ref.shape[1]
    temp_real, temp_imag = first_stage(cf_ref[:, :used], sf_ref[:, :used], x_ref[0])
    power = temp_real * temp_real + temp_imag * temp_imag
    cos_back = cs_ref[...]
    sin_back = ss_ref[...]

    def back_half(d):
        cos_twist = ct_ref[...]
        sin_twist = st_ref[...]
        sigma = jnp.sum(w2_ref[d] * power, axis=(0, 1), keepdims=True)
        data_real = pr_ref[d]
        data_imag = pi_ref[d]
        q_real = (temp_real * data_real + temp_imag * data_imag).astype(bf16)
        q_imag = (temp_real * data_imag - temp_imag * data_real).astype(bf16)
        d_real = dot_nt(q_real, cos_back) - dot_nt(q_imag, sin_back)
        d_imag = dot_nt(q_real, sin_back) + dot_nt(q_imag, cos_back)
        e_real = (d_real * cos_twist - d_imag * sin_twist).astype(bf16)
        e_imag = (d_real * sin_twist + d_imag * cos_twist).astype(bf16)
        return sigma, e_real, e_imag

    sigma0, e_real, e_imag = back_half(0)
    cos_first = cf_ref[...]
    sin_first = sf_ref[...]
    z_real = jnp.dot(cos_first, e_real, preferred_element_type=f32) - jnp.dot(
        sin_first, e_imag, preferred_element_type=f32
    )
    z_imag = jnp.dot(sin_first, e_real, preferred_element_type=f32) + jnp.dot(
        cos_first, e_imag, preferred_element_type=f32
    )
    first = (z_real * z_real + z_imag * z_imag) / (NFFT * sigma0)
    sigma1, e_real, e_imag = back_half(1)
    z_real = jnp.dot(cos_first, e_real, preferred_element_type=f32) - jnp.dot(
        sin_first, e_imag, preferred_element_type=f32
    )
    z_imag = jnp.dot(sin_first, e_real, preferred_element_type=f32) + jnp.dot(
        cos_first, e_imag, preferred_element_type=f32
    )
    rho_ref[...] = (z_real * z_real + z_imag * z_imag) / (NFFT * sigma1)
    rem = scalar_ref[0]
    quot = scalar_ref[2]
    rows = first.shape[0]
    tiles = first.shape[1] // BLK
    for col in range(tiles):
        src = lax.rem(col + rem, tiles)
        carry = (col + rem) // tiles
        cols = pl.ds(pl.multiple_of(src * BLK, BLK), BLK)
        shift = lax.rem(rows - lax.rem(quot + carry, rows), rows)
        second = pltpu.roll(rho_ref[:, cols], shift, 0)
        network = first[:, col * BLK:(col + 1) * BLK] + second
        out_ref[0, :, col:col + 1] = jnp.max(network, axis=1, keepdims=True)


def filter_bank(windowed, tables, signals, weights, shift, det):
    cos_first, sin_first, cos_twist, sin_twist, cos_second, sin_second = tables
    count, rows_used, width = windowed.shape
    pad_rows = 128
    x = jnp.concatenate(
        [windowed, jnp.zeros((count, pad_rows - rows_used, width), windowed.dtype)], axis=1
    )
    tiles = N2 // BLK
    quot = shift // tiles
    scalars = jnp.stack([lax.rem(shift, tiles), det, quot]).astype(jnp.int32)
    operands = [
        cos_twist, sin_twist,
        cos_second, sin_second, cos_first, sin_first,
        signals[0], signals[1], weights[0], weights[1],
    ]

    def whole(array):
        nd = array.ndim
        return pl.BlockSpec(array.shape, lambda i, r, nd=nd: (0,) * nd)

    grid_spec = pltpu.PrefetchScalarGridSpec(
        num_scalar_prefetch=1,
        grid=(count,),
        in_specs=[pl.BlockSpec((1, pad_rows, width), lambda i, r: (i, 0, 0))]
        + [whole(a) for a in operands],
        out_specs=pl.BlockSpec((1, N1, tiles), lambda i, r: (i, 0, 0)),
        scratch_shapes=[
            pltpu.VMEM((N1, N2), jnp.float32),
            pltpu.VMEM((2, N1, N2 // 2), jnp.float32),
            pltpu.VMEM((2, N1, N2 // 2), jnp.float32),
            pltpu.VMEM((2, N1, N2 // 2), jnp.float32),
        ],
    )
    matmuls = 2 * N1 * pad_rows * N2 + 4 * N1 * N2 * (N2 // 2) + 16 * N1 * (N2 // 2) * N2
    out = pl.pallas_call(
        filter_kernel,
        out_shape=jax.ShapeDtypeStruct((count, N1, tiles), jnp.float32),
        grid_spec=grid_spec,
        compiler_params=pltpu.CompilerParams(vmem_limit_bytes=48 * 1024 * 1024),
        cost_estimate=pl.CostEstimate(
            flops=2 * matmuls * count, transcendentals=0, bytes_accessed=8 * 1024 * 1024
        ),
    )(scalars, x, *operands)
    return out.reshape(count, N1 * tiles)


def shards(strain, inv_asd, templates, chirp_blocks, owner, slide):
    tables = make_tables()
    detector = lax.axis_index("det")
    per_dev = templates.shape[0]
    mine = per_dev // 2
    n_blk = NFFT // BLK
    half_blk = n_blk // 2
    filt_count = lax.axis_size("filt")
    swap = [(0, 1), (1, 0)]
    own_signal = strain.reshape(-1, BLK)
    own_weight = inv_asd.reshape(-1, BLK)
    other_signal = lax.ppermute(own_signal, "det", swap)
    other_weight = lax.ppermute(own_weight, "det", swap)
    samples = jnp.arange(TL, dtype=jnp.int32)
    my_rows = lax.dynamic_slice_in_dim(templates, detector * mine, mine)
    my_blocks = lax.dynamic_slice_in_dim(chirp_blocks, detector * mine, mine)
    windowed = jnp.where(
        samples[None, :] < BLK * my_blocks[:, None], my_rows, jnp.zeros_like(my_rows)
    )
    windowed = windowed.reshape(mine, TL // N2, N2)
    full = filter_bank(
        windowed, tables, (own_signal, other_signal), (own_weight, other_weight),
        slide[0], detector,
    )
    keep = lax.dynamic_slice_in_dim(full, detector * half_blk, half_blk, axis=1)
    give = lax.dynamic_slice_in_dim(full, (1 - detector) * half_blk, half_blk, axis=1)
    got = lax.ppermute(give, "det", swap)
    local = jnp.where(
        detector == 0, jnp.concatenate([keep, got], axis=0), jnp.concatenate([got, keep], axis=0)
    )
    local_max = jnp.max(local, axis=0)
    positions = jnp.arange(per_dev, dtype=jnp.int32)
    slots = jnp.arange(filt_count, dtype=jnp.int32)
    placing = owner[None, :] == slots[:, None]
    source = jnp.sum(jnp.where(placing, positions[None, :], 0), axis=1)
    used = jnp.any(placing, axis=1)
    flagged = jnp.concatenate([local, jnp.ones((per_dev, 128), jnp.float32)], axis=1)
    send_rows = jnp.where(used[:, None], jnp.take(flagged, source, axis=0), 0.0)
    split = half_blk + 128
    send_rows = jnp.concatenate(
        [send_rows, jnp.broadcast_to(local_max[None, :], (filt_count, half_blk))], axis=1
    )
    recv_rows, loudest = route_and_max(send_rows[:, None, :], split)
    recv_rows = recv_rows.reshape(filt_count, split + half_blk)
    valid = recv_rows[:, half_blk] > 0.5
    rank = jnp.cumsum(valid.astype(jnp.int32)) - 1
    hits = jnp.logical_and(valid[None, :], rank[None, :] == positions[:, None])
    pick = jnp.sum(jnp.where(hits, slots[None, :], 0), axis=1)
    peaks = jnp.take(recv_rows[:, :half_blk], pick, axis=0)
    return (peaks, loudest)


def solution(mesh):
    return jax.shard_map(
        shards,
        mesh=mesh,
        in_specs=(
            P("det", None),
            P("det", None),
            P(("grp", "filt"), None),
            P(("grp", "filt")),
            P(("grp", "filt")),
            P("grp"),
        ),
        out_specs=(P(("grp", "filt"), "det"), P("det")),
        check_vma=False,
    )
```

```python
import functools

import jax
import ml_dtypes
import numpy as np
import jax.numpy as jnp
from jax import lax
from jax.experimental import pallas as pl
from jax.experimental.pallas import tpu as pltpu
from jax.sharding import PartitionSpec as P

N1 = 256
N2 = 512
NFFT = 131072
BLK = 128
TL = 4096


TWO_PI = 6.283185307179586


def angle_table(rows, cols, period):
    left = np.arange(rows, dtype=np.int64)[:, None]
    right = np.arange(cols, dtype=np.int64)[None, :]
    turns = (left * right % period).astype(np.float32)
    return np.float32(TWO_PI / period) * turns


def make_tables():
    twist = angle_table(N1, N2, NFFT).astype(np.float64)
    second = angle_table(N2, N2 // 2, N2).astype(np.float64)
    cos_second = np.cos(second).astype(np.float32).astype(ml_dtypes.bfloat16)
    sin_second = np.sin(second).astype(np.float32).astype(ml_dtypes.bfloat16)
    return tuple(
        jnp.asarray(table)
        for table in (
            cos_second[0::2],
            sin_second[0::2],
            np.cos(twist).astype(np.float32),
            np.sin(twist).astype(np.float32),
            cos_second,
            sin_second,
        )
    )


def route_kernel(
    split, send_ref, recv_out, out_ref, recv_buf, slot_send, slot_recv, acc_ref,
    held, grp_send, grp_recv,
):
    det = lax.axis_index("det")
    grp = lax.axis_index("grp")
    filt = lax.axis_index("filt")
    n_grp = lax.axis_size("grp")
    n_filt = send_ref.shape[0]
    mesh_ids = pl.DeviceIdType.MESH
    barrier = pltpu.get_barrier_semaphore()
    for i in range(n_filt - 1):
        target = lax.rem(filt + 1 + i, n_filt)
        pl.semaphore_signal(barrier, inc=1, device_id=(det, grp, target), device_id_type=mesh_ids)
    for i in range(n_grp - 1):
        target = lax.rem(grp + 1 + i, n_grp)
        pl.semaphore_signal(barrier, inc=1, device_id=(det, target, filt), device_id_type=mesh_ids)
    pl.semaphore_wait(barrier, n_filt - 1 + n_grp - 1)
    slots = []
    for i in range(n_filt - 1):
        target = lax.rem(filt + 1 + i, n_filt)
        copy = pltpu.make_async_remote_copy(
            src_ref=send_ref.at[target],
            dst_ref=recv_buf.at[filt],
            send_sem=slot_send.at[i],
            recv_sem=slot_recv.at[filt],
            device_id=(det, grp, target),
            device_id_type=mesh_ids,
        )
        copy.start()
        slots.append(copy)
    for copy in slots:
        copy.wait_send()
    for i in range(n_filt - 1):
        origin = lax.rem(filt + 1 + i, n_filt)
        pltpu.make_async_remote_copy(
            src_ref=send_ref.at[origin],
            dst_ref=recv_buf.at[origin],
            send_sem=slot_send.at[i],
            recv_sem=slot_recv.at[origin],
            device_id=(det, grp, origin),
            device_id_type=mesh_ids,
        ).wait_recv()
    recv_buf[filt] = send_ref[filt]
    rows = recv_buf[...]
    recv_out[...] = rows[:, :, :split]
    value = jnp.max(rows[:, :, split:], axis=0)
    if n_grp > 1:
        acc_ref[...] = value
        copies = []
        for i in range(n_grp - 1):
            target = lax.rem(grp + 1 + i, n_grp)
            row = n_grp - 2 - i
            copy = pltpu.make_async_remote_copy(
                src_ref=acc_ref,
                dst_ref=held.at[row],
                send_sem=grp_send.at[i],
                recv_sem=grp_recv.at[row],
                device_id=(det, target, filt),
                device_id_type=mesh_ids,
            )
            copy.start()
            copies.append(copy)
        for copy in copies:
            copy.wait_send()
            copy.wait_recv()
        value = jnp.maximum(value, jnp.max(held[...], axis=0))
    out_ref[...] = value


def route_and_max(send_rows, split):
    n_grp = lax.axis_size("grp")
    n_filt = send_rows.shape[0]
    width = send_rows.shape[-1] - split
    vmem = pl.BlockSpec(memory_space=pltpu.VMEM)
    recv, out = pl.pallas_call(
        functools.partial(route_kernel, split),
        out_shape=(
            jax.ShapeDtypeStruct((n_filt, 1, split), send_rows.dtype),
            jax.ShapeDtypeStruct((1, width), jnp.float32),
        ),
        in_specs=[vmem],
        out_specs=(vmem, vmem),
        scratch_shapes=[
            pltpu.VMEM(send_rows.shape, send_rows.dtype),
            pltpu.SemaphoreType.DMA((n_filt,)),
            pltpu.SemaphoreType.DMA((n_filt,)),
            pltpu.VMEM((1, width), jnp.float32),
            pltpu.VMEM((max(n_grp - 1, 1), 1, width), jnp.float32),
            pltpu.SemaphoreType.DMA((max(n_grp - 1, 1),)),
            pltpu.SemaphoreType.DMA((max(n_grp - 1, 1),)),
        ],
        compiler_params=pltpu.CompilerParams(collective_id=0, has_side_effects=True),
    )(send_rows)
    return recv, out.reshape(width)


def dot_nt(left, right):
    return lax.dot_general(
        left, right, (((1,), (1,)), ((), ())), preferred_element_type=jnp.float32
    )


def filter_kernel(
    scalar_ref, x_ref, ct_ref, st_ref, cs_ref, ss_ref, cf_ref, sf_ref,
    sown_ref, soth_ref, wown_ref, woth_ref, out_ref, rho_ref, pr_ref, pi_ref, w2_ref,
):
    f32 = jnp.float32
    bf16 = jnp.bfloat16

    def first_stage(cos_rows, sin_rows, x):
        cos_twist = ct_ref[...]
        sin_twist = st_ref[...]
        real_a = jnp.dot(cos_rows, x, preferred_element_type=f32)
        imag_a = -jnp.dot(sin_rows, x, preferred_element_type=f32)
        real_b = (real_a * cos_twist + imag_a * sin_twist).astype(bf16)
        imag_b = (imag_a * cos_twist - real_a * sin_twist).astype(bf16)
        cos_second = cs_ref[...]
        sin_second = ss_ref[...]
        real_x = jnp.dot(real_b, cos_second, preferred_element_type=f32) + jnp.dot(
            imag_b, sin_second, preferred_element_type=f32
        )
        imag_x = jnp.dot(imag_b, cos_second, preferred_element_type=f32) - jnp.dot(
            real_b, sin_second, preferred_element_type=f32
        )
        return real_x, imag_x

    @pl.when(pl.program_id(0) == 0)
    def _():
        det = scalar_ref[1]
        for slot, sig_ref, w_ref in ((det, sown_ref, wown_ref), (1 - det, soth_ref, woth_ref)):
            rows = sig_ref.shape[0] // (N2 // BLK)
            signal = jnp.concatenate(
                [sig_ref[pl.ds(c, rows, stride=N2 // BLK), :] for c in range(N2 // BLK)], axis=1
            ).astype(bf16)
            real_s, imag_s = first_stage(cf_ref[...], sf_ref[...], signal)
            halves = N1 // BLK
            raw = jnp.concatenate(
                [w_ref[pl.ds(h, N2 // 2, stride=halves), :] for h in range(halves)], axis=1
            )
            weight = jnp.transpose(raw)
            pr_ref[slot] = weight * real_s
            pi_ref[slot] = weight * imag_s
            w2_ref[slot] = weight * weight

    used = x_ref.shape[1]
    temp_real, temp_imag = first_stage(cf_ref[:, :used], sf_ref[:, :used], x_ref[0])
    power = temp_real * temp_real + temp_imag * temp_imag
    cos_back = cs_ref[...]
    sin_back = ss_ref[...]

    def back_half(d):
        cos_twist = ct_ref[...]
        sin_twist = st_ref[...]
        sigma = jnp.sum(w2_ref[d] * power, axis=(0, 1), keepdims=True)
        data_real = pr_ref[d]
        data_imag = pi_ref[d]
        q_real = (temp_real * data_real + temp_imag * data_imag).astype(bf16)
        q_imag = (temp_real * data_imag - temp_imag * data_real).astype(bf16)
        d_real = dot_nt(q_real, cos_back) - dot_nt(q_imag, sin_back)
        d_imag = dot_nt(q_real, sin_back) + dot_nt(q_imag, cos_back)
        e_real = (d_real * cos_twist - d_imag * sin_twist).astype(bf16)
        e_imag = (d_real * sin_twist + d_imag * cos_twist).astype(bf16)
        return sigma, e_real, e_imag

    sigma0, e_real, e_imag = back_half(0)
    cos_first = cf_ref[...]
    sin_first = sf_ref[...]
    z_real = jnp.dot(cos_first, e_real, preferred_element_type=f32) - jnp.dot(
        sin_first, e_imag, preferred_element_type=f32
    )
    z_imag = jnp.dot(sin_first, e_real, preferred_element_type=f32) + jnp.dot(
        cos_first, e_imag, preferred_element_type=f32
    )
    first = (z_real * z_real + z_imag * z_imag) / (NFFT * sigma0)
    sigma1, e_real, e_imag = back_half(1)
    z_real = jnp.dot(cos_first, e_real, preferred_element_type=f32) - jnp.dot(
        sin_first, e_imag, preferred_element_type=f32
    )
    z_imag = jnp.dot(sin_first, e_real, preferred_element_type=f32) + jnp.dot(
        cos_first, e_imag, preferred_element_type=f32
    )
    rho_ref[...] = (z_real * z_real + z_imag * z_imag) / (NFFT * sigma1)
    rem = scalar_ref[0]
    quot = scalar_ref[2]
    rows = first.shape[0]
    tiles = first.shape[1] // BLK
    for col in range(tiles):
        src = lax.rem(col + rem, tiles)
        carry = (col + rem) // tiles
        cols = pl.ds(pl.multiple_of(src * BLK, BLK), BLK)
        shift = lax.rem(rows - lax.rem(quot + carry, rows), rows)
        second = pltpu.roll(rho_ref[:, cols], shift, 0)
        network = first[:, col * BLK:(col + 1) * BLK] + second
        out_ref[0, :, col:col + 1] = jnp.max(network, axis=1, keepdims=True)


def filter_bank(windowed, tables, signals, weights, shift, det):
    cos_first, sin_first, cos_twist, sin_twist, cos_second, sin_second = tables
    count, rows_used, width = windowed.shape
    pad_rows = 128
    x = jnp.concatenate(
        [windowed, jnp.zeros((count, pad_rows - rows_used, width), windowed.dtype)], axis=1
    )
    tiles = N2 // BLK
    quot = shift // tiles
    scalars = jnp.stack([lax.rem(shift, tiles), det, quot]).astype(jnp.int32)
    operands = [
        cos_twist, sin_twist,
        cos_second, sin_second, cos_first, sin_first,
        signals[0], signals[1], weights[0], weights[1],
    ]

    def whole(array):
        nd = array.ndim
        return pl.BlockSpec(array.shape, lambda i, r, nd=nd: (0,) * nd)

    grid_spec = pltpu.PrefetchScalarGridSpec(
        num_scalar_prefetch=1,
        grid=(count,),
        in_specs=[pl.BlockSpec((1, pad_rows, width), lambda i, r: (i, 0, 0))]
        + [whole(a) for a in operands],
        out_specs=pl.BlockSpec((1, N1, tiles), lambda i, r: (i, 0, 0)),
        scratch_shapes=[
            pltpu.VMEM((N1, N2), jnp.float32),
            pltpu.VMEM((2, N1, N2 // 2), jnp.float32),
            pltpu.VMEM((2, N1, N2 // 2), jnp.float32),
            pltpu.VMEM((2, N1, N2 // 2), jnp.float32),
        ],
    )
    matmuls = 2 * N1 * pad_rows * N2 + 4 * N1 * N2 * (N2 // 2) + 16 * N1 * (N2 // 2) * N2
    out = pl.pallas_call(
        filter_kernel,
        out_shape=jax.ShapeDtypeStruct((count, N1, tiles), jnp.float32),
        grid_spec=grid_spec,
        compiler_params=pltpu.CompilerParams(vmem_limit_bytes=48 * 1024 * 1024),
        cost_estimate=pl.CostEstimate(
            flops=2 * matmuls * count, transcendentals=0, bytes_accessed=8 * 1024 * 1024
        ),
    )(scalars, x, *operands)
    return out.reshape(count, N1 * tiles)


def shards(strain, inv_asd, templates, chirp_blocks, owner, slide):
    tables = make_tables()
    detector = lax.axis_index("det")
    per_dev = templates.shape[0]
    mine = per_dev // 2
    n_blk = NFFT // BLK
    half_blk = n_blk // 2
    filt_count = lax.axis_size("filt")
    swap = [(0, 1), (1, 0)]
    own_signal = strain.reshape(-1, BLK)
    own_weight = inv_asd.reshape(-1, BLK)
    other_signal = lax.ppermute(own_signal, "det", swap)
    other_weight = lax.ppermute(own_weight, "det", swap)
    samples = jnp.arange(TL, dtype=jnp.int32)
    my_rows = lax.dynamic_slice_in_dim(templates, detector * mine, mine)
    my_blocks = lax.dynamic_slice_in_dim(chirp_blocks, detector * mine, mine)
    windowed = jnp.where(
        samples[None, :] < BLK * my_blocks[:, None], my_rows, jnp.zeros_like(my_rows)
    )
    windowed = windowed.reshape(mine, TL // N2, N2)
    full = filter_bank(
        windowed, tables, (own_signal, other_signal), (own_weight, other_weight),
        slide[0], detector,
    )
    keep = lax.dynamic_slice_in_dim(full, detector * half_blk, half_blk, axis=1)
    give = lax.dynamic_slice_in_dim(full, (1 - detector) * half_blk, half_blk, axis=1)
    got = lax.ppermute(give, "det", swap)
    local = jnp.where(
        detector == 0, jnp.concatenate([keep, got], axis=0), jnp.concatenate([got, keep], axis=0)
    )
    local_max = jnp.max(local, axis=0)
    positions = jnp.arange(per_dev, dtype=jnp.int32)
    slots = jnp.arange(filt_count, dtype=jnp.int32)
    placing = owner[None, :] == slots[:, None]
    source = jnp.sum(jnp.where(placing, positions[None, :], 0), axis=1)
    used = jnp.any(placing, axis=1)
    flagged = jnp.concatenate([local, jnp.ones((per_dev, 128), jnp.float32)], axis=1)
    send_rows = jnp.where(used[:, None], jnp.take(flagged, source, axis=0), 0.0)
    split = half_blk + 128
    send_rows = jnp.concatenate(
        [send_rows, jnp.broadcast_to(local_max[None, :], (filt_count, half_blk))], axis=1
    )
    recv_rows, loudest = route_and_max(send_rows[:, None, :], split)
    recv_rows = recv_rows.reshape(filt_count, split)
    valid = recv_rows[:, half_blk] > 0.5
    rank = jnp.cumsum(valid.astype(jnp.int32)) - 1
    hits = jnp.logical_and(valid[None, :], rank[None, :] == positions[:, None])
    pick = jnp.sum(jnp.where(hits, slots[None, :], 0), axis=1)
    peaks = jnp.take(recv_rows[:, :half_blk], pick, axis=0)
    return (peaks, loudest)


def solution(mesh):
    return jax.shard_map(
        shards,
        mesh=mesh,
        in_specs=(
            P("det", None),
            P("det", None),
            P(("grp", "filt"), None),
            P(("grp", "filt")),
            P(("grp", "filt")),
            P("grp"),
        ),
        out_specs=(P(("grp", "filt"), "det"), P("det")),
        check_vma=False,
    )
```

```python
import functools

import jax
import ml_dtypes
import numpy as np
import jax.numpy as jnp
from jax import lax
from jax.experimental import pallas as pl
from jax.experimental.pallas import tpu as pltpu
from jax.sharding import PartitionSpec as P

N1 = 256
N2 = 512
NFFT = 131072
BLK = 128
TL = 4096


TWO_PI = 6.283185307179586


def angle_table(rows, cols, period):
    left = np.arange(rows, dtype=np.int64)[:, None]
    right = np.arange(cols, dtype=np.int64)[None, :]
    turns = (left * right % period).astype(np.float32)
    return np.float32(TWO_PI / period) * turns


def make_tables():
    twist = angle_table(N1, N2, NFFT).astype(np.float64)
    second = angle_table(N2, N2 // 2, N2).astype(np.float64)
    cos_second = np.cos(second).astype(np.float32).astype(ml_dtypes.bfloat16)
    sin_second = np.sin(second).astype(np.float32).astype(ml_dtypes.bfloat16)
    return tuple(
        jnp.asarray(table)
        for table in (
            cos_second[0::2],
            sin_second[0::2],
            np.cos(twist).astype(np.float32),
            np.sin(twist).astype(np.float32),
            cos_second,
            sin_second,
        )
    )


def route_kernel(
    split, send_ref, recv_out, out_ref, recv_buf, slot_send, slot_recv, acc_ref,
    held, grp_send, grp_recv,
):
    det = lax.axis_index("det")
    grp = lax.axis_index("grp")
    filt = lax.axis_index("filt")
    n_grp = lax.axis_size("grp")
    n_filt = send_ref.shape[0]
    mesh_ids = pl.DeviceIdType.MESH
    barrier = pltpu.get_barrier_semaphore()
    for i in range(n_filt - 1):
        target = lax.rem(filt + 1 + i, n_filt)
        pl.semaphore_signal(barrier, inc=1, device_id=(det, grp, target), device_id_type=mesh_ids)
    for i in range(n_grp - 1):
        target = lax.rem(grp + 1 + i, n_grp)
        pl.semaphore_signal(barrier, inc=1, device_id=(det, target, filt), device_id_type=mesh_ids)
    pl.semaphore_wait(barrier, n_filt - 1 + n_grp - 1)
    slots = []
    for i in range(n_filt - 1):
        target = lax.rem(filt + 1 + i, n_filt)
        copy = pltpu.make_async_remote_copy(
            src_ref=send_ref.at[target],
            dst_ref=recv_buf.at[filt],
            send_sem=slot_send.at[i],
            recv_sem=slot_recv.at[filt],
            device_id=(det, grp, target),
            device_id_type=mesh_ids,
        )
        copy.start()
        slots.append(copy)
    for copy in slots:
        copy.wait_send()
    for i in range(n_filt - 1):
        origin = lax.rem(filt + 1 + i, n_filt)
        pltpu.make_async_remote_copy(
            src_ref=send_ref.at[origin],
            dst_ref=recv_buf.at[origin],
            send_sem=slot_send.at[i],
            recv_sem=slot_recv.at[origin],
            device_id=(det, grp, origin),
            device_id_type=mesh_ids,
        ).wait_recv()
    recv_buf[filt] = send_ref[filt]
    rows = recv_buf[...]
    recv_out[...] = rows[:, :, :split]
    value = jnp.max(rows[:, :, split:], axis=0)
    if n_grp > 1:
        acc_ref[...] = value
        copies = []
        for i in range(n_grp - 1):
            target = lax.rem(grp + 1 + i, n_grp)
            row = n_grp - 2 - i
            copy = pltpu.make_async_remote_copy(
                src_ref=acc_ref,
                dst_ref=held.at[row],
                send_sem=grp_send.at[i],
                recv_sem=grp_recv.at[row],
                device_id=(det, target, filt),
                device_id_type=mesh_ids,
            )
            copy.start()
            copies.append(copy)
        for copy in copies:
            copy.wait_send()
            copy.wait_recv()
        value = jnp.maximum(value, jnp.max(held[...], axis=0))
    out_ref[...] = value


def route_and_max(send_rows, split):
    n_grp = lax.axis_size("grp")
    n_filt = send_rows.shape[0]
    width = send_rows.shape[-1] - split
    vmem = pl.BlockSpec(memory_space=pltpu.VMEM)
    recv, out = pl.pallas_call(
        functools.partial(route_kernel, split),
        out_shape=(
            jax.ShapeDtypeStruct((n_filt, 1, split), send_rows.dtype),
            jax.ShapeDtypeStruct((1, width), jnp.float32),
        ),
        in_specs=[vmem],
        out_specs=(vmem, vmem),
        scratch_shapes=[
            pltpu.VMEM(send_rows.shape, send_rows.dtype),
            pltpu.SemaphoreType.DMA((n_filt,)),
            pltpu.SemaphoreType.DMA((n_filt,)),
            pltpu.VMEM((1, width), jnp.float32),
            pltpu.VMEM((max(n_grp - 1, 1), 1, width), jnp.float32),
            pltpu.SemaphoreType.DMA((max(n_grp - 1, 1),)),
            pltpu.SemaphoreType.DMA((max(n_grp - 1, 1),)),
        ],
        compiler_params=pltpu.CompilerParams(collective_id=0, has_side_effects=True),
    )(send_rows)
    return recv, out.reshape(width)


def dot_nt(left, right):
    return lax.dot_general(
        left, right, (((1,), (1,)), ((), ())), preferred_element_type=jnp.float32
    )


def filter_kernel(
    scalar_ref, x_ref, ct_ref, st_ref, cs_ref, ss_ref, cf_ref, sf_ref,
    sown_ref, soth_ref, wown_ref, woth_ref, out_ref, rho_ref, pr_ref, pi_ref, w2_ref,
):
    f32 = jnp.float32
    bf16 = jnp.bfloat16

    def first_stage(cos_rows, sin_rows, x):
        cos_twist = ct_ref[...]
        sin_twist = st_ref[...]
        real_a = jnp.dot(cos_rows, x, preferred_element_type=f32)
        imag_a = -jnp.dot(sin_rows, x, preferred_element_type=f32)
        real_b = (real_a * cos_twist + imag_a * sin_twist).astype(bf16)
        imag_b = (imag_a * cos_twist - real_a * sin_twist).astype(bf16)
        cos_second = cs_ref[...]
        sin_second = ss_ref[...]
        real_x = jnp.dot(real_b, cos_second, preferred_element_type=f32) + jnp.dot(
            imag_b, sin_second, preferred_element_type=f32
        )
        imag_x = jnp.dot(imag_b, cos_second, preferred_element_type=f32) - jnp.dot(
            real_b, sin_second, preferred_element_type=f32
        )
        return real_x, imag_x

    @pl.when(pl.program_id(0) == 0)
    def _():
        det = scalar_ref[1]
        for slot, sig_ref, w_ref in ((det, sown_ref, wown_ref), (1 - det, soth_ref, woth_ref)):
            rows = sig_ref.shape[0] // (N2 // BLK)
            signal = jnp.concatenate(
                [sig_ref[pl.ds(c, rows, stride=N2 // BLK), :] for c in range(N2 // BLK)], axis=1
            ).astype(bf16)
            real_s, imag_s = first_stage(cf_ref[...], sf_ref[...], signal)
            halves = N1 // BLK
            raw = jnp.concatenate(
                [w_ref[pl.ds(h, N2 // 2, stride=halves), :] for h in range(halves)], axis=1
            )
            weight = jnp.transpose(raw)
            pr_ref[slot] = weight * real_s
            pi_ref[slot] = weight * imag_s
            w2_ref[slot] = weight * weight

    def one(j):
        used = x_ref.shape[1]
        temp_real, temp_imag = first_stage(cf_ref[:, :used], sf_ref[:, :used], x_ref[j])
        power = temp_real * temp_real + temp_imag * temp_imag
        cos_back = cs_ref[...]
        sin_back = ss_ref[...]

        def back_half(d):
            cos_twist = ct_ref[...]
            sin_twist = st_ref[...]
            sigma = jnp.sum(w2_ref[d] * power, axis=(0, 1), keepdims=True)
            data_real = pr_ref[d]
            data_imag = pi_ref[d]
            q_real = (temp_real * data_real + temp_imag * data_imag).astype(bf16)
            q_imag = (temp_real * data_imag - temp_imag * data_real).astype(bf16)
            d_real = dot_nt(q_real, cos_back) - dot_nt(q_imag, sin_back)
            d_imag = dot_nt(q_real, sin_back) + dot_nt(q_imag, cos_back)
            e_real = (d_real * cos_twist - d_imag * sin_twist).astype(bf16)
            e_imag = (d_real * sin_twist + d_imag * cos_twist).astype(bf16)
            return sigma, e_real, e_imag

        sigma0, e_real, e_imag = back_half(0)
        cos_first = cf_ref[...]
        sin_first = sf_ref[...]
        z_real = jnp.dot(cos_first, e_real, preferred_element_type=f32) - jnp.dot(
            sin_first, e_imag, preferred_element_type=f32
        )
        z_imag = jnp.dot(sin_first, e_real, preferred_element_type=f32) + jnp.dot(
            cos_first, e_imag, preferred_element_type=f32
        )
        first = (z_real * z_real + z_imag * z_imag) / (NFFT * sigma0)
        sigma1, e_real, e_imag = back_half(1)
        z_real = jnp.dot(cos_first, e_real, preferred_element_type=f32) - jnp.dot(
            sin_first, e_imag, preferred_element_type=f32
        )
        z_imag = jnp.dot(sin_first, e_real, preferred_element_type=f32) + jnp.dot(
            cos_first, e_imag, preferred_element_type=f32
        )
        rho_ref[...] = (z_real * z_real + z_imag * z_imag) / (NFFT * sigma1)
        rem = scalar_ref[0]
        quot = scalar_ref[2]
        rows = first.shape[0]
        tiles = first.shape[1] // BLK
        for col in range(tiles):
            src = lax.rem(col + rem, tiles)
            carry = (col + rem) // tiles
            cols = pl.ds(pl.multiple_of(src * BLK, BLK), BLK)
            shift = lax.rem(rows - lax.rem(quot + carry, rows), rows)
            second = pltpu.roll(rho_ref[:, cols], shift, 0)
            network = first[:, col * BLK:(col + 1) * BLK] + second
            out_ref[j, :, col:col + 1] = jnp.max(network, axis=1, keepdims=True)

    for j in range(x_ref.shape[0]):
        one(j)


def filter_bank(windowed, tables, signals, weights, shift, det):
    cos_first, sin_first, cos_twist, sin_twist, cos_second, sin_second = tables
    count, rows_used, width = windowed.shape
    pad_rows = 128
    x = jnp.concatenate(
        [windowed, jnp.zeros((count, pad_rows - rows_used, width), windowed.dtype)], axis=1
    )
    tiles = N2 // BLK
    quot = shift // tiles
    scalars = jnp.stack([lax.rem(shift, tiles), det, quot]).astype(jnp.int32)
    operands = [
        cos_twist, sin_twist,
        cos_second, sin_second, cos_first, sin_first,
        signals[0], signals[1], weights[0], weights[1],
    ]

    def whole(array):
        nd = array.ndim
        return pl.BlockSpec(array.shape, lambda i, r, nd=nd: (0,) * nd)

    grid_spec = pltpu.PrefetchScalarGridSpec(
        num_scalar_prefetch=1,
        grid=(count // 2,),
        in_specs=[pl.BlockSpec((2, pad_rows, width), lambda i, r: (i, 0, 0))]
        + [whole(a) for a in operands],
        out_specs=pl.BlockSpec((2, N1, tiles), lambda i, r: (i, 0, 0)),
        scratch_shapes=[
            pltpu.VMEM((N1, N2), jnp.float32),
            pltpu.VMEM((2, N1, N2 // 2), jnp.float32),
            pltpu.VMEM((2, N1, N2 // 2), jnp.float32),
            pltpu.VMEM((2, N1, N2 // 2), jnp.float32),
        ],
    )
    matmuls = 2 * N1 * pad_rows * N2 + 4 * N1 * N2 * (N2 // 2) + 16 * N1 * (N2 // 2) * N2
    out = pl.pallas_call(
        filter_kernel,
        out_shape=jax.ShapeDtypeStruct((count, N1, tiles), jnp.float32),
        grid_spec=grid_spec,
        compiler_params=pltpu.CompilerParams(vmem_limit_bytes=48 * 1024 * 1024),
        cost_estimate=pl.CostEstimate(
            flops=2 * matmuls * count, transcendentals=0, bytes_accessed=8 * 1024 * 1024
        ),
    )(scalars, x, *operands)
    return out.reshape(count, N1 * tiles)


def shards(strain, inv_asd, templates, chirp_blocks, owner, slide):
    tables = make_tables()
    detector = lax.axis_index("det")
    per_dev = templates.shape[0]
    mine = per_dev // 2
    n_blk = NFFT // BLK
    half_blk = n_blk // 2
    filt_count = lax.axis_size("filt")
    swap = [(0, 1), (1, 0)]
    own_signal = strain.reshape(-1, BLK)
    own_weight = inv_asd.reshape(-1, BLK)
    other_signal = lax.ppermute(own_signal, "det", swap)
    other_weight = lax.ppermute(own_weight, "det", swap)
    samples = jnp.arange(TL, dtype=jnp.int32)
    my_rows = lax.dynamic_slice_in_dim(templates, detector * mine, mine)
    my_blocks = lax.dynamic_slice_in_dim(chirp_blocks, detector * mine, mine)
    windowed = jnp.where(
        samples[None, :] < BLK * my_blocks[:, None], my_rows, jnp.zeros_like(my_rows)
    )
    windowed = windowed.reshape(mine, TL // N2, N2)
    full = filter_bank(
        windowed, tables, (own_signal, other_signal), (own_weight, other_weight),
        slide[0], detector,
    )
    keep = lax.dynamic_slice_in_dim(full, detector * half_blk, half_blk, axis=1)
    give = lax.dynamic_slice_in_dim(full, (1 - detector) * half_blk, half_blk, axis=1)
    got = lax.ppermute(give, "det", swap)
    local = jnp.where(
        detector == 0, jnp.concatenate([keep, got], axis=0), jnp.concatenate([got, keep], axis=0)
    )
    local_max = jnp.max(local, axis=0)
    positions = jnp.arange(per_dev, dtype=jnp.int32)
    slots = jnp.arange(filt_count, dtype=jnp.int32)
    placing = owner[None, :] == slots[:, None]
    source = jnp.sum(jnp.where(placing, positions[None, :], 0), axis=1)
    used = jnp.any(placing, axis=1)
    flagged = jnp.concatenate([local, jnp.ones((per_dev, 128), jnp.float32)], axis=1)
    send_rows = jnp.where(used[:, None], jnp.take(flagged, source, axis=0), 0.0)
    split = half_blk + 128
    send_rows = jnp.concatenate(
        [send_rows, jnp.broadcast_to(local_max[None, :], (filt_count, half_blk))], axis=1
    )
    recv_rows, loudest = route_and_max(send_rows[:, None, :], split)
    recv_rows = recv_rows.reshape(filt_count, split)
    valid = recv_rows[:, half_blk] > 0.5
    rank = jnp.cumsum(valid.astype(jnp.int32)) - 1
    hits = jnp.logical_and(valid[None, :], rank[None, :] == positions[:, None])
    pick = jnp.sum(jnp.where(hits, slots[None, :], 0), axis=1)
    peaks = jnp.take(recv_rows[:, :half_blk], pick, axis=0)
    return (peaks, loudest)


def solution(mesh):
    return jax.shard_map(
        shards,
        mesh=mesh,
        in_specs=(
            P("det", None),
            P("det", None),
            P(("grp", "filt"), None),
            P(("grp", "filt")),
            P(("grp", "filt")),
            P("grp"),
        ),
        out_specs=(P(("grp", "filt"), "det"), P("det")),
        check_vma=False,
    )
```

```python
import functools

import jax
import ml_dtypes
import numpy as np
import jax.numpy as jnp
from jax import lax
from jax.experimental import pallas as pl
from jax.experimental.pallas import tpu as pltpu
from jax.sharding import PartitionSpec as P

N1 = 256
N2 = 512
NFFT = 131072
BLK = 128
TL = 4096


TWO_PI = 6.283185307179586


def angle_table(rows, cols, period):
    left = np.arange(rows, dtype=np.int64)[:, None]
    right = np.arange(cols, dtype=np.int64)[None, :]
    turns = (left * right % period).astype(np.float32)
    return np.float32(TWO_PI / period) * turns


def make_tables():
    twist = angle_table(N1, N2, NFFT).astype(np.float64)
    second = angle_table(N2, N2 // 2, N2).astype(np.float64)
    cos_second = np.cos(second).astype(np.float32).astype(ml_dtypes.bfloat16)
    sin_second = np.sin(second).astype(np.float32).astype(ml_dtypes.bfloat16)
    return tuple(
        jnp.asarray(table)
        for table in (
            cos_second[0::2],
            sin_second[0::2],
            np.cos(twist).astype(np.float32),
            np.sin(twist).astype(np.float32),
            cos_second,
            sin_second,
        )
    )


def route_kernel(
    split, send_ref, recv_out, out_ref, recv_buf, slot_send, slot_recv, acc_ref,
    held, grp_send, grp_recv,
):
    det = lax.axis_index("det")
    grp = lax.axis_index("grp")
    filt = lax.axis_index("filt")
    n_grp = lax.axis_size("grp")
    n_filt = send_ref.shape[0]
    mesh_ids = pl.DeviceIdType.MESH
    barrier = pltpu.get_barrier_semaphore()
    for i in range(n_filt - 1):
        target = lax.rem(filt + 1 + i, n_filt)
        pl.semaphore_signal(barrier, inc=1, device_id=(det, grp, target), device_id_type=mesh_ids)
    for i in range(n_grp - 1):
        target = lax.rem(grp + 1 + i, n_grp)
        pl.semaphore_signal(barrier, inc=1, device_id=(det, target, filt), device_id_type=mesh_ids)
    pl.semaphore_wait(barrier, n_filt - 1 + n_grp - 1)
    slots = []
    for i in range(n_filt - 1):
        target = lax.rem(filt + 1 + i, n_filt)
        copy = pltpu.make_async_remote_copy(
            src_ref=send_ref.at[target],
            dst_ref=recv_buf.at[filt],
            send_sem=slot_send.at[i],
            recv_sem=slot_recv.at[filt],
            device_id=(det, grp, target),
            device_id_type=mesh_ids,
        )
        copy.start()
        slots.append(copy)
    for copy in slots:
        copy.wait_send()
    for i in range(n_filt - 1):
        origin = lax.rem(filt + 1 + i, n_filt)
        pltpu.make_async_remote_copy(
            src_ref=send_ref.at[origin],
            dst_ref=recv_buf.at[origin],
            send_sem=slot_send.at[i],
            recv_sem=slot_recv.at[origin],
            device_id=(det, grp, origin),
            device_id_type=mesh_ids,
        ).wait_recv()
    recv_buf[filt] = send_ref[filt]
    rows = recv_buf[...]
    recv_out[...] = rows[:, :, :split]
    value = jnp.max(rows[:, :, split:], axis=0)
    if n_grp > 1:
        acc_ref[...] = value
        copies = []
        for i in range(n_grp - 1):
            target = lax.rem(grp + 1 + i, n_grp)
            row = n_grp - 2 - i
            copy = pltpu.make_async_remote_copy(
                src_ref=acc_ref,
                dst_ref=held.at[row],
                send_sem=grp_send.at[i],
                recv_sem=grp_recv.at[row],
                device_id=(det, target, filt),
                device_id_type=mesh_ids,
            )
            copy.start()
            copies.append(copy)
        for copy in copies:
            copy.wait_send()
            copy.wait_recv()
        value = jnp.maximum(value, jnp.max(held[...], axis=0))
    out_ref[...] = value


def route_and_max(send_rows, split):
    n_grp = lax.axis_size("grp")
    n_filt = send_rows.shape[0]
    width = send_rows.shape[-1] - split
    vmem = pl.BlockSpec(memory_space=pltpu.VMEM)
    recv, out = pl.pallas_call(
        functools.partial(route_kernel, split),
        out_shape=(
            jax.ShapeDtypeStruct((n_filt, 1, split), send_rows.dtype),
            jax.ShapeDtypeStruct((1, width), jnp.float32),
        ),
        in_specs=[vmem],
        out_specs=(vmem, vmem),
        scratch_shapes=[
            pltpu.VMEM(send_rows.shape, send_rows.dtype),
            pltpu.SemaphoreType.DMA((n_filt,)),
            pltpu.SemaphoreType.DMA((n_filt,)),
            pltpu.VMEM((1, width), jnp.float32),
            pltpu.VMEM((max(n_grp - 1, 1), 1, width), jnp.float32),
            pltpu.SemaphoreType.DMA((max(n_grp - 1, 1),)),
            pltpu.SemaphoreType.DMA((max(n_grp - 1, 1),)),
        ],
        compiler_params=pltpu.CompilerParams(collective_id=0, has_side_effects=True),
    )(send_rows)
    return recv, out.reshape(width)


def dot_nt(left, right):
    return lax.dot_general(
        left, right, (((1,), (1,)), ((), ())), preferred_element_type=jnp.float32
    )


def filter_kernel(
    scalar_ref, x_ref, ct_ref, st_ref, cs_ref, ss_ref, cf_ref, sf_ref,
    sown_ref, soth_ref, wown_ref, woth_ref, out_ref, rho_ref, pr_ref, pi_ref, w2_ref,
):
    f32 = jnp.float32
    bf16 = jnp.bfloat16

    def first_stage(cos_rows, sin_rows, x):
        cos_twist = ct_ref[...]
        sin_twist = st_ref[...]
        real_a = jnp.dot(cos_rows, x, preferred_element_type=f32)
        imag_a = -jnp.dot(sin_rows, x, preferred_element_type=f32)
        real_b = (real_a * cos_twist + imag_a * sin_twist).astype(bf16)
        imag_b = (imag_a * cos_twist - real_a * sin_twist).astype(bf16)
        cos_second = cs_ref[...]
        sin_second = ss_ref[...]
        real_x = jnp.dot(real_b, cos_second, preferred_element_type=f32) + jnp.dot(
            imag_b, sin_second, preferred_element_type=f32
        )
        imag_x = jnp.dot(imag_b, cos_second, preferred_element_type=f32) - jnp.dot(
            real_b, sin_second, preferred_element_type=f32
        )
        return real_x, imag_x

    @pl.when(pl.program_id(0) == 0)
    def _():
        det = scalar_ref[1]
        for slot, sig_ref, w_ref in ((det, sown_ref, wown_ref), (1 - det, soth_ref, woth_ref)):
            rows = sig_ref.shape[0] // (N2 // BLK)
            signal = jnp.concatenate(
                [sig_ref[pl.ds(c, rows, stride=N2 // BLK), :] for c in range(N2 // BLK)], axis=1
            ).astype(bf16)
            real_s, imag_s = first_stage(cf_ref[...], sf_ref[...], signal)
            halves = N1 // BLK
            raw = jnp.concatenate(
                [w_ref[pl.ds(h, N2 // 2, stride=halves), :] for h in range(halves)], axis=1
            )
            weight = jnp.transpose(raw)
            pr_ref[slot] = weight * real_s
            pi_ref[slot] = weight * imag_s
            w2_ref[slot] = weight * weight

    used = x_ref.shape[1]
    temp_real, temp_imag = first_stage(cf_ref[:, :used], sf_ref[:, :used], x_ref[0])
    power = temp_real * temp_real + temp_imag * temp_imag
    cos_back = cs_ref[...]
    sin_back = ss_ref[...]

    def back_half(d):
        cos_twist = ct_ref[...]
        sin_twist = st_ref[...]
        sigma = jnp.sum(w2_ref[d] * power, axis=(0, 1), keepdims=True)
        data_real = pr_ref[d]
        data_imag = pi_ref[d]
        q_real = (temp_real * data_real + temp_imag * data_imag).astype(bf16)
        q_imag = (temp_real * data_imag - temp_imag * data_real).astype(bf16)
        d_real = dot_nt(q_real, cos_back) - dot_nt(q_imag, sin_back)
        d_imag = dot_nt(q_real, sin_back) + dot_nt(q_imag, cos_back)
        e_real = (d_real * cos_twist - d_imag * sin_twist).astype(bf16)
        e_imag = (d_real * sin_twist + d_imag * cos_twist).astype(bf16)
        return sigma, e_real, e_imag

    sigma0, e_real, e_imag = back_half(0)
    cos_first = cf_ref[...]
    sin_first = sf_ref[...]
    z_real = jnp.dot(cos_first, e_real, preferred_element_type=f32) - jnp.dot(
        sin_first, e_imag, preferred_element_type=f32
    )
    z_imag = jnp.dot(sin_first, e_real, preferred_element_type=f32) + jnp.dot(
        cos_first, e_imag, preferred_element_type=f32
    )
    first = (z_real * z_real + z_imag * z_imag) / (NFFT * sigma0)
    sigma1, e_real, e_imag = back_half(1)
    z_real = jnp.dot(cos_first, e_real, preferred_element_type=f32) - jnp.dot(
        sin_first, e_imag, preferred_element_type=f32
    )
    z_imag = jnp.dot(sin_first, e_real, preferred_element_type=f32) + jnp.dot(
        cos_first, e_imag, preferred_element_type=f32
    )
    rho_ref[...] = (z_real * z_real + z_imag * z_imag) / (NFFT * sigma1)
    rem = scalar_ref[0]
    quot = scalar_ref[2]
    rows = first.shape[0]
    tiles = first.shape[1] // BLK
    for col in range(tiles):
        src = lax.rem(col + rem, tiles)
        carry = (col + rem) // tiles
        cols = pl.ds(pl.multiple_of(src * BLK, BLK), BLK)
        shift = lax.rem(rows - lax.rem(quot + carry, rows), rows)
        second = pltpu.roll(rho_ref[:, cols], shift, 0)
        network = first[:, col * BLK:(col + 1) * BLK] + second
        out_ref[0, :, col:col + 1] = jnp.max(network, axis=1, keepdims=True)


def filter_bank(windowed, tables, signals, weights, shift, det):
    cos_first, sin_first, cos_twist, sin_twist, cos_second, sin_second = tables
    count, rows_used, width = windowed.shape
    pad_rows = 128
    x = jnp.concatenate(
        [windowed, jnp.zeros((count, pad_rows - rows_used, width), windowed.dtype)], axis=1
    )
    tiles = N2 // BLK
    quot = shift // tiles
    scalars = jnp.stack([lax.rem(shift, tiles), det, quot]).astype(jnp.int32)
    operands = [
        cos_twist, sin_twist,
        cos_second, sin_second, cos_first, sin_first,
        signals[0], signals[1], weights[0], weights[1],
    ]

    def whole(array):
        nd = array.ndim
        return pl.BlockSpec(array.shape, lambda i, r, nd=nd: (0,) * nd)

    grid_spec = pltpu.PrefetchScalarGridSpec(
        num_scalar_prefetch=1,
        grid=(count,),
        in_specs=[pl.BlockSpec((1, pad_rows, width), lambda i, r: (i, 0, 0))]
        + [whole(a) for a in operands],
        out_specs=pl.BlockSpec((1, N1, tiles), lambda i, r: (i, 0, 0)),
        scratch_shapes=[
            pltpu.VMEM((N1, N2), jnp.float32),
            pltpu.VMEM((2, N1, N2 // 2), jnp.float32),
            pltpu.VMEM((2, N1, N2 // 2), jnp.float32),
            pltpu.VMEM((2, N1, N2 // 2), jnp.float32),
        ],
    )
    matmuls = 2 * N1 * pad_rows * N2 + 4 * N1 * N2 * (N2 // 2) + 16 * N1 * (N2 // 2) * N2
    out = pl.pallas_call(
        filter_kernel,
        out_shape=jax.ShapeDtypeStruct((count, N1, tiles), jnp.float32),
        grid_spec=grid_spec,
        compiler_params=pltpu.CompilerParams(vmem_limit_bytes=48 * 1024 * 1024),
        cost_estimate=pl.CostEstimate(
            flops=2 * matmuls * count, transcendentals=0, bytes_accessed=8 * 1024 * 1024
        ),
    )(scalars, x, *operands)
    return out.reshape(count, N1 * tiles)


def shards(strain, inv_asd, templates, chirp_blocks, owner, slide):
    tables = make_tables()
    detector = lax.axis_index("det")
    per_dev = templates.shape[0]
    mine = per_dev // 2
    n_blk = NFFT // BLK
    half_blk = n_blk // 2
    filt_count = lax.axis_size("filt")
    swap = [(0, 1), (1, 0)]
    own_signal = strain.reshape(-1, BLK)
    own_weight = inv_asd.reshape(-1, BLK)
    other_signal = lax.ppermute(own_signal, "det", swap)
    other_weight = lax.ppermute(own_weight, "det", swap)
    samples = jnp.arange(TL, dtype=jnp.int32)
    my_rows = lax.dynamic_slice_in_dim(templates, detector * mine, mine)
    my_blocks = lax.dynamic_slice_in_dim(chirp_blocks, detector * mine, mine)
    windowed = jnp.where(
        samples[None, :] < BLK * my_blocks[:, None], my_rows, jnp.zeros_like(my_rows)
    )
    windowed = windowed.reshape(mine, TL // N2, N2)
    full = filter_bank(
        windowed, tables, (own_signal, other_signal), (own_weight, other_weight),
        slide[0], detector,
    )
    keep = lax.dynamic_slice_in_dim(full, detector * half_blk, half_blk, axis=1)
    give = lax.dynamic_slice_in_dim(full, (1 - detector) * half_blk, half_blk, axis=1)
    got = lax.ppermute(give, "det", swap)
    local = jnp.where(
        detector == 0, jnp.concatenate([keep, got], axis=0), jnp.concatenate([got, keep], axis=0)
    )
    local_max = jnp.max(local, axis=0)
    positions = jnp.arange(per_dev, dtype=jnp.int32)
    slots = jnp.arange(filt_count, dtype=jnp.int32)
    placing = owner[None, :] == slots[:, None]
    source = jnp.sum(jnp.where(placing, positions[None, :], 0), axis=1)
    used = jnp.any(placing, axis=1)
    split = half_blk + 128
    flagged = jnp.concatenate(
        [
            local,
            jnp.ones((per_dev, 128), jnp.float32),
            jnp.broadcast_to(local_max[None, :], (per_dev, half_blk)),
        ],
        axis=1,
    )
    columns = jnp.arange(split + half_blk, dtype=jnp.int32)
    keep_cols = jnp.logical_or(used[:, None], columns[None, :] >= split)
    send_rows = jnp.where(keep_cols, jnp.take(flagged, source, axis=0), 0.0)
    recv_rows, loudest = route_and_max(send_rows[:, None, :], split)
    recv_rows = recv_rows.reshape(filt_count, split)
    valid = recv_rows[:, half_blk] > 0.5
    rank = jnp.cumsum(valid.astype(jnp.int32)) - 1
    hits = jnp.logical_and(valid[None, :], rank[None, :] == positions[:, None])
    pick = jnp.sum(jnp.where(hits, slots[None, :], 0), axis=1)
    peaks = jnp.take(recv_rows[:, :half_blk], pick, axis=0)
    return (peaks, loudest)


def solution(mesh):
    return jax.shard_map(
        shards,
        mesh=mesh,
        in_specs=(
            P("det", None),
            P("det", None),
            P(("grp", "filt"), None),
            P(("grp", "filt")),
            P(("grp", "filt")),
            P("grp"),
        ),
        out_specs=(P(("grp", "filt"), "det"), P("det")),
        check_vma=False,
    )
```
